32 devices in a mesh: dp: 4 (over y, core), seq: 8 (over z, x).
Axes of the slice: x: 2, y: 2, z: 4, core: 2. Of those that a mesh axis runs over, the one named last changes fastest.
Arguments:
- inputs: bfloat16 [8, 1024, 512], P('dp', 'seq'), may hold values from -6 to 6
- encoder: bfloat16 [8, 1024, 512], P('dp', 'seq'), may hold values from -6 to 6
- teacher: bfloat16 [8, 1024, 512], P('dp', 'seq')
- dec_seg: int32 [8, 1024], P('dp'), may hold values from 0 to 7, as said below
- enc_seg: int32 [8, 1024], P('dp'), may hold values from 0 to 7, as said below
- dec_valid: int32 [8, 1024], P('dp', 'seq'), may hold values from 0 to 1, as said below
- self_in: bfloat16 [512, 1536], P(('dp', 'seq')), may hold values from -0.25 to 0.25
- self_out: bfloat16 [512, 512], P(('dp', 'seq')), may hold values from -2 to 2
- cross_query: bfloat16 [512, 512], P(('dp', 'seq')), may hold values from -0.25 to 0.25
- cross_in: bfloat16 [512, 1024], P(('dp', 'seq')), may hold values from -0.25 to 0.25
- cross_out: bfloat16 [512, 512], P(('dp', 'seq')), may hold values from -2 to 2
- ffn_up: bfloat16 [512, 2048], P(('dp', 'seq')), may hold values from -0.25 to 0.25
- ffn_down: bfloat16 [2048, 512], P(('dp', 'seq')), may hold values from -0.125 to 0.125
- norm_gain: bfloat16 [3, 512], P(None, ('dp', 'seq')), may hold values from 0.5 to 1.5
- norm_bias: bfloat16 [3, 512], P(None, ('dp', 'seq')), may hold values from -1 to 1
Outputs:
- outputs: bfloat16 [8, 1024, 512], P('dp', 'seq')
- loss: float32 [], replicated
- grad_inputs: float32 [8, 1024, 512], P('dp', 'seq')
- grad_encoder: float32 [8, 1024, 512], P('dp', 'seq')
- grad_self_in: float32 [512, 1536], P(('dp', 'seq'))
- grad_self_out: float32 [512, 512], P(('dp', 'seq'))
- grad_cross_query: float32 [512, 512], P(('dp', 'seq'))
- grad_cross_in: float32 [512, 1024], P(('dp', 'seq'))
- grad_cross_out: float32 [512, 512], P(('dp', 'seq'))
- grad_ffn_up: float32 [512, 2048], P(('dp', 'seq'))
- grad_ffn_down: float32 [2048, 512], P(('dp', 'seq'))
- grad_norm_gain: float32 [3, 512], P(None, ('dp', 'seq'))
- grad_norm_bias: float32 [3, 512], P(None, ('dp', 'seq'))
The draws below stay inside these ranges and needn't reach their ends.
Inputs may be any that keep to these rules, and one draw needn't show every extreme that they name: `dec_seg`: along each sequence the numbers start at 0 and never fall; every number but the largest marks one document of 60 to 640 tokens; the largest marks the padding at the sequence's end, at least one position. The first sequence holds one document of exactly 640 tokens followed by as many documents of exactly 60 tokens as fit before its last position; no sequence holds more documents than it. `enc_seg`: numbered as dec_seg: encoder document k belongs to decoder document k of the same sequence, every decoder document has one, and the largest number marks padding of at least one position, matched by the decoder's padding. The first sequence is laid out as in dec_seg. `dec_valid`: 1 exactly where dec_seg is below its sequence's largest number.
All inputs are finite; a program needn't handle non-finite values.
Results may differ from the reference program's by a relative error of at most 0.02.
Values may be sent and summed in bfloat16 or wider, within the bound.
No kernel may reach another device: no remote copies, remote signals or barrier semaphores. Data moves between devices by JAX's collectives and lax.ppermute only.
A program may use at most 192 MiB of HBM per device.

```python
import math
import jax
import jax.numpy as jnp
from jax import lax

D = 512
HEADS = 8
HEAD_DIM = 64
FF = 2048
DOC_MIN = 60
LEN = 1024
DOC_MAX = 640
NSEQ = 8


def pack_layout(key):
    base_key = jax.random.fold_in(key, 11)
    dec_key, enc_key = jax.random.split(base_key)
    slot_count = LEN // DOC_MIN + 1
    most_docs = 1 + (LEN - 1 - DOC_MAX) // DOC_MIN
    slot_index = jnp.arange(slot_count, dtype=jnp.int32)
    first_row = (jnp.arange(NSEQ, dtype=jnp.int32) == 0)[:, None]
    first_lengths = jnp.where(slot_index == 0, DOC_MAX, DOC_MIN).astype(jnp.int32)[None, :]
    dec_lengths = jnp.where(first_row, first_lengths, jax.random.randint(dec_key, (NSEQ, slot_count), DOC_MIN, DOC_MAX + 1))
    enc_lengths = jnp.where(first_row, first_lengths, jax.random.randint(enc_key, (NSEQ, slot_count), DOC_MIN, DOC_MAX + 1))
    dec_ends = jnp.cumsum(dec_lengths, axis=1)
    enc_ends = jnp.cumsum(enc_lengths, axis=1)
    dec_fit = jnp.sum((dec_ends <= LEN - 1).astype(jnp.int32), axis=1)
    enc_fit = jnp.sum((enc_ends <= LEN - 1).astype(jnp.int32), axis=1)
    doc_count = jnp.minimum(jnp.minimum(dec_fit, enc_fit), most_docs)
    live_slot = slot_index[None, :] < doc_count[:, None]
    positions = jnp.arange(LEN, dtype=jnp.int32)
    dec_numbers = jnp.sum(((dec_ends[:, None, :] <= positions[None, :, None]) & live_slot[:, None, :]).astype(jnp.int32), axis=2)
    enc_numbers = jnp.sum(((enc_ends[:, None, :] <= positions[None, :, None]) & live_slot[:, None, :]).astype(jnp.int32), axis=2)
    dec_stop = jnp.sum(jnp.where(slot_index[None, :] == doc_count[:, None] - 1, dec_ends, 0), axis=1)
    valid_marks = (positions[None, :] < dec_stop[:, None]).astype(jnp.int32)
    return (dec_numbers.astype(jnp.int32), enc_numbers.astype(jnp.int32), valid_marks)


def draw_dec_seg(key, part):
    return pack_layout(key)[0]


def draw_enc_seg(key, part):
    return pack_layout(key)[1]


def draw_dec_valid(key, part):
    return pack_layout(key)[2]


def draw_teacher(key, part):
    teacher_key = jax.random.fold_in(key, 23)
    ramp = jnp.arange(NSEQ, dtype=jnp.float32) / max(NSEQ - 1, 1)
    scales = 0.6 * jnp.power(3.0, ramp)
    base = jnp.clip(jax.random.normal(teacher_key, (NSEQ, LEN, D), jnp.float32), -4.0, 4.0)
    return (base * scales[:, None, None]).astype(jnp.bfloat16)


def steps_of(stream_key, dims, cuts, smallest, top_value):
    gain, own = 1.0, jax.random.fold_in(stream_key, 6)
    for axis_at, shards_of in cuts:
        draws = jnp.exp(jax.random.uniform(jax.random.fold_in(own, axis_at), (shards_of,), jnp.float32, smallest / len(cuts), top_value / len(cuts)))
        gain = gain * jnp.repeat(draws, dims[axis_at] // shards_of).reshape([-1 if axis == axis_at else 1 for axis in range(len(dims))])
    return gain


def scatter_about(key, shape, scale, reach, cuts=(), kind=jnp.bfloat16):
    factor_of = steps_of(key, shape, cuts, -0.22, 0.18) if cuts else 1.0
    array = jax.random.normal(key, shape, jnp.float32) * scale * factor_of
    return jnp.minimum(jnp.maximum(array, -reach), reach).astype(kind)


def setup_inputs(seed: int = 0) -> dict:
    key_list = jax.random.split(jax.random.key(seed), 16)
    inputs = scatter_about(key_list[0], (NSEQ, LEN, D), 1.0, 6.0, ((0, 4), (1, 8)))
    encoder = scatter_about(key_list[1], (NSEQ, LEN, D), 1.0, 6.0, ((0, 4), (1, 8)))
    teacher = draw_teacher(jax.random.fold_in(key_list[15], 71), 0)
    dec_seg = draw_dec_seg(jax.random.fold_in(key_list[15], 71), 0)
    enc_seg = draw_enc_seg(jax.random.fold_in(key_list[15], 71), 0)
    dec_valid = draw_dec_valid(jax.random.fold_in(key_list[15], 71), 0)
    self_in = scatter_about(key_list[6], (D, 3 * D), D ** -0.5, 0.25, ((0, 32),))
    self_out = scatter_about(key_list[7], (D, D), (D // 64) ** -0.5, 2.0, ((0, 32),))
    cross_query = scatter_about(key_list[8], (D, D), D ** -0.5, 0.25, ((0, 32),))
    cross_in = scatter_about(key_list[9], (D, 2 * D), D ** -0.5, 0.25, ((0, 32),))
    cross_out = scatter_about(key_list[10], (D, D), (D // 64) ** -0.5, 2.0, ((0, 32),))
    ffn_up = scatter_about(key_list[11], (D, FF), D ** -0.5, 0.25, ((0, 32),))
    ffn_down = scatter_about(key_list[12], (FF, D), FF ** -0.5, 0.125, ((0, 32),))
    norm_gain = jnp.clip(1.0 + 0.1 * jax.random.normal(key_list[13], (3, D), jnp.float32), 0.5, 1.5).astype(jnp.bfloat16)
    norm_bias = scatter_about(key_list[14], (3, D), 0.2, 1.0, ((1, 32),))
    return {"inputs": inputs, "encoder": encoder, "teacher": teacher, "dec_seg": dec_seg, "enc_seg": enc_seg, "dec_valid": dec_valid, "self_in": self_in, "self_out": self_out, "cross_query": cross_query, "cross_in": cross_in, "cross_out": cross_out, "ffn_up": ffn_up, "ffn_down": ffn_down, "norm_gain": norm_gain, "norm_bias": norm_bias}


NORM_EPSILON = 1e-05
MASK_FLOOR = -1e+30
HIGHEST_MODE = lax.Precision.HIGHEST

@jax.custom_vjp
def low(v):
    return lax.optimization_barrier(v.astype(jnp.bfloat16)).astype(jnp.float32)

@jax.custom_vjp
def low_back(v):
    return v

def low_keep(v):
    return (low(v), None)

def low_pass(kept, grad):
    return (grad,)

def back_keep(v):
    return (v, None)

def back_low(kept, grad):
    return (low(grad),)
low.defvjp(low_keep, low_pass)
low_back.defvjp(back_keep, back_low)

def matmul(left, right):
    return jnp.dot(left, right, precision=HIGHEST_MODE, preferred_element_type=jnp.float32)

def layer_norm(residual, gain_row, bias_row):
    centre = residual - lax.optimization_barrier(jnp.mean(residual, axis=-1, keepdims=True))
    spread = lax.optimization_barrier(jnp.mean(centre * centre, axis=-1, keepdims=True))
    return centre * lax.rsqrt(spread + NORM_EPSILON) * gain_row + bias_row

def attention(queries, key_rows, values, allowed):
    length = queries.shape[0]
    others = key_rows.shape[0]
    query_heads = queries.reshape(length, HEADS, HEAD_DIM)
    key_heads = key_rows.reshape(others, HEADS, HEAD_DIM)
    value_heads = values.reshape(others, HEADS, HEAD_DIM)
    scores = low_back(jnp.einsum('qhd,khd->hqk', query_heads, key_heads, precision=HIGHEST_MODE) * (1.0 / math.sqrt(HEAD_DIM)))
    masked = jnp.where(allowed[None], scores, MASK_FLOOR)
    row_peak = lax.optimization_barrier(jnp.max(masked, axis=2, keepdims=True))
    numerators = jnp.where(allowed[None], jnp.exp(masked - row_peak), 0.0)
    attn_probs = numerators / lax.optimization_barrier(jnp.sum(numerators, axis=2, keepdims=True))
    mixed_out = jnp.einsum('hqk,khd->qhd', low(attn_probs), value_heads, precision=HIGHEST_MODE)
    return low_back(low(mixed_out.reshape(length, HEADS * HEAD_DIM)))

def one_sequence(weights, pieces):
    w_in, w_out, c_query, c_in, c_out, w_up, w_down, gains, biases = weights
    dec_rows, enc_rows, target, dec_segs, enc_segs, valid_rows = pieces
    widths = dec_rows.shape[1]
    positions = jnp.arange(dec_rows.shape[0], dtype=jnp.int32)
    self_allowed = (dec_segs[:, None] == dec_segs[None, :]) & (positions[None, :] <= positions[:, None])
    cross_allowed = dec_segs[:, None] == enc_segs[None, :]
    projected = low_back(low(matmul(dec_rows, w_in)))
    attended = attention(projected[:, :widths], projected[:, widths:2 * widths], projected[:, 2 * widths:], self_allowed)
    normed_one = layer_norm(dec_rows + low_back(matmul(attended, w_out)), gains[0], biases[0])
    cross_q = low_back(low(matmul(low(normed_one), c_query)))
    enc_proj = low_back(low(matmul(enc_rows, c_in)))
    cross_mix = attention(cross_q, enc_proj[:, :widths], enc_proj[:, widths:], cross_allowed)
    normed_two = layer_norm(normed_one + low_back(matmul(cross_mix, c_out)), gains[1], biases[1])
    hidden = low_back(matmul(low(normed_two), w_up))
    residual = normed_two + low_back(matmul(low(jax.nn.silu(hidden)), w_down))
    result = layer_norm(residual, gains[2], biases[2])
    error = (result - target) * valid_rows[:, None]
    return (result, 0.5 * jnp.sum(error * error))

def reference(inputs, encoder, teacher, dec_seg, enc_seg, dec_valid, self_in, self_out, cross_query, cross_in, cross_out, ffn_up, ffn_down, norm_gain, norm_bias):
    float_weights = tuple((w.astype(jnp.float32) for w in (self_in, self_out, cross_query, cross_in, cross_out, ffn_up, ffn_down, norm_gain, norm_bias)))
    target = teacher.astype(jnp.float32)
    valid_rows = dec_valid.astype(jnp.float32)
    stepper = jax.checkpoint(one_sequence)

    def forward(dec_rows, enc_rows, weights):
        results, halves = lax.map(lambda pieces: stepper(weights, pieces), (dec_rows, enc_rows, target, dec_seg, enc_seg, valid_rows))
        return (results, jnp.sum(halves))
    (results, half_total), pullback = jax.vjp(forward, inputs.astype(jnp.float32), encoder.astype(jnp.float32), float_weights)
    grad_in, grad_enc, grad_weights = pullback((jnp.zeros_like(results), jnp.ones_like(half_total)))
    loss_value = 2.0 * half_total / (jnp.sum(valid_rows) * D)
    return (results.astype(jnp.bfloat16), loss_value, grad_in, grad_enc, grad_weights[0], grad_weights[1], grad_weights[2], grad_weights[3], grad_weights[4], grad_weights[5], grad_weights[6], grad_weights[7], grad_weights[8])
```

```python
import functools

import jax
import jax.numpy as jnp
from jax import lax
from jax.experimental import pallas as pl
from jax.experimental.pallas import tpu as pltpu
from jax.sharding import PartitionSpec as P

HEADS = 8
HEAD_DIM = 64
EPS = 1e-5
NEG = -1e30
SCALE = 0.125
D = 512
FF = 2048
G = 32
BF = jnp.bfloat16
F32 = jnp.float32
MIB = 1 << 20

N_PACK = 17

NN = (((1,), (0,)), ((), ()))
NT = (((1,), (1,)), ((), ()))
TN = (((0,), (0,)), ((), ()))


def dot(a, b, dims=NN):
    return lax.dot_general(a, b, dims, preferred_element_type=F32)


def whole(shape):
    return pl.BlockSpec(shape, lambda i: (0,) * len(shape))


def chunks(first, count):
    return pl.BlockSpec((G, count, 16, D), lambda i: (0, first // count, 0, 0))


NORMS = pl.BlockSpec((G, 1, 16, D), lambda i: (0, 16, 0, 0))


def call(body, ins, outs, scratch=(), name=None, cost=None):
    return pl.pallas_call(
        body,
        grid=(1,),
        in_specs=[whole(a.shape) if s is None else s for a, s in ins],
        out_specs=[whole(s) for s, _ in outs],
        out_shape=[jax.ShapeDtypeStruct(s, t) for s, t in outs],
        scratch_shapes=list(scratch),
        compiler_params=pltpu.CompilerParams(vmem_limit_bytes=56 * MIB),
        name=name,
        cost_estimate=cost,
    )(*[a for a, _ in ins])


def cost(flops, nbytes):
    return pl.CostEstimate(flops=int(flops), bytes_accessed=int(nbytes), transcendentals=0)


def weight(ref, j):
    return ref[:, j].reshape(D, D)


def put(ref, j, value):
    ref[:, j] = value.astype(BF).reshape(G, 16, D)


def norm_rows(ref):
    return jnp.sum(ref[:, 0].astype(F32), axis=0)


def norm_forward(resid, gain, bias):
    centre = resid - jnp.mean(resid, axis=-1, keepdims=True)
    rstd = lax.rsqrt(jnp.mean(centre * centre, axis=-1, keepdims=True) + EPS)
    xhat = centre * rstd
    return xhat, rstd, xhat * gain + bias


def norm_back(g, xhat, rstd, gain):
    e = g * gain
    m1 = jnp.mean(e, axis=-1, keepdims=True)
    m2 = jnp.mean(e * xhat, axis=-1, keepdims=True)
    dr = (e - m1 - xhat * m2) * rstd
    return dr, jnp.sum(g * xhat, axis=0, keepdims=True), jnp.sum(g, axis=0, keepdims=True)


def head_half(x, e):
    lane = lax.broadcasted_iota(jnp.int32, x.shape, 1)
    return jnp.where((lane < HEAD_DIM) == (e == 0), x, jnp.zeros_like(x))


def attend(q_ref, kv_ref, mask_ref, p_ref, rl_ref, at_ref):
    def pair(hp, carry):
        c0 = pl.multiple_of(hp * 128, 128)
        k2 = kv_ref[:, pl.ds(c0, 128)]
        v2 = kv_ref[:, pl.ds(pl.multiple_of(D + c0, 128), 128)]
        q2 = q_ref[:, pl.ds(c0, 128)]
        for e in range(2):
            s = dot(k2, head_half(q2, e), NT) + mask_ref[...]
            p = jnp.exp(s - jnp.max(s, axis=0, keepdims=True))
            rl = 1.0 / jnp.sum(p, axis=0, keepdims=True)
            pb = p.astype(BF)
            p_ref[2 * hp + e] = pb
            rl_ref[2 * hp + e] = rl
            o = dot(v2, pb, TN) * rl
            at_ref[pl.ds(pl.multiple_of((2 * hp + e) * HEAD_DIM, HEAD_DIM), HEAD_DIM), :] = o[
                e * HEAD_DIM : (e + 1) * HEAD_DIM
            ].astype(BF)
        return carry

    lax.fori_loop(0, HEADS // 2, pair, 0)


def attend_back(q_ref, kv_ref, p_ref, rl_ref, do_ref, dkv_ref, dqt_ref):
    def pair(hp, carry):
        c0 = pl.multiple_of(hp * 128, 128)
        c1 = pl.multiple_of(D + c0, 128)
        k2 = kv_ref[:, pl.ds(c0, 128)]
        v2 = kv_ref[:, pl.ds(c1, 128)]
        q2 = q_ref[:, pl.ds(c0, 128)]
        do2 = do_ref[:, pl.ds(c0, 128)]
        dk = dv = None
        for e in range(2):
            dom = head_half(do2, e)
            dp = dot(v2, dom, NT)
            p = p_ref[2 * hp + e].astype(F32) * rl_ref[2 * hp + e]
            t = p * dp
            ds = (t - p * jnp.sum(t, axis=0, keepdims=True)).astype(BF)
            dk_e = dot(ds, head_half(q2, e))
            dv_e = dot(p.astype(BF), dom)
            dk = dk_e if dk is None else dk + dk_e
            dv = dv_e if dv is None else dv + dv_e
            dqt = dot(k2, ds, TN) * SCALE
            dqt_ref[pl.ds(pl.multiple_of((2 * hp + e) * HEAD_DIM, HEAD_DIM), HEAD_DIM), :] = dqt[
                e * HEAD_DIM : (e + 1) * HEAD_DIM
            ]
        dkv_ref[:, pl.ds(c0, 128)] = dk.astype(BF)
        dkv_ref[:, pl.ds(c1, 128)] = dv.astype(BF)
        return carry

    lax.fori_loop(0, HEADS // 2, pair, 0)


def self_forward(rows, xf, w, mask, q, kv, p, rl, at):
    q[...] = (dot(xf[:rows], weight(w, 0)).astype(BF).astype(F32) * SCALE).astype(BF)
    kv[:, :D] = dot(xf[...], weight(w, 1)).astype(BF)
    kv[:, D:] = dot(xf[...], weight(w, 2)).astype(BF)
    attend(q, kv, mask, p, rl, at)


def cross_forward(rows, xf, ef, at1, w_out, w_cin, w_cq, norms, mask, xh1, rs1, low1, q, kv, p, rl, at):
    gb = norm_rows(norms)
    resid = xf[:rows].astype(F32) + dot(at1[...], weight(w_out, 0), TN)
    xhat, rstd, n1 = norm_forward(resid, gb[0:1], gb[3:4])
    xh1[...] = xhat
    rs1[...] = rstd
    low1[...] = n1.astype(BF)
    q[...] = (dot(low1[...], weight(w_cq, 0)).astype(BF).astype(F32) * SCALE).astype(BF)
    kv[:, :D] = dot(ef[...], weight(w_cin, 0)).astype(BF)
    kv[:, D:] = dot(ef[...], weight(w_cin, 1)).astype(BF)
    attend(q, kv, mask, p, rl, at)


def ffn_both(xh1, at2, teach, valid, w_co, w_up, w_dn, norms,
             out, small, d_r2, d_mix, g_up, g_dn, g_co, act, hid):
    gb = norm_rows(norms)
    n1 = xh1[...] * gb[0:1] + gb[3:4]
    wco = weight(w_co, 0)
    xh2, rs2, n2 = norm_forward(n1 + dot(at2[...], wco, TN), gb[1:2], gb[4:5])
    low2 = n2.astype(BF)
    r3 = n2
    for j in range(4):
        h = dot(low2, weight(w_up, j))
        hid[j] = h
        a = (h / (1.0 + jnp.exp(-h))).astype(BF)
        act[:, j * D : (j + 1) * D] = a
    wdn = w_dn[...].reshape(FF, D)
    r3 = n2 + dot(act[...], wdn)
    xh3, rs3, final = norm_forward(r3, gb[2:3], gb[5:6])
    out[...] = final.astype(BF)
    err = (final - teach[...].astype(F32)) * valid[...]
    small[...] = jnp.zeros_like(small)
    small[6:7] = jnp.sum(err * err, axis=0, keepdims=True)
    d_r3, dg, db = norm_back(err, xh3, rs3, gb[2:3])
    small[2:3] = dg
    small[5:6] = db
    dffn = d_r3.astype(BF)
    g_dn[...] = dot(act[...], dffn, TN).astype(BF).reshape(G, 4, 16, D)
    dn2 = d_r3
    for j in range(4):
        da = dot(dffn, wdn[j * D : (j + 1) * D], NT)
        h = hid[j]
        sig = 1.0 / (1.0 + jnp.exp(-h))
        dh = (da * (sig * (1.0 + h * (1.0 - sig)))).astype(BF)
        put(g_up, j, dot(low2, dh, TN))
        dn2 = dn2 + dot(dh, weight(w_up, j), NT)
    dr2, dg, db = norm_back(dn2, xh2, rs2, gb[1:2])
    small[1:2] = dg
    small[4:5] = db
    d_r2[...] = dr2
    dcross = dr2.astype(BF)
    put(g_co, 0, dot(at2[...], dcross))
    d_mix[...] = dot(dcross, wco, NT).astype(BF)


def cross_back(ef, q, kv, p, rl, d_mix, w_cin, w_cq, w_out, norms, d_r2, low1, xh1, rs1, at1, small_in,
               d_enc, g_cin, g_cq, g_so, d_mix1, d_r1, small, dkv, dqt):
    attend_back(q, kv, p, rl, d_mix, dkv, dqt)
    d_enc[...] = (
        dot(dkv[:, :D], weight(w_cin, 0), NT) + dot(dkv[:, D:], weight(w_cin, 1), NT)
    ).astype(BF)
    put(g_cin, 0, dot(ef[...], dkv[:, :D], TN))
    put(g_cin, 1, dot(ef[...], dkv[:, D:], TN))
    dq = jnp.transpose(dqt[...]).astype(BF)
    put(g_cq, 0, dot(low1[...], dq, TN))
    gb = norm_rows(norms)
    dn1 = d_r2[...] + dot(dq, weight(w_cq, 0), NT)
    dr1, dg, db = norm_back(dn1, xh1[...], rs1[...], gb[0:1])
    small[...] = small_in[...]
    small[0:1] = dg
    small[3:4] = db
    d_r1[...] = dr1
    dself = dr1.astype(BF)
    put(g_so, 0, dot(at1[...], dself))
    d_mix1[...] = dot(dself, weight(w_out, 0), NT).astype(BF)


def self_back(rows, xf, q, kv, p, rl, d_mix, w, d_r1, d_x, d_own, g_in, dkv, dqt):
    attend_back(q, kv, p, rl, d_mix, dkv, dqt)
    d_x[...] = (dot(dkv[:, :D], weight(w, 1), NT) + dot(dkv[:, D:], weight(w, 2), NT)).astype(BF)
    dq = jnp.transpose(dqt[...]).astype(BF)
    d_own[...] = d_r1[...] + dot(dq, weight(w, 0), NT)
    put(g_in, 0, dot(xf[:rows], dq, TN))
    put(g_in, 1, dot(xf[...], dkv[:, :D], TN))
    put(g_in, 2, dot(xf[...], dkv[:, D:], TN))


def flip(axis, size, bit):
    return functools.partial(
        lax.ppermute, axis_name=axis, perm=[(i, i ^ bit) for i in range(size)]
    )


def make_shards(nd, ns):
    n_dev = nd * ns
    half = ns // 2
    per = G * 16 // n_dev

    def shards(inputs, encoder, teacher, dec_seg, enc_seg, dec_valid, self_in, self_out,
               cross_query, cross_in, cross_out, ffn_up, ffn_down, norm_gain, norm_bias):
        tok = inputs.shape[1]
        rows = 2 * tok
        length = dec_seg.shape[1]
        dp_at, seq_at = lax.axis_index("dp"), lax.axis_index("seq")
        dev = dp_at * ns + seq_at
        mine = seq_at // half

        def cut(w):
            return w.reshape(per, w.shape[1] // D, D).transpose(1, 0, 2)

        norms = lax.dynamic_update_slice(
            jnp.zeros((16, D), BF), jnp.concatenate([norm_gain, norm_bias], 0), (0, dev * per)
        )
        packed = [cut(self_in), cut(self_out), cut(cross_in), cut(cross_query), cut(cross_out), cut(ffn_up)]
        packed = jnp.concatenate(packed, 0)
        if per == 16:
            packed = jnp.concatenate([packed, ffn_down.reshape(4, 16, D), norms[None]], 0)
            wall = lax.all_gather(packed, ("dp", "seq"), axis=0)
        else:
            packed = jnp.concatenate([packed, ffn_down.reshape(4, per, D)], 0)
            wall = lax.all_gather(packed, ("dp", "seq"), axis=0)
            down = wall[:, 12:].reshape(G, 4, 16, D)
            rest = wall[:, :12].reshape(G, 16 // per, 12, per, D)
            rest = rest.transpose(0, 2, 1, 3, 4).reshape(G, 12, 16, D)
            all_norms = lax.all_gather(norms, ("dp", "seq"), axis=0)
            all_norms = all_norms.astype(F32).reshape(G, n_dev // G, 16, D).sum(1).astype(BF)
            wall = jnp.concatenate([rest, down, all_norms[:, None]], 1)

        def of(x, i):
            return lax.dynamic_index_in_dim(x, i, 0, keepdims=False)

        def top(x):
            return flip("seq", ns, half)(x)

        valid_rows = jnp.pad(of(dec_valid, 1 - mine).astype(BF)[None], ((0, 15), (0, D - tok)))
        got = top(
            jnp.concatenate(
                [of(inputs, 1 - mine), of(encoder, 1 - mine), of(teacher, 1 - mine), valid_rows], 0
            )
        )
        both = jnp.stack(
            [
                jnp.concatenate([of(inputs, mine), got[:tok]], 0),
                jnp.concatenate([of(encoder, mine), got[tok : 2 * tok]], 0),
            ]
        )
        teach = jnp.concatenate([of(teacher, mine), got[2 * tok : 3 * tok]], 0)
        valid = jnp.concatenate([of(dec_valid, mine).astype(F32), got[3 * tok, :tok].astype(F32)])[:, None]
        bit = 1
        while bit < half:
            both = jnp.concatenate([both, flip("seq", ns, bit)(both)], 1)
            bit *= 2
        xf, ef = both[0], both[1]

        slots = jnp.arange(half, dtype=jnp.int32)[:, None]
        pieces = (seq_at ^ slots ^ jnp.array([[0, half]], jnp.int32)).reshape(-1)
        pos = (pieces[:, None] * tok + jnp.arange(tok, dtype=jnp.int32)[None]).reshape(-1)
        dec_k = of(dec_seg, mine).reshape(ns, tok)[pieces].reshape(-1)
        enc_k = of(enc_seg, mine).reshape(ns, tok)[pieces].reshape(-1)
        dec_q = dec_k[:rows]
        ok_self = (dec_k[:, None] == dec_q[None]) & (pos[:, None] <= pos[None, :rows])
        ok_cross = enc_k[:, None] == dec_q[None]
        mask_self = jnp.where(ok_self, 0.0, NEG).astype(F32)
        mask_cross = jnp.where(ok_cross, 0.0, NEG).astype(F32)

        p_shape = (HEADS, length, rows)
        attn_flops = 4 * HEADS * length * rows * 128
        kv_flops = 4 * length * D * D
        q1, kv1, p1, rl1, at1 = call(
            functools.partial(self_forward, rows),
            [(xf, None), (wall, chunks(0, 3)), (mask_self, None)],
            [((rows, D), BF), ((length, 2 * D), BF), (p_shape, BF), ((HEADS, 1, rows), F32), ((D, rows), BF)],
            name="self_forward",
            cost=cost(attn_flops + kv_flops, 9 * MIB),
        )
        xh1, rs1, low1, q2, kv2, p2, rl2, at2 = call(
            functools.partial(cross_forward, rows),
            [(xf, None), (ef, None), (at1, None), (wall, chunks(3, 1)), (wall, chunks(4, 2)),
             (wall, chunks(6, 1)), (wall, NORMS), (mask_cross, None)],
            [((rows, D), F32), ((rows, 1), F32), ((rows, D), BF), ((rows, D), BF), ((length, 2 * D), BF),
             (p_shape, BF), ((HEADS, 1, rows), F32), ((D, rows), BF)],
            name="cross_forward",
            cost=cost(attn_flops + kv_flops, 12 * MIB),
        )
        out, small, d_r2, d_mix2, g_up, g_dn, g_co = call(
            ffn_both,
            [(xh1, None), (at2, None), (teach, None), (valid, None), (wall, chunks(7, 1)),
             (wall, chunks(8, 4)), (wall, chunks(12, 4)), (wall, NORMS)],
            [((rows, D), BF), ((16, D), F32), ((rows, D), F32), ((rows, D), BF), ((G, 4, 16, D), BF),
             ((G, 4, 16, D), BF), ((G, 1, 16, D), BF)],
            scratch=[pltpu.VMEM((rows, FF), BF), pltpu.VMEM((4, rows, D), F32)],
            name="ffn_both",
            cost=cost(12 * rows * D * FF, 12 * MIB),
        )

        back_scratch = [pltpu.VMEM((length, 2 * D), BF), pltpu.VMEM((D, rows), F32)]
        d_enc, g_cin, g_cq, g_so, d_mix1, d_r1, small = call(
            cross_back,
            [(ef, None), (q2, None), (kv2, None), (p2, None), (rl2, None), (d_mix2, None),
             (wall, chunks(4, 2)), (wall, chunks(6, 1)), (wall, chunks(3, 1)), (wall, NORMS),
             (d_r2, None), (low1, None), (xh1, None), (rs1, None), (at1, None), (small, None)],
            [((length, D), BF), ((G, 2, 16, D), BF), ((G, 1, 16, D), BF), ((G, 1, 16, D), BF),
             ((rows, D), BF), ((rows, D), F32), ((16, D), F32)],
            scratch=back_scratch,
            name="cross_back",
            cost=cost(3 * attn_flops + 2 * kv_flops, 14 * MIB),
        )
        d_x, d_own, g_in = call(
            functools.partial(self_back, rows),
            [(xf, None), (q1, None), (kv1, None), (p1, None), (rl1, None), (d_mix1, None),
             (wall, chunks(0, 3)), (d_r1, None)],
            [((length, D), BF), ((rows, D), F32), ((G, 3, 16, D), BF)],
            scratch=back_scratch,
            name="self_back",
            cost=cost(3 * attn_flops + 2 * kv_flops, 14 * MIB),
        )

        def by_device(g):
            if per == 16:
                return g
            n = g.shape[1]
            return g.reshape(G, n, 16 // per, per, D).transpose(0, 2, 1, 3, 4).reshape(n_dev, n, per, D)

        def reduce_to_owner(g, small=None):
            tail = g.shape[1:]
            dp_bits, seq_bits = nd.bit_length() - 1, ns.bit_length() - 1
            acc = g.reshape((2,) * (dp_bits + seq_bits) + tail)
            order = [("dp", 0)] + [("dp", b) for b in range(dp_bits - 1, 0, -1)]
            order += [("seq", b) for b in range(seq_bits)]
            names = [("dp", b) for b in range(dp_bits - 1, -1, -1)]
            names += [("seq", b) for b in range(seq_bits - 1, -1, -1)]
            for axis, b in order:
                at = names.index((axis, b))
                size = nd if axis == "dp" else ns
                here = ((dp_at if axis == "dp" else seq_at) >> b) & 1
                keep = lax.dynamic_index_in_dim(acc, here, at, keepdims=False)
                send = lax.dynamic_index_in_dim(acc, 1 - here, at, keepdims=False).astype(BF)
                shape = send.shape
                send = send.reshape(-1, D)
                if small is not None:
                    low_small = small.astype(BF)
                    send = jnp.concatenate([send, low_small], 0)
                recv = flip(axis, size, 1 << b)(send)
                if small is not None:
                    small = low_small.astype(F32) + recv[-16:].astype(F32)
                    recv = recv[:-16]
                acc = keep.astype(F32) + recv.reshape(shape).astype(F32)
                names.pop(at)
            return acc, small

        def wide(g):
            return g.transpose(1, 0, 2).reshape(per, -1)

        g_dn = g_dn if per == 16 else g_dn.reshape(n_dev, 4, per, D)
        s_ffn, _ = reduce_to_owner(jnp.concatenate([by_device(g_up), g_dn], 1))
        s_mid, _ = reduce_to_owner(
            jnp.concatenate([by_device(g_co), by_device(g_cin), by_device(g_cq), by_device(g_so)], 1)
        )
        lane = lax.broadcasted_iota(jnp.int32, (16, D), 1)
        row = lax.broadcasted_iota(jnp.int32, (16, D), 0)
        count = jnp.sum(dec_valid).astype(F32)
        small = jnp.where((row == 7) & (lane == dev), count, small)
        s_in, small = reduce_to_owner(by_device(g_in), small)
        loss = jnp.sum(small[6]) / (jnp.sum(small[7]) * D)
        g_norm = lax.dynamic_slice(small, (0, dev * per), (6, per))

        def rows_to_owner(part):
            bit = half // 2
            acc = part
            while bit:
                cut_at = bit * rows
                acc = acc[:cut_at].astype(F32) + flip("seq", ns, bit)(acc[cut_at:].astype(BF)).astype(F32)
                bit //= 2
            return acc

        e_own = rows_to_owner(d_enc)
        x_own = rows_to_owner(d_x) + d_own

        def back_home(kept, recv):
            return jnp.where(mine == 0, jnp.stack([kept, recv]), jnp.stack([recv, kept]))

        home = top(jnp.concatenate([out[tok:], x_own[tok:].astype(BF), e_own[tok:].astype(BF)], 0))
        outputs = back_home(out[:tok], home[:tok])
        grad_inputs = back_home(x_own[:tok], home[tok : 2 * tok].astype(F32))
        grad_encoder = back_home(e_own[:tok], home[2 * tok :].astype(F32))
        return (
            outputs,
            loss,
            grad_inputs,
            grad_encoder,
            wide(s_in),
            wide(s_mid[4:5]),
            wide(s_mid[3:4]),
            wide(s_mid[1:3]),
            wide(s_mid[0:1]),
            wide(s_ffn[:4]),
            s_ffn[4:].reshape(4 * per, D),
            g_norm[:3],
            g_norm[3:],
        )

    return shards


def solution(mesh):
    rows, both = P("dp", "seq", None), P(("dp", "seq"), None)
    norm = P(None, ("dp", "seq"))
    return jax.shard_map(
        make_shards(mesh.shape["dp"], mesh.shape["seq"]),
        mesh=mesh,
        in_specs=(rows, rows, rows, P("dp", None), P("dp", None), P("dp", "seq")) + (both,) * 7 + (norm, norm),
        out_specs=(rows, P(), rows, rows) + (both,) * 7 + (norm, norm),
        check_vma=False,
    )
```

```python
import functools

import jax
import jax.numpy as jnp
from jax import lax
from jax.experimental import pallas as pl
from jax.experimental.pallas import tpu as pltpu
from jax.sharding import PartitionSpec as P

HEADS = 8
HEAD_DIM = 64
EPS = 1e-5
NEG = -1e30
SCALE = 0.125
D = 512
FF = 2048
HALF = 256
G = 32
BF = jnp.bfloat16
F32 = jnp.float32
MIB = 1 << 20

N_PACK = 17

NN = (((1,), (0,)), ((), ()))
NT = (((1,), (1,)), ((), ()))
TN = (((0,), (0,)), ((), ()))


def dot(a, b, dims=NN):
    return lax.dot_general(a, b, dims, preferred_element_type=F32)


def whole(shape):
    return pl.BlockSpec(shape, lambda i: (0,) * len(shape))


def chunks(first, count):
    return pl.BlockSpec((G, count, 16, D), lambda i: (0, first // count, 0, 0))


SMEM = pl.BlockSpec(memory_space=pltpu.SMEM)
NORMS = pl.BlockSpec((G, 1, 16, D), lambda i: (0, 16, 0, 0))


def call(body, ins, outs, scratch=(), name=None):
    return pl.pallas_call(
        body,
        grid=(1,),
        in_specs=[whole(a.shape) if s is None else s for a, s in ins],
        out_specs=[whole(s) for s, _ in outs],
        out_shape=[jax.ShapeDtypeStruct(s, t) for s, t in outs],
        scratch_shapes=list(scratch),
        compiler_params=pltpu.CompilerParams(vmem_limit_bytes=56 * MIB),
        name=name,
    )(*[a for a, _ in ins])


def weight(ref, j):
    return ref[:, j].reshape(D, D)


def norm_rows(ref):
    return jnp.sum(ref[:, 0].astype(F32), axis=0)


def norm_forward(resid, gain, bias):
    centre = resid - jnp.mean(resid, axis=-1, keepdims=True)
    rstd = lax.rsqrt(jnp.mean(centre * centre, axis=-1, keepdims=True) + EPS)
    xhat = centre * rstd
    return xhat, rstd, xhat * gain + bias


def norm_back(g, xhat, rstd, gain):
    e = g * gain
    m1 = jnp.mean(e, axis=-1, keepdims=True)
    m2 = jnp.mean(e * xhat, axis=-1, keepdims=True)
    dr = (e - m1 - xhat * m2) * rstd
    return dr, jnp.sum(g * xhat, axis=0, keepdims=True), jnp.sum(g, axis=0, keepdims=True)


def head_half(x, e):
    lane = lax.broadcasted_iota(jnp.int32, x.shape, 1)
    return jnp.where((lane < HEAD_DIM) == (e == 0), x, jnp.zeros_like(x))


def attend(q_ref, kv_ref, mask_ref, p_ref, rl_ref, at_ref):
    def pair(hp, carry):
        c0 = pl.multiple_of(hp * 128, 128)
        k2 = kv_ref[:, pl.ds(c0, 128)]
        v2 = kv_ref[:, pl.ds(pl.multiple_of(D + c0, 128), 128)]
        q2 = q_ref[:, pl.ds(c0, 128)]
        for e in range(2):
            s = dot(k2, head_half(q2, e), NT) + mask_ref[...]
            p = jnp.exp(s - jnp.max(s, axis=0, keepdims=True))
            rl = 1.0 / jnp.sum(p, axis=0, keepdims=True)
            pb = p.astype(BF)
            p_ref[2 * hp + e] = pb
            rl_ref[2 * hp + e] = rl
            o = dot(v2, pb, TN) * rl
            at_ref[pl.ds(pl.multiple_of((2 * hp + e) * HEAD_DIM, HEAD_DIM), HEAD_DIM), :] = o[
                e * HEAD_DIM : (e + 1) * HEAD_DIM
            ].astype(BF)
        return carry

    lax.fori_loop(0, HEADS // 2, pair, 0)


def attend_back(first, q_ref, kv_ref, p_ref, rl_ref, do_ref, dkv_ref, dqt_ref):
    def pair(i, carry):
        hp = first // 2 + i
        c0 = pl.multiple_of(hp * 128, 128)
        o0 = pl.multiple_of(i * 128, 128)
        k2 = kv_ref[:, pl.ds(c0, 128)]
        v2 = kv_ref[:, pl.ds(pl.multiple_of(D + c0, 128), 128)]
        q2 = q_ref[:, pl.ds(c0, 128)]
        do2 = do_ref[:, pl.ds(c0, 128)]
        dk = dv = None
        for e in range(2):
            dom = head_half(do2, e)
            dp = dot(v2, dom, NT)
            p = p_ref[2 * hp + e].astype(F32) * rl_ref[2 * hp + e]
            t = p * dp
            ds = (t - p * jnp.sum(t, axis=0, keepdims=True)).astype(BF)
            dk_e = dot(ds, head_half(q2, e))
            dv_e = dot(p.astype(BF), dom)
            dk = dk_e if dk is None else dk + dk_e
            dv = dv_e if dv is None else dv + dv_e
            dqt = dot(k2, ds, TN) * SCALE
            dqt_ref[pl.ds(pl.multiple_of((2 * i + e) * HEAD_DIM, HEAD_DIM), HEAD_DIM), :] = dqt[
                e * HEAD_DIM : (e + 1) * HEAD_DIM
            ]
        dkv_ref[:, pl.ds(o0, 128)] = dk.astype(BF)
        dkv_ref[:, pl.ds(pl.multiple_of(HALF + o0, 128), 128)] = dv.astype(BF)
        return carry

    lax.fori_loop(0, HEADS // 4, pair, 0)


def cols(ref, c, width):
    picks = [ref[:, pl.ds(pl.multiple_of((2 * y + c) * width, width), width)] for y in range(2)]
    return jnp.concatenate(picks, 1)


def rows_of(ref, c, width):
    picks = [ref[pl.ds(pl.multiple_of((2 * y + c) * width, width), width), :] for y in range(2)]
    return jnp.concatenate(picks, 0)


def put_half(ref, lhs, dq, dk, dv, lhs_q):
    a = jnp.concatenate([dot(lhs_q, dq, TN), dot(lhs, dk, TN)], 1)
    ref[:, :, 0:16] = a.astype(BF).reshape(2, 8, 16, D)
    v = dot(lhs, dv, TN).reshape(2, 8, 2, 8, HALF)
    ref[:, :, 16:24] = jnp.concatenate([v[:, :, 0], v[:, :, 1]], -1).astype(BF)


def self_forward(rows, xf, w, mask, q, kv, p, rl, at):
    q[...] = (dot(xf[:rows], weight(w, 0)).astype(BF).astype(F32) * SCALE).astype(BF)
    kv[:, :D] = dot(xf[...], weight(w, 1)).astype(BF)
    kv[:, D:] = dot(xf[...], weight(w, 2)).astype(BF)
    attend(q, kv, mask, p, rl, at)


def cross_forward(rows, xf, ef, at1, w_out, w_cin, w_cq, norms, mask, xh1, rs1, low1, q, kv, p, rl, at):
    gb = norm_rows(norms)
    resid = xf[:rows].astype(F32) + dot(at1[...], weight(w_out, 0), TN)
    xhat, rstd, n1 = norm_forward(resid, gb[0:1], gb[3:4])
    xh1[...] = xhat
    rs1[...] = rstd
    low1[...] = n1.astype(BF)
    q[...] = (dot(low1[...], weight(w_cq, 0)).astype(BF).astype(F32) * SCALE).astype(BF)
    kv[:, :D] = dot(ef[...], weight(w_cin, 0)).astype(BF)
    kv[:, D:] = dot(ef[...], weight(w_cin, 1)).astype(BF)
    attend(q, kv, mask, p, rl, at)


def ffn_both(core, xh1, at2, teach, valid, w_co, w_up, w_dn, norms,
             out, small, d_r2, d_mix, keep, send, act, hid, low2):
    gb = norm_rows(norms)
    n1 = xh1[...] * gb[0:1] + gb[3:4]
    wco = weight(w_co, 0)
    xh2, rs2, n2 = norm_forward(n1 + dot(at2[...], wco, TN), gb[1:2], gb[4:5])
    low2[...] = n2.astype(BF)
    for j in range(4):
        h = dot(low2[...], weight(w_up, j))
        hid[j] = h
        act[:, j * D : (j + 1) * D] = (h / (1.0 + jnp.exp(-h))).astype(BF)
    wdn = w_dn[...].reshape(FF, D)
    r3 = n2 + dot(act[...], wdn)
    xh3, rs3, final = norm_forward(r3, gb[2:3], gb[5:6])
    out[...] = final.astype(BF)
    err = (final - teach[...].astype(F32)) * valid[...]
    small[...] = jnp.zeros_like(small)
    small[6:7] = jnp.sum(err * err, axis=0, keepdims=True)
    d_r3, dg, db = norm_back(err, xh3, rs3, gb[2:3])
    small[2:3] = dg
    small[5:6] = db
    dffn = d_r3.astype(BF)
    c = core[0]
    sides = ((send, 1 - c), (keep, c))
    for ref, at in sides:
        ref[:, :, 4:8] = dot(cols(act, at, FF // 4), dffn, TN).astype(BF).reshape(2, 8, 4, 16, D)
    dn2 = d_r3
    for j in range(4):
        da = dot(dffn, wdn[j * D : (j + 1) * D], NT)
        h = hid[j]
        sig = 1.0 / (1.0 + jnp.exp(-h))
        dh = (da * (sig * (1.0 + h * (1.0 - sig)))).astype(BF)
        for ref, at in sides:
            ref[:, :, j] = dot(cols(low2, at, 128), dh, TN).astype(BF).reshape(2, 8, 16, D)
        dn2 = dn2 + dot(dh, weight(w_up, j), NT)
    dr2, dg, db = norm_back(dn2, xh2, rs2, gb[1:2])
    small[1:2] = dg
    small[4:5] = db
    d_r2[...] = dr2
    dcross = dr2.astype(BF)
    for ref, at in sides:
        ref[:, :, 8] = dot(rows_of(at2, at, 128), dcross).astype(BF).reshape(2, 8, 16, D)
    d_mix[...] = dot(dcross, wco, NT).astype(BF)


def cross_back_a(q, kv, p, rl, d_mix, dkv, dq, dqt):
    attend_back(0, q, kv, p, rl, d_mix, dkv, dqt)
    dq[...] = jnp.transpose(dqt[...]).astype(BF)


def project(dkv_a, dkv_b, wk, wv):
    out = dot(dkv_a[:, :HALF], wk[:, :HALF], NT) + dot(dkv_b[:, :HALF], wk[:, HALF:], NT)
    return out + dot(dkv_a[:, HALF:], wv[:, :HALF], NT) + dot(dkv_b[:, HALF:], wv[:, HALF:], NT)


def cross_back_b(core, ef, q, kv, p, rl, d_mix, dkv_a, dq_a, w_cin, w_cq, w_out, norms, d_r2, low1, xh1,
                 rs1, at1, small_in, d_enc, d_mix1, d_r1, small, keep, send, dkv, dqt):
    attend_back(4, q, kv, p, rl, d_mix, dkv, dqt)
    d_enc[...] = project(dkv_a, dkv, weight(w_cin, 0), weight(w_cin, 1)).astype(BF)
    dq = jnp.concatenate([dq_a[...], jnp.transpose(dqt[...]).astype(BF)], 1)
    gb = norm_rows(norms)
    dn1 = d_r2[...] + dot(dq, weight(w_cq, 0), NT)
    dr1, dg, db = norm_back(dn1, xh1[...], rs1[...], gb[0:1])
    small[...] = small_in[...]
    small[0:1] = dg
    small[3:4] = db
    d_r1[...] = dr1
    dself = dr1.astype(BF)
    c = core[0]
    for ref, at in ((send, 1 - c), (keep, c)):
        lhs = cols(ef, at, 128)
        for j in range(2):
            span = slice(j * HALF, (j + 1) * HALF)
            g = jnp.concatenate([dot(lhs, dkv_a[:, span], TN), dot(lhs, dkv[:, span], TN)], 1)
            ref[:, :, j] = g.astype(BF).reshape(2, 8, 16, D)
        ref[:, :, 2] = dot(cols(low1, at, 128), dq, TN).astype(BF).reshape(2, 8, 16, D)
        ref[:, :, 3] = dot(rows_of(at1, at, 128), dself).astype(BF).reshape(2, 8, 16, D)
    d_mix1[...] = dot(dself, weight(w_out, 0), NT).astype(BF)


def self_back_a(rows, core, xf, q, kv, p, rl, d_mix, dkv, dq, keep, send, dqt):
    attend_back(0, q, kv, p, rl, d_mix, dkv, dqt)
    dq[...] = jnp.transpose(dqt[...]).astype(BF)
    c = core[0]
    for ref, at in ((send, 1 - c), (keep, c)):
        lhs = cols(xf, at, 128)
        put_half(ref, lhs, dq[...], dkv[:, :HALF], dkv[:, HALF:], lhs[:rows])


def self_back_b(rows, core, xf, q, kv, p, rl, d_mix, dkv_a, dq_a, w, d_r1, d_x, d_own, keep, send, dkv, dqt):
    attend_back(4, q, kv, p, rl, d_mix, dkv, dqt)
    d_x[...] = project(dkv_a, dkv, weight(w, 1), weight(w, 2)).astype(BF)
    dq = jnp.transpose(dqt[...]).astype(BF)
    d_own[...] = d_r1[...] + dot(jnp.concatenate([dq_a[...], dq], 1), weight(w, 0), NT)
    c = core[0]
    for ref, at in ((send, 1 - c), (keep, c)):
        lhs = cols(xf, at, 128)
        put_half(ref, lhs, dq, dkv[:, :HALF], dkv[:, HALF:], lhs[:rows])


def flip(axis, size, bit):
    return functools.partial(
        lax.ppermute, axis_name=axis, perm=[(i, i ^ bit) for i in range(size)]
    )


def tie(x, *deps):
    return lax.optimization_barrier((x, *deps))[0]


def pick(x, i, at):
    if isinstance(i, int):
        return lax.index_in_dim(x, i, at, keepdims=False)
    return lax.dynamic_index_in_dim(x, i, at, keepdims=False)


class Halved:
    def __init__(self, terms, axes):
        self.terms, self.axes = list(terms), list(axes)

    def total(self, terms=None):
        terms = self.terms if terms is None else terms
        return sum(t.astype(F32) for t in terms[1:]) + terms[0].astype(F32) if len(terms) > 1 else terms[0].astype(F32)

    def give(self, bit, here):
        at = self.axes.index(bit)
        away = [pick(t, 1 - here, at) for t in self.terms]
        self.terms = [pick(t, here, at) for t in self.terms]
        self.axes.pop(at)
        return self.total(away).astype(BF)

    def take(self, got):
        self.terms.append(got)


class Everywhere(Halved):
    def give(self, bit, here):
        self.terms = [self.total().astype(BF)]
        return self.terms[0]


class Near(Halved):
    def give(self, bit, here):
        return super().give(bit, 0)


def make_shards(nd, ns):
    n_dev = nd * ns
    half = ns // 2
    per = G * 16 // n_dev

    def shards(inputs, encoder, teacher, dec_seg, enc_seg, dec_valid, self_in, self_out,
               cross_query, cross_in, cross_out, ffn_up, ffn_down, norm_gain, norm_bias):
        tok = inputs.shape[1]
        rows = 2 * tok
        length = dec_seg.shape[1]
        dp_at, seq_at = lax.axis_index("dp"), lax.axis_index("seq")
        dev = dp_at * ns + seq_at
        mine = seq_at // half

        def cut(w):
            return w.reshape(per, w.shape[1] // D, D).transpose(1, 0, 2)

        norms = lax.dynamic_update_slice(
            jnp.zeros((16, D), BF), jnp.concatenate([norm_gain, norm_bias], 0), (0, dev * per)
        )
        packed = [cut(self_in), cut(self_out), cut(cross_in), cut(cross_query), cut(cross_out), cut(ffn_up)]
        packed = jnp.concatenate(packed, 0)
        if per == 16:
            packed = jnp.concatenate([packed, ffn_down.reshape(4, 16, D), norms[None]], 0)
            wall = lax.all_gather(packed, ("dp", "seq"), axis=0)
        else:
            packed = jnp.concatenate([packed, ffn_down.reshape(4, per, D)], 0)
            wall = lax.all_gather(packed, ("dp", "seq"), axis=0)
            down = wall[:, 12:].reshape(G, 4, 16, D)
            rest = wall[:, :12].reshape(G, 16 // per, 12, per, D)
            rest = rest.transpose(0, 2, 1, 3, 4).reshape(G, 12, 16, D)
            all_norms = lax.all_gather(norms, ("dp", "seq"), axis=0)
            all_norms = all_norms.astype(F32).reshape(G, n_dev // G, 16, D).sum(1).astype(BF)
            wall = jnp.concatenate([rest, down, all_norms[:, None]], 1)

        def of(x, i):
            return lax.dynamic_index_in_dim(x, i, 0, keepdims=False)

        def top(x):
            return flip("seq", ns, half)(x)

        valid_rows = jnp.pad(of(dec_valid, 1 - mine).astype(BF)[None], ((0, 15), (0, D - tok)))
        got = top(
            jnp.concatenate(
                [of(inputs, 1 - mine), of(encoder, 1 - mine), of(teacher, 1 - mine), valid_rows], 0
            )
        )
        both = jnp.stack(
            [
                jnp.concatenate([of(inputs, mine), got[:tok]], 0),
                jnp.concatenate([of(encoder, mine), got[tok : 2 * tok]], 0),
            ]
        )
        teach = jnp.concatenate([of(teacher, mine), got[2 * tok : 3 * tok]], 0)
        valid = jnp.concatenate([of(dec_valid, mine).astype(F32), got[3 * tok, :tok].astype(F32)])[:, None]
        bit = 1
        while bit < half:
            both = jnp.concatenate([both, flip("seq", ns, bit)(both)], 1)
            bit *= 2
        xf, ef = both[0], both[1]

        slots = jnp.arange(half, dtype=jnp.int32)[:, None]
        pieces = (seq_at ^ slots ^ jnp.array([[0, half]], jnp.int32)).reshape(-1)
        pos = (pieces[:, None] * tok + jnp.arange(tok, dtype=jnp.int32)[None]).reshape(-1)
        dec_k = of(dec_seg, mine).reshape(ns, tok)[pieces].reshape(-1)
        enc_k = of(enc_seg, mine).reshape(ns, tok)[pieces].reshape(-1)
        dec_q = dec_k[:rows]
        ok_self = (dec_k[:, None] == dec_q[None]) & (pos[:, None] <= pos[None, :rows])
        ok_cross = enc_k[:, None] == dec_q[None]
        mask_self = jnp.where(ok_self, 0.0, NEG).astype(F32)
        mask_cross = jnp.where(ok_cross, 0.0, NEG).astype(F32)

        p_shape = (HEADS, length, rows)
        q1, kv1, p1, rl1, at1 = call(
            functools.partial(self_forward, rows),
            [(xf, None), (wall, chunks(0, 3)), (mask_self, None)],
            [((rows, D), BF), ((length, 2 * D), BF), (p_shape, BF), ((HEADS, 1, rows), F32), ((D, rows), BF)],
            name="self_forward",
        )
        xh1, rs1, low1, q2, kv2, p2, rl2, at2 = call(
            functools.partial(cross_forward, rows),
            [(xf, None), (ef, None), (at1, None), (wall, chunks(3, 1)), (wall, chunks(4, 2)),
             (wall, chunks(6, 1)), (wall, NORMS), (mask_cross, None)],
            [((rows, D), F32), ((rows, 1), F32), ((rows, D), BF), ((rows, D), BF), ((length, 2 * D), BF),
             (p_shape, BF), ((HEADS, 1, rows), F32), ((D, rows), BF)],
            name="cross_forward",
        )
        core = ((dp_at & 1) if nd == 4 and ns == 8 else jnp.zeros_like(dp_at)).astype(jnp.int32)[None]
        out, small, d_r2, d_mix2, keep1, send1 = call(
            ffn_both,
            [(core, SMEM), (xh1, None), (at2, None), (teach, None), (valid, None), (wall, chunks(7, 1)),
             (wall, chunks(8, 4)), (wall, chunks(12, 4)), (wall, NORMS)],
            [((rows, D), BF), ((16, D), F32), ((rows, D), F32), ((rows, D), BF)] + [((2, 8, 9, 16, D), BF)] * 2,
            scratch=[pltpu.VMEM((rows, FF), BF), pltpu.VMEM((4, rows, D), F32), pltpu.VMEM((rows, D), BF)],
            name="ffn_both",
        )

        kv_half = [((length, D), BF), ((rows, HALF), BF)]
        d_rows = [pltpu.VMEM((HALF, rows), F32)]
        both_scratch = [pltpu.VMEM((length, D), BF)] + d_rows
        halves = lambda n: [((2, 8, n, 16, D), BF)] * 2
        packed = [((2, 8, 24, D), BF)] * 2

        def trade(bit, *groups):
            axis, b = bit
            size, at = (nd, dp_at) if axis == "dp" else (ns, seq_at)
            sends = [g.give(bit, (at >> b) & 1) for g in groups]
            flat = [x.reshape(-1, D) for x in sends]
            got = flip(axis, size, 1 << b)(flat[0] if len(flat) == 1 else jnp.concatenate(flat, 0))
            start = 0
            for g, x, f in zip(groups, sends, flat):
                g.take(lax.slice_in_dim(got, start, start + f.shape[0]).reshape(x.shape))
                start += f.shape[0]
            return got

        def other_core(x):
            return flip("dp", nd, 1)(x)

        core_bit, y_bit = ("dp", 0), ("dp", 1)
        x_bit, zl_bit, zh_bit = ("seq", 0), ("seq", 1), ("seq", 2)
        fast = nd == 4 and ns == 8

        def weight_sum(keep, got):
            split = (2, 2, 2, 2) + keep.shape[2:]
            return Halved([keep.reshape(split), got.reshape(split)], [y_bit, zh_bit, zl_bit, x_bit])

        got1 = other_core(send1)
        dkv2, dq2 = call(
            cross_back_a,
            [(q2, None), (kv2, None), (p2, None), (rl2, None), (d_mix2, None)],
            kv_half,
            scratch=d_rows,
            name="cross_back_a",
        )
        d_enc, d_mix1, d_r1, small, keep2, send2 = call(
            cross_back_b,
            [(core, SMEM), (ef, None), (q2, None), (kv2, None), (p2, None), (rl2, None),
             (tie(d_mix2, got1), None), (dkv2, None), (dq2, None), (wall, chunks(4, 2)), (wall, chunks(6, 1)),
             (wall, chunks(3, 1)), (wall, NORMS), (d_r2, None), (low1, None), (xh1, None), (rs1, None),
             (at1, None), (small, None)],
            [((length, D), BF), ((rows, D), BF), ((rows, D), F32), ((16, D), F32)] + halves(4),
            scratch=both_scratch,
            name="cross_back_b",
        )
        lane = lax.broadcasted_iota(jnp.int32, (16, D), 1)
        row = lax.broadcasted_iota(jnp.int32, (16, D), 0)
        small = jnp.where((row == 7) & (lane == dev), jnp.sum(dec_valid).astype(F32), small)
        small = Everywhere([small], [])

        def own_first(part):
            return Near([part.reshape((2,) * (half.bit_length() - 1) + (rows, D))],
                        [("seq", b) for b in range(half.bit_length() - 2, -1, -1)])

        self_a = [(core, SMEM), (xf, None), (q1, None), (kv1, None), (p1, None), (rl1, None), (d_mix1, None)]
        self_b_outs = [((length, D), BF), ((rows, D), F32)] + packed
        enc = own_first(d_enc)
        if fast:
            group1 = weight_sum(keep1, got1)
            trade(y_bit, group1)
            got2 = other_core(send2)
            got_e = trade(x_bit, enc)
            dkv1, dq1, keep3, send3 = call(
                functools.partial(self_back_a, rows), self_a, kv_half + packed, scratch=d_rows, name="self_back_a"
            )
            got3 = other_core(send3)
            trade(zl_bit, enc)
            self_b = self_a[:-1] + [(tie(d_mix1, got2, got_e), None)]
        else:
            dkv1, dq1, keep3, send3 = call(
                functools.partial(self_back_a, rows), self_a, kv_half + packed, scratch=d_rows, name="self_back_a"
            )
            self_b = self_a
        d_x, d_own, keep4, send4 = call(
            functools.partial(self_back_b, rows),
            self_b + [(dkv1, None), (dq1, None), (wall, chunks(0, 3)), (d_r1, None)],
            self_b_outs,
            scratch=both_scratch,
            name="self_back_b",
        )
        dx = own_first(d_x)

        def back_home(kept, recv):
            return jnp.where(mine == 0, jnp.stack([kept, recv]), jnp.stack([recv, kept]))

        def wide(g):
            return g.transpose(1, 0, 2).reshape(per, -1)

        def unpack(a, b):
            def three(g):
                v = g[..., 16:, :]
                v = jnp.concatenate([v[..., :HALF], v[..., HALF:]], -2)
                return g[..., :16, :HALF], g[..., :16, HALF:], v

            parts = [x for pair in zip(three(a), three(b)) for x in pair]
            return jnp.concatenate(parts, -1)

        if fast:
            e_own = enc.total()
            home = top(jnp.concatenate([out[tok:], e_own[tok:].astype(BF)], 0))
            group2, group3 = weight_sum(keep2, got2), weight_sum(keep3, got3)
            trade(y_bit, group2, group3)
            trade(zl_bit, group1)
            trade(x_bit, dx)
            low_small = small.give(core_bit, 0)
            got4 = other_core(jnp.concatenate([send4.reshape(-1, D), low_small], 0))
            small.take(got4[-16:])
            group4 = weight_sum(keep4, got4[:-16])
            trade(zl_bit, dx)
            trade(x_bit, group1, group2, group3)
            trade(y_bit, group4, small)
            x_own = dx.total() + d_own
            away_x = x_own[tok:].astype(BF)
            away_1 = group1.give(zh_bit, (seq_at >> 2) & 1)
            got = top(jnp.concatenate([away_x, away_1.reshape(-1, D)], 0))
            home_x = got[:tok]
            group1.take(got[tok:].reshape(away_1.shape))
            trade(x_bit, group4, small)
            trade(zl_bit, group2, group3, group4, small)
            trade(zh_bit, group2, group3, group4, small)
            s1, s2, small = group1.total(), group2.total(), small.total()
            g_up, g_down, g_co = wide(s1[:4]), s1[4:8].reshape(4 * per, D), s1[8]
            g_cin, g_cq, g_so = wide(s2[:2]), s2[2], s2[3]
            g_in = unpack(group3.total(), group4.total())
        else:
            for b in range(half.bit_length() - 1):
                trade(("seq", b), enc, dx)
            e_own = enc.total()
            x_own = dx.total() + d_own
            home = top(jnp.concatenate([out[tok:], e_own[tok:].astype(BF), x_own[tok:].astype(BF)], 0))
            home_x = home[2 * tok :]
            small = lax.psum(small.terms[0], ("dp", "seq"))

            def summed(g):
                return lax.psum_scatter(g, ("dp", "seq"), scatter_dimension=0, tiled=True).astype(F32)

            def rejoin(keep, send):
                g = jnp.stack([keep, send], 1)
                return g.reshape((G,) + g.shape[3:])

            def full(g):
                return g.transpose(0, 2, 1, 3).reshape(G * 16, -1)

            all1, all2 = rejoin(keep1, send1), rejoin(keep2, send2)
            g_up = summed(full(all1[:, :4]))
            g_down = summed(all1[:, 4:8].reshape(FF, D))
            g_co = summed(full(all1[:, 8:]))
            g_cin, g_cq, g_so = summed(full(all2[:, :2])), summed(full(all2[:, 2:3])), summed(full(all2[:, 3:]))
            g_in = summed(unpack(rejoin(keep3, send3), rejoin(keep4, send4)).reshape(G * 16, -1))

        loss = jnp.sum(small[6]) / (jnp.sum(small[7]) * D)
        g_norm = lax.dynamic_slice(small, (0, dev * per), (6, per))
        outputs = back_home(out[:tok], home[:tok])
        grad_encoder = back_home(e_own[:tok], home[tok : 2 * tok].astype(F32))
        grad_inputs = back_home(x_own[:tok], home_x.astype(F32))
        return (outputs, loss, grad_inputs, grad_encoder, g_in, g_so, g_cq, g_cin, g_co, g_up, g_down,
                g_norm[:3], g_norm[3:])

    return shards


def solution(mesh):
    rows, both = P("dp", "seq", None), P(("dp", "seq"), None)
    norm = P(None, ("dp", "seq"))
    return jax.shard_map(
        make_shards(mesh.shape["dp"], mesh.shape["seq"]),
        mesh=mesh,
        in_specs=(rows, rows, rows, P("dp", None), P("dp", None), P("dp", "seq")) + (both,) * 7 + (norm, norm),
        out_specs=(rows, P(), rows, rows) + (both,) * 7 + (norm, norm),
        check_vma=False,
    )
```

```python
import functools

import jax
import jax.numpy as jnp
from jax import lax
from jax.experimental import pallas as pl
from jax.experimental.pallas import tpu as pltpu
from jax.sharding import PartitionSpec as P

HEADS = 8
HEAD_DIM = 64
EPS = 1e-5
NEG = -1e30
SCALE = 0.125
D = 512
FF = 2048
HALF = 256
G = 32
BF = jnp.bfloat16
F32 = jnp.float32
MIB = 1 << 20

PLACE_1, PLACE_2, SLOT = 1, 17, 33

NN = (((1,), (0,)), ((), ()))
NT = (((1,), (1,)), ((), ()))
TN = (((0,), (0,)), ((), ()))


def dot(a, b, dims=NN):
    return lax.dot_general(a, b, dims, preferred_element_type=F32)


def whole(shape):
    return pl.BlockSpec(shape, lambda i: (0,) * len(shape))


SMEM = pl.BlockSpec(memory_space=pltpu.SMEM)


def chunks(first, count):
    return pl.BlockSpec((G, count, 16, D), lambda i: (0, first // count, 0, 0))


def whole_weight(ref, j):
    return ref[:, j].reshape(D, D)


def call(body, ins, outs, scratch=(), name=None):
    return pl.pallas_call(
        body,
        grid=(1,),
        in_specs=[whole(a.shape) if s is None else s for a, s in ins],
        out_specs=[whole(s) for s, _ in outs],
        out_shape=[jax.ShapeDtypeStruct(s, t) for s, t in outs],
        scratch_shapes=list(scratch),
        compiler_params=pltpu.CompilerParams(vmem_limit_bytes=56 * MIB),
        name=name,
        cost_estimate=pl.CostEstimate(flops=1000, bytes_accessed=1000, transcendentals=0),
    )(*[a for a, _ in ins])


def weight(ids, near, far, j):
    picks = []
    for g in range(G):
        at = ids[SLOT + g]
        low = at & (G // 2 - 1)
        picks.append(jnp.where(at < G // 2, near[low, j], far[low, j]))
    return jnp.concatenate(picks, 0)


def norm_rows(ref):
    return jnp.sum(ref[:, 0].astype(F32), axis=0)


def put(ids, first, ref, j, value):
    value = value.astype(BF)
    for i in range(16):
        ref[ids[first + i], j] = value[16 * i : 16 * i + 16]


def norm_forward(resid, gain, bias):
    centre = resid - jnp.mean(resid, axis=-1, keepdims=True)
    rstd = lax.rsqrt(jnp.mean(centre * centre, axis=-1, keepdims=True) + EPS)
    xhat = centre * rstd
    return xhat, rstd, xhat * gain + bias


def norm_back(g, xhat, rstd, gain):
    e = g * gain
    m1 = jnp.mean(e, axis=-1, keepdims=True)
    m2 = jnp.mean(e * xhat, axis=-1, keepdims=True)
    dr = (e - m1 - xhat * m2) * rstd
    return dr, jnp.sum(g * xhat, axis=0, keepdims=True), jnp.sum(g, axis=0, keepdims=True)


def head_half(x, e):
    lane = lax.broadcasted_iota(jnp.int32, x.shape, 1)
    return jnp.where((lane < HEAD_DIM) == (e == 0), x, jnp.zeros_like(x))


def attend(q_ref, kv_ref, mask_ref, p_ref, rl_ref, at_ref):
    def pair(hp, carry):
        c0 = pl.multiple_of(hp * 128, 128)
        k2 = kv_ref[:, pl.ds(c0, 128)]
        v2 = kv_ref[:, pl.ds(pl.multiple_of(D + c0, 128), 128)]
        q2 = q_ref[:, pl.ds(c0, 128)]
        for e in range(2):
            s = dot(k2, head_half(q2, e), NT) + mask_ref[...]
            p = jnp.exp(s - jnp.max(s, axis=0, keepdims=True))
            rl = 1.0 / jnp.sum(p, axis=0, keepdims=True)
            pb = p.astype(BF)
            p_ref[2 * hp + e] = pb
            rl_ref[2 * hp + e] = rl
            o = dot(v2, pb, TN) * rl
            at_ref[pl.ds(pl.multiple_of((2 * hp + e) * HEAD_DIM, HEAD_DIM), HEAD_DIM), :] = o[
                e * HEAD_DIM : (e + 1) * HEAD_DIM
            ].astype(BF)
        return carry

    lax.fori_loop(0, HEADS // 2, pair, 0)


def attend_back(first, q_ref, kv_ref, p_ref, rl_ref, do_ref, dkv_ref, dqt_ref):
    def pair(i, carry):
        hp = first // 2 + i
        c0 = pl.multiple_of(hp * 128, 128)
        o0 = pl.multiple_of(i * 128, 128)
        k2 = kv_ref[:, pl.ds(c0, 128)]
        v2 = kv_ref[:, pl.ds(pl.multiple_of(D + c0, 128), 128)]
        q2 = q_ref[:, pl.ds(c0, 128)]
        do2 = do_ref[:, pl.ds(c0, 128)]
        dk = dv = None
        for e in range(2):
            dom = head_half(do2, e)
            dp = dot(v2, dom, NT)
            p = p_ref[2 * hp + e].astype(F32) * rl_ref[2 * hp + e]
            t = p * dp
            ds = (t - p * jnp.sum(t, axis=0, keepdims=True)).astype(BF)
            dk_e = dot(ds, head_half(q2, e))
            dv_e = dot(p.astype(BF), dom)
            dk = dk_e if dk is None else dk + dk_e
            dv = dv_e if dv is None else dv + dv_e
            dqt = dot(k2, ds, TN) * SCALE
            dqt_ref[pl.ds(pl.multiple_of((2 * i + e) * HEAD_DIM, HEAD_DIM), HEAD_DIM), :] = dqt[
                e * HEAD_DIM : (e + 1) * HEAD_DIM
            ]
        dkv_ref[:, pl.ds(o0, 128)] = dk.astype(BF)
        dkv_ref[:, pl.ds(pl.multiple_of(HALF + o0, 128), 128)] = dv.astype(BF)
        return carry

    lax.fori_loop(0, HEADS // 4, pair, 0)


def cols(ref, c, width):
    picks = [ref[:, pl.ds(pl.multiple_of((2 * y + c) * width, width), width)] for y in range(2)]
    return jnp.concatenate(picks, 1)


def rows_of(ref, c, width):
    picks = [ref[pl.ds(pl.multiple_of((2 * y + c) * width, width), width), :] for y in range(2)]
    return jnp.concatenate(picks, 0)


def put_half(ids, ref, lhs, dq, dk, dv, lhs_q):
    qk = jnp.concatenate([dot(lhs_q, dq, TN), dot(lhs, dk, TN)], 1).astype(BF)
    v = dot(lhs, dv, TN)
    for i in range(16):
        at = ids[PLACE_2 + i]
        ref[at, 0:16] = qk[16 * i : 16 * i + 16]
        ref[at, 16:24] = jnp.concatenate([v[16 * i : 16 * i + 8], v[16 * i + 8 : 16 * i + 16]], 1).astype(BF)


def sides(ids, keep, send):
    return ((send, 1 - ids[0]), (keep, ids[0]))


def pack(s_in, s_out, c_in, c_q, c_out, up, down, gain, bias, at, pa, pb):
    for j in range(3):
        pa[j] = s_in[:, j * D : (j + 1) * D]
    pb[8] = s_out[...]
    for j in range(2):
        pb[9 + j] = c_in[:, j * D : (j + 1) * D]
    pb[11] = c_q[...]
    pb[12] = c_out[...]
    for j in range(4):
        pb[j] = up[:, j * D : (j + 1) * D]
        pb[4 + j] = down[16 * j : 16 * j + 16, :]
    rows = jnp.concatenate([gain[...], bias[...], jnp.zeros((10, 16), BF)], 0)
    column = lax.broadcasted_iota(jnp.int32, (16, D), 1)
    row = lax.broadcasted_iota(jnp.int32, (16, D), 0)
    pick = (column == at[0] * 16 + row).astype(BF)
    pb[13] = dot(rows, pick).astype(BF)


def join(full, near, far):
    half = near.shape[0]
    full[:half] = near[...]
    full[half:] = far[...]


def self_forward(rows, ids, near, far, wa, wa_far, mask, xf, q, kv, p, rl, at):
    join(xf, near, far)
    q[...] = (dot(xf[:rows], weight(ids, wa, wa_far, 0)).astype(BF).astype(F32) * SCALE).astype(BF)
    kv[:, :D] = dot(xf[...], weight(ids, wa, wa_far, 1)).astype(BF)
    kv[:, D:] = dot(xf[...], weight(ids, wa, wa_far, 2)).astype(BF)
    attend(q, kv, mask, p, rl, at)


def cross_forward(rows, ids, xf, near, far, at1, wb, norms, mask, ef, xh1, rs1, low1, q, kv, p, rl, at):
    join(ef, near, far)
    gb = norm_rows(norms)
    resid = xf[:rows].astype(F32) + dot(at1[...], whole_weight(wb, 0), TN)
    xhat, rstd, n1 = norm_forward(resid, gb[0:1], gb[3:4])
    xh1[...] = xhat
    rs1[...] = rstd
    low1[...] = n1.astype(BF)
    q[...] = (dot(low1[...], whole_weight(wb, 3)).astype(BF).astype(F32) * SCALE).astype(BF)
    kv[:, :D] = dot(ef[...], whole_weight(wb, 1)).astype(BF)
    kv[:, D:] = dot(ef[...], whole_weight(wb, 2)).astype(BF)
    attend(q, kv, mask, p, rl, at)


def ffn_both(ids, xh1, at2, teach, valid, w_up, w_dn, w_co, norms,
             out, small, d_r2, d_mix, keep, send, act, hid, low2, wup):
    gb = norm_rows(norms)
    n1 = xh1[...] * gb[0:1] + gb[3:4]
    wco = whole_weight(w_co, 0)
    for j in range(4):
        wup[j] = whole_weight(w_up, j)
    wdn = w_dn[...].reshape(FF, D)
    xh2, rs2, n2 = norm_forward(n1 + dot(at2[...], wco, TN), gb[1:2], gb[4:5])
    low2[...] = n2.astype(BF)
    for j in range(4):
        h = dot(low2[...], wup[j])
        hid[j] = h
        act[:, j * D : (j + 1) * D] = (h / (1.0 + jnp.exp(-h))).astype(BF)
    r3 = n2 + dot(act[...], wdn)
    xh3, rs3, final = norm_forward(r3, gb[2:3], gb[5:6])
    out[...] = final.astype(BF)
    err = (final - teach[...].astype(F32)) * valid[...]
    small[...] = jnp.zeros_like(small)
    small[6:7] = jnp.sum(err * err, axis=0, keepdims=True)
    d_r3, dg, db = norm_back(err, xh3, rs3, gb[2:3])
    small[2:3] = dg
    small[5:6] = db
    dffn = d_r3.astype(BF)
    for ref, at in sides(ids, keep, send):
        g = dot(cols(act, at, FF // 4), dffn, TN).astype(BF)
        for i in range(16):
            ref[ids[PLACE_1 + i], 4:8] = g[64 * i : 64 * i + 64].reshape(4, 16, D)
    dn2 = d_r3
    for j in range(4):
        da = dot(dffn, wdn[j * D : (j + 1) * D], NT)
        h = hid[j]
        sig = 1.0 / (1.0 + jnp.exp(-h))
        dh = (da * (sig * (1.0 + h * (1.0 - sig)))).astype(BF)
        for ref, at in sides(ids, keep, send):
            put(ids, PLACE_1, ref, j, dot(cols(low2, at, 128), dh, TN))
        dn2 = dn2 + dot(dh, wup[j], NT)
    dr2, dg, db = norm_back(dn2, xh2, rs2, gb[1:2])
    small[1:2] = dg
    small[4:5] = db
    d_r2[...] = dr2
    dcross = dr2.astype(BF)
    for ref, at in sides(ids, keep, send):
        put(ids, PLACE_1, ref, 8, dot(rows_of(at2, at, 128), dcross))
    d_mix[...] = dot(dcross, wco, NT).astype(BF)


def cross_back_a(q, kv, p, rl, d_mix, dkv, dq, dqt):
    attend_back(0, q, kv, p, rl, d_mix, dkv, dqt)
    dq[...] = jnp.transpose(dqt[...]).astype(BF)


def project(near, far, dkv_a, dkv_b, wk, wv):
    out = dot(dkv_a[:, :HALF], wk[:, :HALF], NT) + dot(dkv_b[:, :HALF], wk[:, HALF:], NT)
    out = out + dot(dkv_a[:, HALF:], wv[:, :HALF], NT) + dot(dkv_b[:, HALF:], wv[:, HALF:], NT)
    half = out.shape[0] // 2
    near[...] = out[:half].astype(BF)
    far[...] = out[half:].astype(BF)


def cross_back_b(ids, ef, q, kv, p, rl, d_mix, dkv_a, dq_a, wb, norms, d_r2, low1, xh1,
                 rs1, at1, small_in, near, far, d_mix1, d_r1, small, keep, send, dkv, dqt):
    attend_back(4, q, kv, p, rl, d_mix, dkv, dqt)
    project(near, far, dkv_a, dkv, whole_weight(wb, 1), whole_weight(wb, 2))
    dq = jnp.concatenate([dq_a[...], jnp.transpose(dqt[...]).astype(BF)], 1)
    gb = norm_rows(norms)
    dn1 = d_r2[...] + dot(dq, whole_weight(wb, 3), NT)
    dr1, dg, db = norm_back(dn1, xh1[...], rs1[...], gb[0:1])
    small[...] = small_in[...]
    small[0:1] = dg
    small[3:4] = db
    d_r1[...] = dr1
    dself = dr1.astype(BF)
    for ref, at in sides(ids, keep, send):
        lhs = cols(ef, at, 128)
        for j in range(2):
            span = slice(j * HALF, (j + 1) * HALF)
            g = jnp.concatenate([dot(lhs, dkv_a[:, span], TN), dot(lhs, dkv[:, span], TN)], 1)
            put(ids, PLACE_2, ref, j, g)
        put(ids, PLACE_2, ref, 2, dot(cols(low1, at, 128), dq, TN))
        put(ids, PLACE_2, ref, 3, dot(rows_of(at1, at, 128), dself))
    d_mix1[...] = dot(dself, whole_weight(wb, 0), NT).astype(BF)


def self_back_a(rows, ids, xf, q, kv, p, rl, d_mix, dkv, dq, keep, send, dqt):
    attend_back(0, q, kv, p, rl, d_mix, dkv, dqt)
    dq[...] = jnp.transpose(dqt[...]).astype(BF)
    for ref, at in sides(ids, keep, send):
        lhs = cols(xf, at, 128)
        put_half(ids, ref, lhs, dq[...], dkv[:, :HALF], dkv[:, HALF:], lhs[:rows])


def self_back_b(rows, ids, xf, q, kv, p, rl, d_mix, dkv_a, dq_a, wa, wa_far, d_r1, near, far, d_own, keep, send, dkv, dqt):
    attend_back(4, q, kv, p, rl, d_mix, dkv, dqt)
    project(near, far, dkv_a, dkv, weight(ids, wa, wa_far, 1), weight(ids, wa, wa_far, 2))
    dq = jnp.transpose(dqt[...]).astype(BF)
    d_own[...] = d_r1[...] + dot(jnp.concatenate([dq_a[...], dq], 1), weight(ids, wa, wa_far, 0), NT)
    for ref, at in sides(ids, keep, send):
        lhs = cols(xf, at, 128)
        put_half(ids, ref, lhs, dq, dkv[:, :HALF], dkv[:, HALF:], lhs[:rows])


def tie(*values):
    return lax.optimization_barrier(values)


class Halved:
    def __init__(self, *terms):
        self.terms = list(terms)

    def total(self, terms=None):
        first, *rest = [t.astype(F32) for t in (self.terms if terms is None else terms)]
        return sum(rest, first)

    def give(self):
        half = self.terms[0].shape[0] // 2
        away = [t[half:] for t in self.terms]
        self.terms = [t[:half] for t in self.terms]
        return self.total(away).astype(BF)

    def take(self, got):
        self.terms.append(got)


class Everywhere(Halved):
    def give(self):
        self.terms = [self.total().astype(BF)]
        return self.terms[0]


def make_shards(nd, ns):
    n_dev = nd * ns
    half = ns // 2
    per = G * 16 // n_dev
    fast = nd == 4 and ns == 8

    core, y, x, zl, zh = ("dp", 1), ("dp", 2), ("seq", 1), ("seq", 2), ("seq", 4)

    def shards(inputs, encoder, teacher, dec_seg, enc_seg, dec_valid, self_in, self_out,
               cross_query, cross_in, cross_out, ffn_up, ffn_down, norm_gain, norm_bias):
        tok = inputs.shape[1]
        rows = 2 * tok
        length = dec_seg.shape[1]
        dp_at, seq_at = lax.axis_index("dp"), lax.axis_index("seq")
        dev = dp_at * ns + seq_at
        mine = seq_at // half

        def flip(bit, arrays):
            axis, b = bit
            size = nd if axis == "dp" else ns
            flat = [v.reshape(-1, D) for v in arrays]
            got = lax.ppermute(
                flat[0] if len(flat) == 1 else jnp.concatenate(flat, 0),
                axis, [(i, i ^ b) for i in range(size)],
            )
            out, start = [], 0
            for v, f in zip(arrays, flat):
                out.append(lax.slice_in_dim(got, start, start + f.shape[0]).reshape(v.shape))
                start += f.shape[0]
            return out

        def trade(bit, *groups):
            for g, got in zip(groups, flip(bit, [g.give() for g in groups])):
                g.take(got)

        def of(v, i):
            return lax.dynamic_index_in_dim(v, i, 0, keepdims=False)

        def other(v):
            return of(v, 1 - mine)

        def append(v, got):
            return jnp.concatenate([v, got], 0)

        valid_away = jnp.pad(other(dec_valid).astype(BF)[None], ((0, 15), (0, D - tok)))

        if fast:
            mats = [self_in, self_out, cross_in, cross_query, cross_out, ffn_up, ffn_down, norm_gain, norm_bias]
            wa, pack_b = call(
                pack,
                [(w, None) for w in mats] + [(dev.astype(jnp.int32)[None], SMEM)],
                [((3, 16, D), BF), ((14, 16, D), BF)],
                name="pack",
            )
            wb = lax.all_gather(pack_b, ("dp", "seq"))
            wa = wa[None]
            got_x, got_a = flip(zh, [other(inputs), wa])
            got_x, got_a, away_e = tie(got_x, got_a, other(encoder))
            xf, wa = jnp.stack([of(inputs, mine), got_x])[None], append(wa, got_a)
            got_e, got_t, got_v = flip(zh, [away_e, other(teacher), valid_away])
            got_x, got_a = flip(zl, [xf, wa])
            xf, wa = append(xf, got_x), append(wa, got_a)
            (got_a,) = flip(x, [wa])
            (got_x,) = flip(x, [xf])
            wa = append(wa, got_a)
            wa = append(wa, flip(y, [wa])[0])
            (wa_far,) = flip(core, [wa])
            ef = jnp.stack([of(encoder, mine), got_e])[None]
            got_a, ef = tie(got_a, ef)
            ef = append(ef, flip(zl, [ef])[0])
            got_x, ef = tie(got_x, ef)
            (got_e,) = flip(x, [ef])
            x_bits = e_bits = (2, 1)
        else:
            got_x, got_e, got_t, got_v = flip(
                ("seq", half), [other(inputs), other(encoder), other(teacher), valid_away]
            )
            xf, ef = jnp.stack([of(inputs, mine), got_x])[None], jnp.stack([of(encoder, mine), got_e])[None]
            x_bits = e_bits = tuple(1 << b for b in range(half.bit_length() - 1))
            for bit in x_bits:
                got_x, got_e = flip(("seq", bit), [xf, ef])
                if bit != x_bits[-1]:
                    xf, ef = append(xf, got_x), append(ef, got_e)

            def gathered(w):
                return lax.all_gather(w, ("dp", "seq"), axis=0, tiled=True)

            def grouped(w):
                return w.reshape(G, 16, w.shape[1] // D, D).transpose(0, 2, 1, 3)

            wa = grouped(gathered(self_in))
            norms = lax.dynamic_update_slice(
                jnp.zeros((16, D), BF), jnp.concatenate([norm_gain, norm_bias], 0), (0, dev * per)
            )
            all_norms = lax.psum(norms.astype(F32), ("dp", "seq")).astype(BF)
            all_norms = jnp.pad(all_norms[None], ((0, G - 1), (0, 0), (0, 0)))[:, None]
            rest = [grouped(gathered(w)) for w in (self_out, cross_in, cross_query, cross_out)]
            down = gathered(ffn_down).reshape(G, 4, 16, D)
            wb = jnp.concatenate([grouped(gathered(ffn_up)), down] + rest + [all_norms], 1)
            wa, wa_far = wa[: G // 2], wa[G // 2 :]
        x_near, x_far = xf.reshape(-1, D), got_x.reshape(-1, D)
        teach = jnp.concatenate([of(teacher, mine), got_t], 0)
        valid = jnp.concatenate([of(dec_valid, mine).astype(F32), got_v[0, :tok].astype(F32)])[:, None]

        def spread(v, bits):
            return sum((((v & b) != 0).astype(jnp.int32) << i) for i, b in enumerate(bits))

        if fast:
            i16 = jnp.arange(16, dtype=jnp.int32)
            g32 = jnp.arange(32, dtype=jnp.int32)
            dev16 = (dp_at >> 1) * 8 + seq_at
            ids = jnp.concatenate(
                [
                    (dp_at & 1).astype(jnp.int32)[None],
                    spread(i16 ^ dev16, (4, 2, 1, 8)),
                    spread(i16 ^ dev16, (4, 1, 2, 8)),
                    spread(g32 ^ dev, (4, 2, 1, 16, 8)),
                ]
            )
        else:
            i16, g32 = jnp.arange(16, dtype=jnp.int32), jnp.arange(32, dtype=jnp.int32)
            ids = jnp.concatenate([jnp.zeros((1,), jnp.int32), i16, i16, g32])

        slots = jnp.arange(half, dtype=jnp.int32)

        def pieces(bits):
            masks = sum((((slots >> i) & 1) * b) for i, b in enumerate(bits))[:, None]
            return (seq_at ^ masks ^ jnp.array([[0, half]], jnp.int32)).reshape(-1)

        pos = (pieces(x_bits)[:, None] * tok + jnp.arange(tok, dtype=jnp.int32)[None]).reshape(-1)
        dec_k = of(dec_seg, mine).reshape(ns, tok)[pieces(x_bits)].reshape(-1)
        enc_k = of(enc_seg, mine).reshape(ns, tok)[pieces(e_bits)].reshape(-1)
        dec_q = dec_k[:rows]
        ok_self = (dec_k[:, None] == dec_q[None]) & (pos[:, None] <= pos[None, :rows])
        ok_cross = enc_k[:, None] == dec_q[None]
        mask_self = jnp.where(ok_self, 0.0, NEG).astype(F32)
        mask_cross = jnp.where(ok_cross, 0.0, NEG).astype(F32)

        sm = (ids, SMEM)
        p_shape = (HEADS, length, rows)
        xf, q1, kv1, p1, rl1, at1 = call(
            functools.partial(self_forward, rows),
            [sm, (x_near, None), (x_far, None), (wa, None), (wa_far, None), (mask_self, None)],
            [((length, D), BF), ((rows, D), BF), ((length, 2 * D), BF), (p_shape, BF), ((HEADS, 1, rows), F32), ((D, rows), BF)],
            name="self_forward",
        )
        got_e, at1 = tie(got_e, at1)
        e_near, e_far = ef.reshape(-1, D), got_e.reshape(-1, D)
        ef, xh1, rs1, low1, q2, kv2, p2, rl2, at2 = call(
            functools.partial(cross_forward, rows),
            [sm, (xf, None), (e_near, None), (e_far, None), (at1, None), (wb, chunks(8, 4)), (wb, chunks(13, 1)),
             (mask_cross, None)],
            [((length, D), BF), ((rows, D), F32), ((rows, 1), F32), ((rows, D), BF), ((rows, D), BF), ((length, 2 * D), BF),
             (p_shape, BF), ((HEADS, 1, rows), F32), ((D, rows), BF)],
            name="cross_forward",
        )
        out, small, d_r2, d_mix2, keep1, send1 = call(
            ffn_both,
            [sm, (xh1, None), (at2, None), (teach, None), (valid, None), (wb, chunks(0, 4)), (wb, chunks(4, 4)),
             (wb, chunks(12, 1)), (wb, chunks(13, 1))],
            [((rows, D), BF), ((16, D), F32), ((rows, D), F32), ((rows, D), BF)] + [((16, 9, 16, D), BF)] * 2,
            scratch=[pltpu.VMEM((rows, FF), BF), pltpu.VMEM((4, rows, D), F32), pltpu.VMEM((rows, D), BF),
                     pltpu.VMEM((4, D, D), BF)],
            name="ffn_both",
        )

        kv_half = [((length, D), BF), ((rows, HALF), BF)]
        d_rows = [pltpu.VMEM((HALF, rows), F32)]
        both_scratch = [pltpu.VMEM((length, D), BF)] + d_rows
        packed = [((16, 24, D), BF)] * 2

        if fast:
            (got1,) = flip(core, [send1])
        dkv2, dq2 = call(
            cross_back_a,
            [(q2, None), (kv2, None), (p2, None), (rl2, None), (d_mix2, None)],
            kv_half,
            scratch=d_rows,
            name="cross_back_a",
        )
        if fast:
            got1, d_mix2, dkv2 = tie(got1, d_mix2, dkv2)
            group1 = Halved(keep1, got1)
            trade(y, group1)
        two_halves = [((length // 2, D), BF)] * 2
        enc_near, enc_far, d_mix1, d_r1, small, keep2, send2 = call(
            cross_back_b,
            [sm, (ef, None), (q2, None), (kv2, None), (p2, None), (rl2, None), (d_mix2, None),
             (dkv2, None), (dq2, None), (wb, chunks(8, 4)), (wb, chunks(13, 1)), (d_r2, None), (low1, None), (xh1, None), (rs1, None),
             (at1, None), (small, None)],
            two_halves + [((rows, D), BF), ((rows, D), F32), ((16, D), F32)] + [((16, 4, 16, D), BF)] * 2,
            scratch=both_scratch,
            name="cross_back_b",
        )
        lane = lax.broadcasted_iota(jnp.int32, (16, D), 1)
        row = lax.broadcasted_iota(jnp.int32, (16, D), 0)
        small = jnp.where((row == 7) & (lane == dev), jnp.sum(dec_valid).astype(F32), small)
        small = Everywhere(small)
        if fast:
            (got2,) = flip(core, [send2])
            (got_e,) = flip(x, [enc_far])
        dkv1, dq1, keep3, send3 = call(
            functools.partial(self_back_a, rows),
            [sm, (xf, None), (q1, None), (kv1, None), (p1, None), (rl1, None), (d_mix1, None)],
            kv_half + packed,
            scratch=d_rows,
            name="self_back_a",
        )
        if fast:
            (got3,) = flip(core, [send3])
            got2, got3, d_mix1, got_e, group1.terms[-1] = tie(got2, got3, d_mix1, got_e, group1.terms[-1])
            group2, group3, enc = Halved(keep2, got2), Halved(keep3, got3), Halved(enc_near, got_e)
            trade(y, group2, group3)
            trade(x, group1)
            trade(zl, enc)
        x_near, x_far, d_own, keep4, send4 = call(
            functools.partial(self_back_b, rows),
            [sm, (xf, None), (q1, None), (kv1, None), (p1, None), (rl1, None), (d_mix1, None),
             (dkv1, None), (dq1, None), (wa, None), (wa_far, None), (d_r1, None)],
            two_halves + [((rows, D), F32)] + packed,
            scratch=both_scratch,
            name="self_back_b",
        )

        def back_home(kept, recv):
            return jnp.where(mine == 0, jnp.stack([kept, recv]), jnp.stack([recv, kept]))

        def wide(g):
            return g.transpose(1, 0, 2).reshape(per, -1)

        def unpack(a, b):
            def three(g):
                v = g[..., 16:, :]
                v = jnp.concatenate([v[..., :HALF], v[..., HALF:]], -2)
                return g[..., :16, :HALF], g[..., :16, HALF:], v

            return jnp.concatenate([v for pair in zip(three(a), three(b)) for v in pair], -1)

        if fast:
            x_far, send4, group1.terms[-1] = tie(x_far, send4, group1.terms[-1])
            low_small = small.give()
            (got_x,) = flip(x, [x_far])
            got4, got_small = flip(core, [send4, low_small])
            small.take(got_small)
            group4, dx = Halved(keep4, got4), Halved(x_near, got_x)
            trade(zl, group1, group2, group3)
            trade(y, group4, small)
            dx.terms[-1], group4.terms[-1] = tie(dx.terms[-1], group4.terms[-1])
            trade(zl, dx, group4, small)
            group1.terms[-1], e_own = tie(group1.terms[-1], enc.total())
            away_1 = group1.give()
            got_1, home, home_e = flip(zh, [away_1, out[tok:], e_own[tok:].astype(BF)])
            group1.take(got_1)
            trade(x, group2, group3)
            x_own = dx.total() + d_own
            away_x = x_own[tok:].astype(BF)
            away_2, away_3 = group2.give(), group3.give()
            home_x, got_2, got_3 = flip(zh, [away_x, away_2, away_3])
            group2.take(got_2)
            group3.take(got_3)
            trade(x, group4, small)
            trade(zh, group4, small)
            s1, s2, small = group1.total()[0], group2.total()[0], small.total()
            g_up, g_down, g_co = wide(s1[:4]), s1[4:8].reshape(4 * per, D), s1[8]
            g_cin, g_cq, g_so = wide(s2[:2]), s2[2], s2[3]
            g_in = unpack(group3.total()[0], group4.total()[0])
        else:
            enc = Halved(jnp.concatenate([enc_near, enc_far], 0))
            dx = Halved(jnp.concatenate([x_near, x_far], 0))
            for bit in reversed(x_bits):
                trade(("seq", bit), enc, dx)
            e_own = enc.total()
            x_own = dx.total() + d_own
            home, home_e, home_x = flip(
                ("seq", half), [out[tok:], e_own[tok:].astype(BF), x_own[tok:].astype(BF)]
            )
            small = lax.psum(small.terms[0], ("dp", "seq"))

            def summed(g):
                return lax.psum_scatter(g, ("dp", "seq"), scatter_dimension=0, tiled=True).astype(F32)

            def rejoin(keep, send):
                g = jnp.stack([keep.reshape((2, 8) + keep.shape[1:]), send.reshape((2, 8) + keep.shape[1:])], 1)
                return g.reshape((G,) + keep.shape[1:])

            def full(g):
                return g.transpose(0, 2, 1, 3).reshape(G * 16, -1)

            all1, all2 = rejoin(keep1, send1), rejoin(keep2, send2)
            g_up = summed(full(all1[:, :4]))
            g_down = summed(all1[:, 4:8].reshape(FF, D))
            g_co = summed(full(all1[:, 8:]))
            g_cin, g_cq, g_so = summed(full(all2[:, :2])), summed(full(all2[:, 2:3])), summed(full(all2[:, 3:]))
            g_in = summed(unpack(rejoin(keep3, send3), rejoin(keep4, send4)).reshape(G * 16, -1))

        loss = jnp.sum(small[6]) / (jnp.sum(small[7]) * D)
        g_norm = lax.dynamic_slice(small, (0, dev * per), (6, per))
        outputs = back_home(out[:tok], home)
        grad_encoder = back_home(e_own[:tok], home_e.astype(F32))
        grad_inputs = back_home(x_own[:tok], home_x.astype(F32))
        return (outputs, loss, grad_inputs, grad_encoder, g_in, g_so, g_cq, g_cin, g_co, g_up, g_down,
                g_norm[:3], g_norm[3:])

    return shards


def solution(mesh):
    rows, both = P("dp", "seq", None), P(("dp", "seq"), None)
    norm = P(None, ("dp", "seq"))
    return jax.shard_map(
        make_shards(mesh.shape["dp"], mesh.shape["seq"]),
        mesh=mesh,
        in_specs=(rows, rows, rows, P("dp", None), P("dp", None), P("dp", "seq")) + (both,) * 7 + (norm, norm),
        out_specs=(rows, P(), rows, rows) + (both,) * 7 + (norm, norm),
        check_vma=False,
    )
```

```python
import functools

import jax
import jax.numpy as jnp
from jax import lax
from jax.experimental import pallas as pl
from jax.experimental.pallas import tpu as pltpu
from jax.sharding import PartitionSpec as P

HEADS = 8
HEAD_DIM = 64
EPS = 1e-5
NEG = -1e30
SCALE = 0.125
D = 512
FF = 2048
HALF = 256
G = 32
BF = jnp.bfloat16
F32 = jnp.float32
MIB = 1 << 20

DEVICE, PLACE_1, PLACE_2, SLOT = 1, 2, 18, 34

NN = (((1,), (0,)), ((), ()))
NT = (((1,), (1,)), ((), ()))
TN = (((0,), (0,)), ((), ()))


def dot(a, b, dims=NN):
    return lax.dot_general(a, b, dims, preferred_element_type=F32)


def whole(shape):
    return pl.BlockSpec(shape, lambda i: (0,) * len(shape))


SMEM = pl.BlockSpec(memory_space=pltpu.SMEM)


def chunks(first, count):
    return pl.BlockSpec((G, count, 16, D), lambda i: (0, first // count, 0, 0))


def whole_weight(ref, j):
    return ref[:, j].reshape(D, D)


def call(body, ins, outs, scratch=(), name=None, vmem=16):
    return pl.pallas_call(
        body,
        grid=(1,),
        in_specs=[whole(a.shape) if s is None else s for a, s in ins],
        out_specs=[whole(s) for s, _ in outs],
        out_shape=[jax.ShapeDtypeStruct(s, t) for s, t in outs],
        scratch_shapes=list(scratch),
        compiler_params=pltpu.CompilerParams(vmem_limit_bytes=vmem * MIB),
        name=name,
        cost_estimate=pl.CostEstimate(flops=1000, bytes_accessed=1000, transcendentals=0),
    )(*[a for a, _ in ins])


def weight(ids, near, far, j):
    picks = []
    for g in range(G):
        at = ids[SLOT + g]
        low = at & (G // 2 - 1)
        picks.append(jnp.where(at < G // 2, near[low, j], far[low, j]))
    return jnp.concatenate(picks, 0)


def norm_rows(ref):
    return jnp.sum(ref[:, 0].astype(F32), axis=0)


def put(ids, first, ref, chunks_each, j, value):
    value = value.astype(BF)
    each = value.shape[0] // 16
    for i in range(16):
        at = ids[first + i] * (16 * chunks_each) + 16 * j
        ref[pl.ds(pl.multiple_of(at, 16), each), :] = value[each * i : each * i + each]


def norm_forward(resid, gain, bias):
    centre = resid - jnp.mean(resid, axis=-1, keepdims=True)
    rstd = lax.rsqrt(jnp.mean(centre * centre, axis=-1, keepdims=True) + EPS)
    xhat = centre * rstd
    return xhat, rstd, xhat * gain + bias


def norm_back(g, xhat, rstd, gain):
    e = g * gain
    m1 = jnp.mean(e, axis=-1, keepdims=True)
    m2 = jnp.mean(e * xhat, axis=-1, keepdims=True)
    dr = (e - m1 - xhat * m2) * rstd
    return dr, jnp.sum(g * xhat, axis=0, keepdims=True), jnp.sum(g, axis=0, keepdims=True)


def head_half(x, e):
    lane = lax.broadcasted_iota(jnp.int32, x.shape, 1)
    return jnp.where((lane < HEAD_DIM) == (e == 0), x, jnp.zeros_like(x))


def attend(q_ref, kv_ref, mask_ref, p_ref, rl_ref, at_ref):
    def pair(hp, carry):
        c0 = pl.multiple_of(hp * 128, 128)
        k2 = kv_ref[:, pl.ds(c0, 128)]
        v2 = kv_ref[:, pl.ds(pl.multiple_of(D + c0, 128), 128)]
        q2 = q_ref[:, pl.ds(c0, 128)]
        for e in range(2):
            s = dot(k2, head_half(q2, e), NT) + mask_ref[...]
            p = jnp.exp(s - jnp.max(s, axis=0, keepdims=True))
            rl = 1.0 / jnp.sum(p, axis=0, keepdims=True)
            pb = p.astype(BF)
            p_ref[2 * hp + e] = pb
            rl_ref[2 * hp + e] = rl
            o = dot(v2, pb, TN) * rl
            at_ref[pl.ds(pl.multiple_of((2 * hp + e) * HEAD_DIM, HEAD_DIM), HEAD_DIM), :] = o[
                e * HEAD_DIM : (e + 1) * HEAD_DIM
            ].astype(BF)
        return carry

    lax.fori_loop(0, HEADS // 2, pair, 0)


def attend_back(first, q_ref, kv_ref, p_ref, rl_ref, do_ref, dkv_ref, dqt_ref):
    def pair(i, carry):
        hp = first // 2 + i
        c0 = pl.multiple_of(hp * 128, 128)
        o0 = pl.multiple_of(i * 128, 128)
        k2 = kv_ref[:, pl.ds(c0, 128)]
        v2 = kv_ref[:, pl.ds(pl.multiple_of(D + c0, 128), 128)]
        q2 = q_ref[:, pl.ds(c0, 128)]
        do2 = do_ref[:, pl.ds(c0, 128)]
        dk = dv = None
        for e in range(2):
            dom = head_half(do2, e)
            dp = dot(v2, dom, NT)
            p = p_ref[2 * hp + e].astype(F32) * rl_ref[2 * hp + e]
            t = p * dp
            ds = (t - p * jnp.sum(t, axis=0, keepdims=True)).astype(BF)
            dk_e = dot(ds, head_half(q2, e))
            dv_e = dot(p.astype(BF), dom)
            dk = dk_e if dk is None else dk + dk_e
            dv = dv_e if dv is None else dv + dv_e
            dqt = dot(k2, ds, TN) * SCALE
            dqt_ref[pl.ds(pl.multiple_of((2 * i + e) * HEAD_DIM, HEAD_DIM), HEAD_DIM), :] = dqt[
                e * HEAD_DIM : (e + 1) * HEAD_DIM
            ]
        dkv_ref[:, pl.ds(o0, 128)] = dk.astype(BF)
        dkv_ref[:, pl.ds(pl.multiple_of(HALF + o0, 128), 128)] = dv.astype(BF)
        return carry

    lax.fori_loop(0, HEADS // 4, pair, 0)


def cols(ref, c, width):
    picks = [ref[:, pl.ds(pl.multiple_of((2 * y + c) * width, width), width)] for y in range(2)]
    return jnp.concatenate(picks, 1)


def rows_of(ref, c, width):
    picks = [ref[pl.ds(pl.multiple_of((2 * y + c) * width, width), width), :] for y in range(2)]
    return jnp.concatenate(picks, 0)


def sides(ids, keep, send):
    return ((send, 1 - ids[0]), (keep, ids[0]))


def pack(s_in, s_out, c_in, c_q, c_out, up, down, gain, bias, at, pa, pb):
    for j in range(3):
        pa[j] = s_in[:, j * D : (j + 1) * D]
    pb[8] = s_out[...]
    for j in range(2):
        pb[9 + j] = c_in[:, j * D : (j + 1) * D]
    pb[11] = c_q[...]
    pb[12] = c_out[...]
    for j in range(4):
        pb[j] = up[:, j * D : (j + 1) * D]
        pb[4 + j] = down[16 * j : 16 * j + 16, :]
    rows = jnp.concatenate([gain[...], bias[...], jnp.zeros((10, 16), BF)], 0)
    column = lax.broadcasted_iota(jnp.int32, (16, D), 1)
    row = lax.broadcasted_iota(jnp.int32, (16, D), 0)
    pick = (column == at[0] * 16 + row).astype(BF)
    pb[13] = dot(rows, pick).astype(BF)


def join(full, near, far):
    half = near.shape[0]
    full[:half] = near[...]
    full[half:] = far[...]


def self_forward(rows, ids, near, far, wa, wa_far, mask, xf, q, kv, p, rl, at):
    join(xf, near, far)
    q[...] = (dot(xf[:rows], weight(ids, wa, wa_far, 0)).astype(BF).astype(F32) * SCALE).astype(BF)
    kv[:, :D] = dot(xf[...], weight(ids, wa, wa_far, 1)).astype(BF)
    kv[:, D:] = dot(xf[...], weight(ids, wa, wa_far, 2)).astype(BF)
    attend(q, kv, mask, p, rl, at)


def cross_forward(rows, ids, xf, near, far, at1, wb, norms, mask, ef, xh1, rs1, low1, q, kv, p, rl, at):
    join(ef, near, far)
    gb = norm_rows(norms)
    resid = xf[:rows].astype(F32) + dot(at1[...], whole_weight(wb, 0), TN)
    xhat, rstd, n1 = norm_forward(resid, gb[0:1], gb[3:4])
    xh1[...] = xhat
    rs1[...] = rstd
    low1[...] = n1.astype(BF)
    q[...] = (dot(low1[...], whole_weight(wb, 3)).astype(BF).astype(F32) * SCALE).astype(BF)
    kv[:, :D] = dot(ef[...], whole_weight(wb, 1)).astype(BF)
    kv[:, D:] = dot(ef[...], whole_weight(wb, 2)).astype(BF)
    attend(q, kv, mask, p, rl, at)


def ffn_both(ids, xh1, at2, teach, valid, w_up, w_dn, w_co, norms,
             out, small, d_r2, d_mix, keep, send, act, hid, low2, wup):
    gb = norm_rows(norms)
    n1 = xh1[...] * gb[0:1] + gb[3:4]
    wco = whole_weight(w_co, 0)
    for j in range(4):
        wup[j] = whole_weight(w_up, j)
    wdn = w_dn[...].reshape(FF, D)
    xh2, rs2, n2 = norm_forward(n1 + dot(at2[...], wco, TN), gb[1:2], gb[4:5])
    low2[...] = n2.astype(BF)
    for j in range(4):
        h = dot(low2[...], wup[j])
        hid[j] = h
        act[:, j * D : (j + 1) * D] = (h / (1.0 + jnp.exp(-h))).astype(BF)
    r3 = n2 + dot(act[...], wdn)
    xh3, rs3, final = norm_forward(r3, gb[2:3], gb[5:6])
    out[...] = final.astype(BF)
    err = (final - teach[...].astype(F32)) * valid[...]
    small[...] = jnp.zeros_like(small)
    small[6:7] = jnp.sum(err * err, axis=0, keepdims=True)
    lane = lax.broadcasted_iota(jnp.int32, (1, D), 1)
    small[7:8] = jnp.where(lane == ids[DEVICE], jnp.sum(valid[...]), 0.0)
    d_r3, dg, db = norm_back(err, xh3, rs3, gb[2:3])
    small[2:3] = dg
    small[5:6] = db
    dffn = d_r3.astype(BF)
    for ref, at in sides(ids, keep, send):
        put(ids, PLACE_1, ref, 9, 4, dot(cols(act, at, FF // 4), dffn, TN))
    dn2 = d_r3
    for j in range(4):
        da = dot(dffn, wdn[j * D : (j + 1) * D], NT)
        h = hid[j]
        sig = 1.0 / (1.0 + jnp.exp(-h))
        dh = (da * (sig * (1.0 + h * (1.0 - sig)))).astype(BF)
        for ref, at in sides(ids, keep, send):
            put(ids, PLACE_1, ref, 9, j, dot(cols(low2, at, 128), dh, TN))
        dn2 = dn2 + dot(dh, wup[j], NT)
    dr2, dg, db = norm_back(dn2, xh2, rs2, gb[1:2])
    small[1:2] = dg
    small[4:5] = db
    d_r2[...] = dr2
    dcross = dr2.astype(BF)
    for ref, at in sides(ids, keep, send):
        put(ids, PLACE_1, ref, 9, 8, dot(rows_of(at2, at, 128), dcross))
    d_mix[...] = dot(dcross, wco, NT).astype(BF)


def cross_back_a(q, kv, p, rl, d_mix, dkv, dq, dqt):
    attend_back(0, q, kv, p, rl, d_mix, dkv, dqt)
    dq[...] = jnp.transpose(dqt[...]).astype(BF)


def project(own, parts, dkv_a, dkv_b, wk, wv, extra=0.0):
    out = dot(dkv_a[:, :HALF], wk[:, :HALF], NT) + dot(dkv_b[:, :HALF], wk[:, HALF:], NT)
    out = out + dot(dkv_a[:, HALF:], wv[:, :HALF], NT) + dot(dkv_b[:, HALF:], wv[:, HALF:], NT)
    each = own.shape[0]
    own[...] = out[:each] + extra
    for i, part in enumerate(parts):
        part[...] = out[each * (i + 1) : each * (i + 2)].astype(BF)


def cross_back_b(n_parts, ids, ef, q, kv, p, rl, d_mix, dkv_a, dq_a, wb, norms, d_r2, low1, xh1,
                 rs1, at1, small, own, *rest):
    parts, (d_mix1, d_r1, keep, send, dkv, dqt) = rest[:n_parts], rest[n_parts:]
    attend_back(4, q, kv, p, rl, d_mix, dkv, dqt)
    project(own, parts, dkv_a, dkv, whole_weight(wb, 1), whole_weight(wb, 2))
    dq = jnp.concatenate([dq_a[...], jnp.transpose(dqt[...]).astype(BF)], 1)
    gb = norm_rows(norms)
    dn1 = d_r2[...] + dot(dq, whole_weight(wb, 3), NT)
    dr1, dg, db = norm_back(dn1, xh1[...], rs1[...], gb[0:1])
    row = lax.broadcasted_iota(jnp.int32, (16, D), 0)
    sums = jnp.where(row == 0, dg, jnp.where(row == 3, db, small[...]))
    send[1024:1040] = sums.astype(BF)
    d_r1[...] = dr1
    dself = dr1.astype(BF)
    for ref, at in sides(ids, keep, send):
        lhs = cols(ef, at, 128)
        for j in range(2):
            span = slice(j * HALF, (j + 1) * HALF)
            g = jnp.concatenate([dot(lhs, dkv_a[:, span], TN), dot(lhs, dkv[:, span], TN)], 1)
            put(ids, PLACE_2, ref, 4, j, g)
        put(ids, PLACE_2, ref, 4, 2, dot(cols(low1, at, 128), dq, TN))
        put(ids, PLACE_2, ref, 4, 3, dot(rows_of(at1, at, 128), dself))
    d_mix1[...] = dot(dself, whole_weight(wb, 0), NT).astype(BF)


def self_back_b(n_parts, rows, ids, xf, q, kv, p, rl, d_mix, dkv_a, dq_a, wa, wa_far, d_r1, own, *rest):
    parts, (keep, send, dkv, dqt) = rest[:n_parts], rest[n_parts:]
    attend_back(4, q, kv, p, rl, d_mix, dkv, dqt)
    dq = jnp.concatenate([dq_a[...], jnp.transpose(dqt[...]).astype(BF)], 1)
    through_q = d_r1[...] + dot(dq, weight(ids, wa, wa_far, 0), NT)
    project(own, parts, dkv_a, dkv, weight(ids, wa, wa_far, 1), weight(ids, wa, wa_far, 2), through_q)
    for ref, at in sides(ids, keep, send):
        lhs = cols(xf, at, 128)
        put(ids, PLACE_2, ref, 3, 0, dot(lhs[:rows], dq, TN))
        for j in range(2):
            span = slice(j * HALF, (j + 1) * HALF)
            g = jnp.concatenate([dot(lhs, dkv_a[:, span], TN), dot(lhs, dkv[:, span], TN)], 1)
            put(ids, PLACE_2, ref, 3, 1 + j, g)


def tree_sum(terms):
    while len(terms) > 1:
        terms = [a + b for a, b in zip(terms[::2], terms[1::2])] + terms[len(terms) & ~1 :]
    return terms[0]


ANY = pl.BlockSpec(memory_space=pl.ANY)


def fetch(ref, start, count, to, sem):
    copy = pltpu.make_async_copy(ref.at[pl.ds(start, count)], to, sem)
    copy.start()
    return copy


def mix(name, *outs):
    arrays, terms, plan = [], [], []
    for dtype, segments in outs:
        plan.append([])
        for segment in segments:
            used = []
            for array, start, count in segment:
                at = [i for i, v in enumerate(arrays) if v is array]
                if not at:
                    arrays.append(array)
                used.append(len(terms))
                terms.append((at[0] if at else len(arrays) - 1, start, count, array.dtype))
            plan[-1].append(used)

    def body(*refs):
        for out, segments in zip(refs[len(arrays) :], plan):
            first = 0
            for used in segments:
                count = terms[used[0]][2]
                parts = [refs[k][start : start + count].astype(F32) for k, start, _, _ in (terms[i] for i in used)]
                out[first : first + count] = tree_sum(parts).astype(out.dtype)
                first += count

    shapes = [((sum(t[0][2] for t in segments), D), dtype) for dtype, segments in outs]
    return call(body, [(v, None) for v in arrays], shapes, name=name)


def finish(counts, *refs):
    where, refs = refs[0], refs[1:]
    sources, results = refs[: len(counts)], refs[len(counts) :]
    refs = [ref.at[:count] for ref, count in zip(sources, counts)]
    one, (out, home, e_keep, x_keep, home_x, z_own, z_got, *refs) = refs[:6], refs[6:]
    two, three = refs[:6], refs[6:]
    outputs, loss, g_x, g_e, g_in, g_so, g_cq, g_cin, g_co, g_up, g_down, g_gain, g_bias = results
    mine = where[0]
    tok = e_keep.shape[0]
    outputs[mine] = out[...]
    outputs[1 - mine] = home[:tok]
    g_e[mine] = e_keep[...]
    g_e[1 - mine] = home[tok : 2 * tok].astype(F32)
    g_x[mine] = x_keep[...]
    g_x[1 - mine] = home_x[...].astype(F32)
    t1 = tree_sum([r[...].astype(F32) for r in one] + [home[2 * tok :].astype(F32)])
    for j in range(4):
        g_up[:, j * D : (j + 1) * D] = t1[16 * j : 16 * j + 16]
    g_down[...] = t1[64:128]
    g_co[...] = t1[128:144]
    t2 = tree_sum([r[...].astype(F32) for r in two[:3]] + [r[:64].astype(F32) for r in two[3:]] + [z_got[:64].astype(F32)])
    for j in range(2):
        g_cin[:, j * D : (j + 1) * D] = t2[16 * j : 16 * j + 16]
    g_cq[...] = t2[32:48]
    g_so[...] = t2[48:64]
    t3 = tree_sum([r[...].astype(F32) for r in three] + [r[128:176].astype(F32) for r in two[3:]] + [z_got[64:112].astype(F32)])
    for j in range(3):
        g_in[:, j * D : (j + 1) * D] = t3[16 * j : 16 * j + 16]
    small = z_own[112:128].astype(F32) + z_got[112:128].astype(F32)
    total = jnp.sum(small[6:7], axis=1, keepdims=True)
    loss[...] = total / (jnp.sum(small[7:8], axis=1, keepdims=True) * D)
    column = lax.broadcasted_iota(jnp.int32, (16, D), 1)
    row = lax.broadcasted_iota(jnp.int32, (16, D), 0)
    pick = (column == where[1] * 16 + row).astype(F32)
    own = lax.dot_general(small[:8], pick, NT, precision=lax.Precision.HIGHEST, preferred_element_type=F32)
    g_gain[...] = own[0:3]
    g_bias[...] = own[3:6]


def tie(*values):
    return lax.optimization_barrier(values)


def make_shards(nd, ns):
    n_dev = nd * ns
    half = ns // 2
    per = G * 16 // n_dev
    fast = nd == 4 and ns == 8
    run = functools.partial(call, vmem=16 if fast else 44)

    core, y, x, zl, zh = ("dp", 1), ("dp", 2), ("seq", 1), ("seq", 2), ("seq", 4)

    def shards(inputs, encoder, teacher, dec_seg, enc_seg, dec_valid, self_in, self_out,
               cross_query, cross_in, cross_out, ffn_up, ffn_down, norm_gain, norm_bias):
        tok = inputs.shape[1]
        rows = 2 * tok
        length = dec_seg.shape[1]
        dp_at, seq_at = lax.axis_index("dp"), lax.axis_index("seq")
        dev = dp_at * ns + seq_at
        mine = seq_at // half

        def flip(bit, arrays):
            axis, b = bit
            size = nd if axis == "dp" else ns
            flat = [v.reshape(-1, D) for v in arrays]
            got = lax.ppermute(
                flat[0] if len(flat) == 1 else jnp.concatenate(flat, 0),
                axis, [(i, i ^ b) for i in range(size)],
            )
            out, start = [], 0
            for v, f in zip(arrays, flat):
                out.append(lax.slice_in_dim(got, start, start + f.shape[0]).reshape(v.shape))
                start += f.shape[0]
            return out

        def swap(bit, array):
            return flip(bit, [array])[0]

        def of(v, i):
            return lax.dynamic_index_in_dim(v, i, 0, keepdims=False)

        def other(v):
            return of(v, 1 - mine)

        def append(v, got):
            return jnp.concatenate([v, got], 0)

        valid_away = jnp.pad(other(dec_valid).astype(BF)[None], ((0, 15), (0, D - tok)))

        if fast:
            mats = [self_in, self_out, cross_in, cross_query, cross_out, ffn_up, ffn_down, norm_gain, norm_bias]
            wa, pack_b = run(
                pack,
                [(w, None) for w in mats] + [(dev.astype(jnp.int32)[None], SMEM)],
                [((3, 16, D), BF), ((14, 16, D), BF)],
                name="pack",
                vmem=56,
            )
            wb = lax.all_gather(pack_b, ("dp", "seq"))
            wa = wa[None]
            got_x, got_a = flip(zh, [other(inputs), wa])
            got_x, got_a, away_e = tie(got_x, got_a, other(encoder))
            xf, wa = jnp.stack([of(inputs, mine), got_x])[None], append(wa, got_a)
            got_e, got_t, got_v = flip(zh, [away_e, other(teacher), valid_away])
            got_x, got_a = flip(zl, [xf, wa])
            xf, wa = append(xf, got_x), append(wa, got_a)
            (got_a,) = flip(x, [wa])
            (got_x,) = flip(x, [xf])
            wa = append(wa, got_a)
            wa = append(wa, flip(y, [wa])[0])
            (wa_far,) = flip(core, [wa])
            ef = jnp.stack([of(encoder, mine), got_e])[None]
            got_a, ef = tie(got_a, ef)
            ef = append(ef, flip(zl, [ef])[0])
            got_x, ef = tie(got_x, ef)
            (got_e,) = flip(x, [ef])
            x_bits = e_bits = (2, 1)
        else:
            got_x, got_e, got_t, got_v = flip(
                ("seq", half), [other(inputs), other(encoder), other(teacher), valid_away]
            )
            xf, ef = jnp.stack([of(inputs, mine), got_x])[None], jnp.stack([of(encoder, mine), got_e])[None]
            x_bits = e_bits = tuple(1 << b for b in range(half.bit_length() - 1))
            for bit in x_bits:
                got_x, got_e = flip(("seq", bit), [xf, ef])
                if bit != x_bits[-1]:
                    xf, ef = append(xf, got_x), append(ef, got_e)

            def gathered(w):
                return lax.all_gather(w, ("dp", "seq"), axis=0, tiled=True)

            def grouped(w):
                return w.reshape(G, 16, w.shape[1] // D, D).transpose(0, 2, 1, 3)

            wa = grouped(gathered(self_in))
            norms = lax.dynamic_update_slice(
                jnp.zeros((16, D), BF), jnp.concatenate([norm_gain, norm_bias], 0), (0, dev * per)
            )
            all_norms = lax.psum(norms.astype(F32), ("dp", "seq")).astype(BF)
            all_norms = jnp.pad(all_norms[None], ((0, G - 1), (0, 0), (0, 0)))[:, None]
            rest = [grouped(gathered(w)) for w in (self_out, cross_in, cross_query, cross_out)]
            down = gathered(ffn_down).reshape(G, 4, 16, D)
            wb = jnp.concatenate([grouped(gathered(ffn_up)), down] + rest + [all_norms], 1)
            wa, wa_far = wa[: G // 2], wa[G // 2 :]
        x_near, x_far = xf.reshape(-1, D), got_x.reshape(-1, D)
        teach = jnp.concatenate([of(teacher, mine), got_t], 0)
        valid = jnp.concatenate([of(dec_valid, mine).astype(F32), got_v[0, :tok].astype(F32)])[:, None]

        def spread(v, bits):
            return sum((((v & b) != 0).astype(jnp.int32) << i) for i, b in enumerate(bits))

        if fast:
            i16 = jnp.arange(16, dtype=jnp.int32)
            g32 = jnp.arange(32, dtype=jnp.int32)
            dev16 = (dp_at >> 1) * 8 + seq_at
            ids = jnp.concatenate(
                [
                    jnp.stack([dp_at & 1, dev]).astype(jnp.int32),
                    spread(i16 ^ dev16, (4, 2, 1, 8)),
                    spread(i16 ^ dev16, (4, 2, 1, 8)),
                    spread(g32 ^ dev, (4, 2, 1, 16, 8)),
                ]
            )
        else:
            i16, g32 = jnp.arange(16, dtype=jnp.int32), jnp.arange(32, dtype=jnp.int32)
            ids = jnp.concatenate([jnp.stack([0 * dev, dev]).astype(jnp.int32), i16, i16, g32])

        slots = jnp.arange(half, dtype=jnp.int32)

        def pieces(bits):
            masks = sum((((slots >> i) & 1) * b) for i, b in enumerate(bits))[:, None]
            return (seq_at ^ masks ^ jnp.array([[0, half]], jnp.int32)).reshape(-1)

        pos = (pieces(x_bits)[:, None] * tok + jnp.arange(tok, dtype=jnp.int32)[None]).reshape(-1)
        dec_k = of(dec_seg, mine).reshape(ns, tok)[pieces(x_bits)].reshape(-1)
        enc_k = of(enc_seg, mine).reshape(ns, tok)[pieces(e_bits)].reshape(-1)
        dec_q = dec_k[:rows]
        ok_self = (dec_k[:, None] == dec_q[None]) & (pos[:, None] <= pos[None, :rows])
        ok_cross = enc_k[:, None] == dec_q[None]
        mask_self = jnp.where(ok_self, 0.0, NEG).astype(F32)
        mask_cross = jnp.where(ok_cross, 0.0, NEG).astype(F32)

        sm = (ids, SMEM)
        p_shape = (HEADS, length, rows)
        xf, q1, kv1, p1, rl1, at1 = run(
            functools.partial(self_forward, rows),
            [sm, (x_near, None), (x_far, None), (wa, None), (wa_far, None), (mask_self, None)],
            [((length, D), BF), ((rows, D), BF), ((length, 2 * D), BF), (p_shape, BF), ((HEADS, 1, rows), F32), ((D, rows), BF)],
            name="self_forward",
        )
        got_e, at1 = tie(got_e, at1)
        e_near, e_far = ef.reshape(-1, D), got_e.reshape(-1, D)
        ef, xh1, rs1, low1, q2, kv2, p2, rl2, at2 = run(
            functools.partial(cross_forward, rows),
            [sm, (xf, None), (e_near, None), (e_far, None), (at1, None), (wb, chunks(8, 4)), (wb, chunks(13, 1)),
             (mask_cross, None)],
            [((length, D), BF), ((rows, D), F32), ((rows, 1), F32), ((rows, D), BF), ((rows, D), BF), ((length, 2 * D), BF),
             (p_shape, BF), ((HEADS, 1, rows), F32), ((D, rows), BF)],
            name="cross_forward",
        )
        out, small, d_r2, d_mix2, keep1, send1 = run(
            ffn_both,
            [sm, (xh1, None), (at2, None), (teach, None), (valid, None), (wb, chunks(0, 4)), (wb, chunks(4, 4)),
             (wb, chunks(12, 1)), (wb, chunks(13, 1))],
            [((rows, D), BF), ((16, D), F32), ((rows, D), F32), ((rows, D), BF)] + [((2304, D), BF)] * 2,
            scratch=[pltpu.VMEM((rows, FF), BF), pltpu.VMEM((4, rows, D), F32), pltpu.VMEM((rows, D), BF),
                     pltpu.VMEM((4, D, D), BF)],
            name="ffn_both",
        )

        kv_half = [((length, D), BF), ((rows, HALF), BF)]
        d_rows = [pltpu.VMEM((HALF, rows), F32)]
        both_scratch = [pltpu.VMEM((length, D), BF)] + d_rows
        row_parts = [((rows, D), F32)] + [((rows, D), BF)] * (half - 1)
        partners = [sum(((i >> k) & 1) * b for k, b in enumerate(x_bits)) for i in range(1, half)]

        if fast:
            got1 = swap(core, send1)
        dkv2, dq2 = run(
            cross_back_a,
            [(q2, None), (kv2, None), (p2, None), (rl2, None), (d_mix2, None)],
            kv_half,
            scratch=d_rows,
            name="cross_back_a",
        )
        if fast:
            got1, d_mix2, dkv2 = tie(got1, d_mix2, dkv2)
            got_y1 = swap(y, (keep1[1152:].astype(F32) + got1[1152:].astype(F32)).astype(BF))
        e_own, *rest = run(
            functools.partial(cross_back_b, half - 1),
            [sm, (ef, None), (q2, None), (kv2, None), (p2, None), (rl2, None), (d_mix2, None),
             (dkv2, None), (dq2, None), (wb, chunks(8, 4)), (wb, chunks(13, 1)), (d_r2, None), (low1, None),
             (xh1, None), (rs1, None), (at1, None), (small, None)],
            row_parts + [((rows, D), BF), ((rows, D), F32), ((1024, D), BF), ((1040, D), BF)],
            scratch=both_scratch,
            name="cross_back_b",
        )
        e_parts, (d_mix1, d_r1, keep2, send2) = rest[: half - 1], rest[half - 1 :]
        if fast:
            got2 = swap(core, send2)
        e_got = [swap(("seq", m), part) for m, part in zip(partners, e_parts)]
        dkv1, dq1 = run(
            cross_back_a,
            [(q1, None), (kv1, None), (p1, None), (rl1, None), (d_mix1, None)],
            kv_half,
            scratch=d_rows,
            name="self_back_a",
        )
        if fast:
            got2, got_y1, d_mix1, dkv1, *e_got = tie(got2, got_y1, d_mix1, dkv1, *e_got)
            one = lambda start, count: [(v, start, count) for v in (keep1, got1, got_y1)]
            away, *quads1 = mix(
                "sum_y2",
                (BF, [[(keep2, 512, 512), (got2, 512, 512)], [(send2, 1024, 16), (got2, 1024, 16)]]),
                *[(BF, [one(288 * i, 288)]) for i in (1, 2, 3)],
            )
            got_y2 = swap(y, away)
            small_y2 = (away, 512, 16)
            q1_got = [swap(("seq", m), part) for m, part in zip(partners, quads1)]
        x_own, *rest = run(
            functools.partial(self_back_b, half - 1, rows),
            [sm, (xf, None), (q1, None), (kv1, None), (p1, None), (rl1, None), (d_mix1, None),
             (dkv1, None), (dq1, None), (wa, None), (wa_far, None), (d_r1, None)],
            row_parts + [((768, D), BF)] * 2,
            scratch=both_scratch,
            name="self_back_b",
        )
        x_parts, (keep3, send3) = rest[: half - 1], rest[half - 1 :]

        def summed_rows(name, own, got, *more):
            terms = [own] + got
            return mix(name, (F32, [[(t, 0, tok) for t in terms]]),
                       (BF, [*more[:1], [(t, tok, tok) for t in terms], *more[1:]]))

        if fast:
            q1_got[0], q1_got[1], q1_got[2], got_y2, send3, *x_parts = tie(*q1_got, got_y2, send3, *x_parts)
        x_got = [swap(("seq", m), part) for m, part in zip(partners, x_parts)]
        if fast:
            got3 = swap(core, send3)
        more = [one(144, 144) + [(v, 144, 144) for v in q1_got]] if fast else []
        e_keep, away = summed_rows("sum_e", e_own, e_got, [(out, tok, tok)], *more)
        home = swap(("seq", half), away)
        if fast:
            (away,) = mix("sum_y3", (BF, [[(keep3, 384, 384), (got3, 384, 384)]]))
            got_y3 = swap(y, away)
        x_keep, away = summed_rows("sum_x", x_own, x_got)
        home_x = swap(("seq", half), away)

        if fast:
            def two(start, count):
                return [(v, start, count) for v in (keep2, got2, got_y2)]

            def three(start, count):
                return [(v, start, count) for v in (keep3, got3, got_y3)]

            quads = mix(
                "sum_quads",
                *[(BF, [two(128 * i, 128), three(96 * i, 96), [small_y2, (got_y2, 512, 16)]]) for i in (1, 2, 3)],
            )
            q_got = [swap(("seq", m), part) for m, part in zip(partners, quads)]
            (away,) = mix(
                "sum_zh",
                (BF, [two(64, 64) + [(v, 64, 64) for v in q_got], three(48, 48) + [(v, 176, 48) for v in q_got],
                      [(quads[0], 224, 16)] + [(v, 224, 16) for v in q_got]]),
            )
            got_z = swap(zh, away)
            where = jnp.stack([mine, dev]).astype(jnp.int32)

            last = [(v, 144) for v in (keep1, got1, got_y1, *q1_got)] + [(out, tok)]
            last += [(v, v.shape[0]) for v in (home, e_keep, x_keep, home_x, away, got_z)]
            last += [(v, 64) for v in (keep2, got2, got_y2)] + [(v, v.shape[0]) for v in q_got]
            last += [(v, 48) for v in (keep3, got3, got_y3)]
            counts = [c for _, c in last]
            flat = [((per, w), F32) for w in (3 * D, D, D, 2 * D, D, FF)] + [((4 * per, D), F32)]
            done = run(
                functools.partial(finish, counts),
                [(where, SMEM)] + [(v, None) for v, _ in last],
                [((2, tok, D), BF), ((1, 1), F32), ((2, tok, D), F32), ((2, tok, D), F32)] + flat + [((3, per), F32)] * 2,
                name="finish",
            )
            return (done[0], done[1].reshape(()), *done[2:])

        def back_home(kept, recv):
            return jnp.where(mine == 0, jnp.stack([kept, recv]), jnp.stack([recv, kept]))

        def summed(g):
            return lax.psum_scatter(g, ("dp", "seq"), scatter_dimension=0, tiled=True).astype(F32)

        def rejoin(keep, send, n):
            g = jnp.stack([v[: 256 * n].reshape(2, 8, n, 16, D) for v in (keep, send)], 1)
            return g.reshape(G, n, 16, D)

        def full(g):
            return g.transpose(0, 2, 1, 3).reshape(G * 16, -1)

        small = lax.psum(send2[1024:].astype(F32), ("dp", "seq"))
        all1, all2, all3 = rejoin(keep1, send1, 9), rejoin(keep2, send2, 4), rejoin(keep3, send3, 3)
        g_norm = lax.dynamic_slice(small, (0, dev * per), (6, per))
        return (
            back_home(out[:tok], home[:tok]),
            jnp.sum(small[6]) / (jnp.sum(small[7]) * D),
            back_home(x_keep, home_x.astype(F32)),
            back_home(e_keep, home[tok:].astype(F32)),
            summed(full(all3)),
            summed(full(all2[:, 3:])),
            summed(full(all2[:, 2:3])),
            summed(full(all2[:, :2])),
            summed(full(all1[:, 8:])),
            summed(full(all1[:, :4])),
            summed(all1[:, 4:8].reshape(FF, D)),
            g_norm[:3],
            g_norm[3:],
        )

    return shards


def solution(mesh):
    rows, both = P("dp", "seq", None), P(("dp", "seq"), None)
    norm = P(None, ("dp", "seq"))
    return jax.shard_map(
        make_shards(mesh.shape["dp"], mesh.shape["seq"]),
        mesh=mesh,
        in_specs=(rows, rows, rows, P("dp", None), P("dp", None), P("dp", "seq")) + (both,) * 7 + (norm, norm),
        out_specs=(rows, P(), rows, rows) + (both,) * 7 + (norm, norm),
        check_vma=False,
    )
```

```python
import functools

import jax
import jax.numpy as jnp
from jax import lax
from jax.experimental import pallas as pl
from jax.experimental.pallas import tpu as pltpu
from jax.sharding import PartitionSpec as P

HEADS = 8
HEAD_DIM = 64
EPS = 1e-5
NEG = -1e30
SCALE = 0.125
D = 512
FF = 2048
HALF = 256
G = 32
BF = jnp.bfloat16
F32 = jnp.float32
MIB = 1 << 20

DEVICE, PLACE_1, PLACE_2, SLOT_A, SLOT_B, SLOT_F = 1, 2, 18, 34, 66, 98

NN = (((1,), (0,)), ((), ()))
NT = (((1,), (1,)), ((), ()))
TN = (((0,), (0,)), ((), ()))


def dot(a, b, dims=NN):
    return lax.dot_general(a, b, dims, preferred_element_type=F32)


def whole(shape):
    return pl.BlockSpec(shape, lambda i: (0,) * len(shape))


SMEM = pl.BlockSpec(memory_space=pltpu.SMEM)


def call(body, ins, outs, scratch=(), name=None, vmem=16):
    return pl.pallas_call(
        body,
        grid=(1,),
        in_specs=[whole(a.shape) if s is None else s for a, s in ins],
        out_specs=[whole(o[0]) if len(o) == 2 else pl.BlockSpec(memory_space=pltpu.HBM) for o in outs],
        out_shape=[jax.ShapeDtypeStruct(*o) if len(o) == 2 else pltpu.HBM(*o[:2]) for o in outs],
        scratch_shapes=list(scratch),
        compiler_params=pltpu.CompilerParams(vmem_limit_bytes=vmem * MIB),
        name=name,
        cost_estimate=pl.CostEstimate(flops=1000, bytes_accessed=1000, transcendentals=0),
    )(*[a for a, _ in ins])


def unpack(ids, table, parts, *targets):
    each = parts[0].shape[0]
    for p, part in enumerate(parts):
        for i in range(each):
            group = ids[table + each * p + i]
            for ref, first, count, height in targets:
                at = pl.multiple_of(group * height, 16)
                block = part[i, first : first + count]
                if height == 16:
                    ref[:, pl.ds(at, 16), :] = block
                else:
                    ref[pl.ds(at, height), :] = block.reshape(height, D)


def norm_rows(parts):
    return sum(jnp.sum(part[:, 5].astype(F32), axis=0) for part in parts)


def set_mask(mask, segs, key, query, position):
    length, rows = mask.shape
    columns = jnp.transpose(segs[...])
    same = columns[:, key : key + 1] == segs[query : query + 1, :rows]
    ahead = columns[:, position : position + 1] <= segs[position : position + 1, :rows]
    mask[...] = jnp.where(same & ahead, 0.0, NEG)


def put(ids, first, ref, chunks_each, j, value):
    value = value.astype(BF)
    each = value.shape[0] // 16
    for i in range(16):
        at = ids[first + i] * (16 * chunks_each) + 16 * j
        ref[pl.ds(pl.multiple_of(at, 16), each), :] = value[each * i : each * i + each]


def norm_forward(resid, gain, bias):
    centre = resid - jnp.mean(resid, axis=-1, keepdims=True)
    rstd = lax.rsqrt(jnp.mean(centre * centre, axis=-1, keepdims=True) + EPS)
    xhat = centre * rstd
    return xhat, rstd, xhat * gain + bias


def norm_back(g, xhat, rstd, gain):
    e = g * gain
    m1 = jnp.mean(e, axis=-1, keepdims=True)
    m2 = jnp.mean(e * xhat, axis=-1, keepdims=True)
    dr = (e - m1 - xhat * m2) * rstd
    return dr, jnp.sum(g * xhat, axis=0, keepdims=True), jnp.sum(g, axis=0, keepdims=True)


def head_half(x, e):
    lane = lax.broadcasted_iota(jnp.int32, x.shape, 1)
    return jnp.where((lane < HEAD_DIM) == (e == 0), x, jnp.zeros_like(x))


def attend(q_ref, kv_ref, mask_ref, p_ref, rl_ref, at_ref, p_out, sems):
    def leave(hp, slot):
        return pltpu.make_async_copy(p_ref.at[slot], p_out.at[pl.ds(2 * hp, 2)], sems.at[slot])

    def pair(hp, carry):
        slot = hp % 2

        @pl.when(hp >= 2)
        def _():
            leave(hp - 2, slot).wait()

        c0 = pl.multiple_of(hp * 128, 128)
        k2 = kv_ref[:, pl.ds(c0, 128)]
        v2 = kv_ref[:, pl.ds(pl.multiple_of(D + c0, 128), 128)]
        q2 = q_ref[:, pl.ds(c0, 128)]
        for e in range(2):
            s = dot(k2, head_half(q2, e), NT) + mask_ref[...]
            p = jnp.exp(s - jnp.max(s, axis=0, keepdims=True))
            rl = 1.0 / jnp.sum(p, axis=0, keepdims=True)
            pb = p.astype(BF)
            p_ref[slot, e] = pb
            rl_ref[2 * hp + e] = rl
            o = dot(v2, pb, TN) * rl
            at_ref[pl.ds(pl.multiple_of((2 * hp + e) * HEAD_DIM, HEAD_DIM), HEAD_DIM), :] = o[
                e * HEAD_DIM : (e + 1) * HEAD_DIM
            ].astype(BF)
        leave(hp, slot).start()
        return carry

    pairs = HEADS // 2
    lax.fori_loop(0, pairs, pair, 0)
    for hp in (pairs - 2, pairs - 1):
        leave(hp, hp % 2).wait()


def keep_copy(held, out, sem):
    copy = pltpu.make_async_copy(held, out, sem)
    copy.start()
    return copy


def attend_back(first, q_ref, kv_ref, p_ref, rl_ref, do_ref, dkv_ref, dqt_ref):
    def pair(i, carry):
        hp = first // 2 + i
        c0 = pl.multiple_of(hp * 128, 128)
        o0 = pl.multiple_of(i * 128, 128)
        k2 = kv_ref[:, pl.ds(c0, 128)]
        v2 = kv_ref[:, pl.ds(pl.multiple_of(D + c0, 128), 128)]
        q2 = q_ref[:, pl.ds(c0, 128)]
        do2 = do_ref[:, pl.ds(c0, 128)]
        dk = dv = None
        for e in range(2):
            dom = head_half(do2, e)
            dp = dot(v2, dom, NT)
            p = p_ref[2 * hp + e].astype(F32) * rl_ref[2 * hp + e]
            t = p * dp
            ds = (t - p * jnp.sum(t, axis=0, keepdims=True)).astype(BF)
            dk_e = dot(ds, head_half(q2, e))
            dv_e = dot(p.astype(BF), dom)
            dk = dk_e if dk is None else dk + dk_e
            dv = dv_e if dv is None else dv + dv_e
            dqt = dot(k2, ds, TN) * SCALE
            dqt_ref[pl.ds(pl.multiple_of((2 * i + e) * HEAD_DIM, HEAD_DIM), HEAD_DIM), :] = dqt[
                e * HEAD_DIM : (e + 1) * HEAD_DIM
            ]
        dkv_ref[:, pl.ds(o0, 128)] = dk.astype(BF)
        dkv_ref[:, pl.ds(pl.multiple_of(HALF + o0, 128), 128)] = dv.astype(BF)
        return carry

    lax.fori_loop(0, HEADS // 4, pair, 0)


def cols(ref, c, width):
    picks = [ref[:, pl.ds(pl.multiple_of((2 * y + c) * width, width), width)] for y in range(2)]
    return jnp.concatenate(picks, 1)


def rows_of(ref, c, width):
    picks = [ref[pl.ds(pl.multiple_of((2 * y + c) * width, width), width), :] for y in range(2)]
    return jnp.concatenate(picks, 0)


def sides(ids, keep, send):
    return ((send, 1 - ids[0]), (keep, ids[0]))


def pack(s_in, s_out, c_in, c_q, c_out, up, down, gain, bias, at, pa, pb, pf):
    for j in range(3):
        pa[j] = s_in[:, j * D : (j + 1) * D]
    pb[0] = s_out[...]
    for j in range(2):
        pb[1 + j] = c_in[:, j * D : (j + 1) * D]
    pb[3] = c_q[...]
    pb[4] = c_out[...]
    for j in range(4):
        pf[j] = up[:, j * D : (j + 1) * D]
        pf[4 + j] = down[16 * j : 16 * j + 16, :]
    rows = jnp.concatenate([gain[...], bias[...], jnp.zeros((10, 16), BF)], 0)
    column = lax.broadcasted_iota(jnp.int32, (16, D), 1)
    row = lax.broadcasted_iota(jnp.int32, (16, D), 0)
    pick = (column == at[0] * 16 + row).astype(BF)
    pb[5] = dot(rows, pick).astype(BF)


def join(full, near, far):
    half = near.shape[0]
    full[:half] = near[...]
    full[half:] = far[...]


def self_forward(rows, ids, near, far, wa0, wa1, wa2, wa3, segs,
                 xf_out, w_out, q_out, kv_out, p_out, rl, at, mask, xf, w, q, kv, p, p_sems, sems):
    join(xf, near, far)
    copies = [keep_copy(xf, xf_out, sems.at[0])]
    unpack(ids, SLOT_A, (wa0, wa1, wa2, wa3), (w, 0, 3, 16))
    copies.append(keep_copy(w, w_out, sems.at[1]))
    set_mask(mask, segs, 0, 0, 1)
    q[...] = (dot(xf[:rows], w[0]).astype(BF).astype(F32) * SCALE).astype(BF)
    kv[:, :D] = dot(xf[...], w[1]).astype(BF)
    kv[:, D:] = dot(xf[...], w[2]).astype(BF)
    copies += [keep_copy(q, q_out, sems.at[2]), keep_copy(kv, kv_out, sems.at[3])]
    attend(q, kv, mask, p, rl, at, p_out, p_sems)
    for copy in copies:
        copy.wait()


def cross_forward(rows, ids, xf, near, far, at1, wb0, wb1, wb2, wb3, segs,
                  ef_out, w, norms, xh1, rs1, low1_out, q_out, kv_out, p_out, rl, at,
                  mask, ef, low1, q, kv, p, p_sems, sems):
    join(ef, near, far)
    copies = [keep_copy(ef, ef_out, sems.at[0])]
    unpack(ids, SLOT_B, (wb0, wb1, wb2, wb3), (w, 0, 5, 16))
    set_mask(mask, segs, 2, 0, 3)
    gb = norm_rows((wb0, wb1, wb2, wb3))
    norms[...] = gb
    resid = xf[...].astype(F32) + dot(at1[...], w[0], TN)
    xhat, rstd, n1 = norm_forward(resid, gb[0:1], gb[3:4])
    xh1[...] = xhat
    rs1[...] = rstd
    low1[...] = n1.astype(BF)
    copies.append(keep_copy(low1, low1_out, sems.at[1]))
    q[...] = (dot(low1[...], w[3]).astype(BF).astype(F32) * SCALE).astype(BF)
    kv[:, :D] = dot(ef[...], w[1]).astype(BF)
    kv[:, D:] = dot(ef[...], w[2]).astype(BF)
    copies += [keep_copy(q, q_out, sems.at[2]), keep_copy(kv, kv_out, sems.at[3])]
    attend(q, kv, mask, p, rl, at, p_out, p_sems)
    for copy in copies:
        copy.wait()


def ffn_both(ids, xh1, at2, teach, valid, wb, norms, wf0, wf1, wf2, wf3,
             out, small, d_r2, d_mix, keep, send, act, hid, low2, wup, wdn):
    gb = norms[...]
    n1 = xh1[...] * gb[0:1] + gb[3:4]
    wco = wb[4]
    unpack(ids, SLOT_F, (wf0, wf1, wf2, wf3), (wup, 0, 4, 16), (wdn, 4, 4, 64))
    xh2, rs2, n2 = norm_forward(n1 + dot(at2[...], wco, TN), gb[1:2], gb[4:5])
    low2[...] = n2.astype(BF)
    for j in range(4):
        h = dot(low2[...], wup[j])
        hid[j] = h
        act[:, j * D : (j + 1) * D] = (h / (1.0 + jnp.exp(-h))).astype(BF)
    r3 = n2 + dot(act[...], wdn[...])
    xh3, rs3, final = norm_forward(r3, gb[2:3], gb[5:6])
    out[...] = final.astype(BF)
    err = (final - teach[...].astype(F32)) * valid[...]
    small[...] = jnp.zeros_like(small)
    small[6:7] = jnp.sum(err * err, axis=0, keepdims=True)
    lane = lax.broadcasted_iota(jnp.int32, (1, D), 1)
    small[7:8] = jnp.where(lane == ids[DEVICE], jnp.sum(valid[...]), 0.0)
    d_r3, dg, db = norm_back(err, xh3, rs3, gb[2:3])
    small[2:3] = dg
    small[5:6] = db
    dffn = d_r3.astype(BF)
    for ref, at in sides(ids, keep, send):
        put(ids, PLACE_1, ref, 9, 4, dot(cols(act, at, FF // 4), dffn, TN))
    dn2 = d_r3
    for j in range(4):
        da = dot(dffn, wdn[j * D : (j + 1) * D], NT)
        h = hid[j]
        sig = 1.0 / (1.0 + jnp.exp(-h))
        dh = (da * (sig * (1.0 + h * (1.0 - sig)))).astype(BF)
        for ref, at in sides(ids, keep, send):
            put(ids, PLACE_1, ref, 9, j, dot(cols(low2, at, 128), dh, TN))
        dn2 = dn2 + dot(dh, wup[j], NT)
    dr2, dg, db = norm_back(dn2, xh2, rs2, gb[1:2])
    small[1:2] = dg
    small[4:5] = db
    d_r2[...] = dr2
    dcross = dr2.astype(BF)
    for ref, at in sides(ids, keep, send):
        put(ids, PLACE_1, ref, 9, 8, dot(rows_of(at2, at, 128), dcross))
    d_mix[...] = dot(dcross, wco, NT).astype(BF)


def cross_back_a(q, kv, p, rl, d_mix, dkv, dq, dqt):
    attend_back(0, q, kv, p, rl, d_mix, dkv, dqt)
    dq[...] = jnp.transpose(dqt[...]).astype(BF)


def project(own, parts, dkv_a, dkv_b, wk, wv, extra=0.0):
    out = dot(dkv_a[:, :HALF], wk[:, :HALF], NT) + dot(dkv_b[:, :HALF], wk[:, HALF:], NT)
    out = out + dot(dkv_a[:, HALF:], wv[:, :HALF], NT) + dot(dkv_b[:, HALF:], wv[:, HALF:], NT)
    each = own.shape[0]
    own[...] = out[:each] + extra
    for i, part in enumerate(parts):
        part[...] = out[each * (i + 1) : each * (i + 2)].astype(BF)


def cross_back_b(n_parts, ids, ef, q, kv, p, rl, d_mix, dkv_a, dq_a, wb, norms, d_r2, low1, xh1,
                 rs1, at1, small, own, *rest):
    parts, (d_mix1, d_r1, keep, send, dkv, dqt) = rest[:n_parts], rest[n_parts:]
    attend_back(4, q, kv, p, rl, d_mix, dkv, dqt)
    project(own, parts, dkv_a, dkv, wb[1], wb[2])
    dq = jnp.concatenate([dq_a[...], jnp.transpose(dqt[...]).astype(BF)], 1)
    gb = norms[...]
    dn1 = d_r2[...] + dot(dq, wb[3], NT)
    dr1, dg, db = norm_back(dn1, xh1[...], rs1[...], gb[0:1])
    row = lax.broadcasted_iota(jnp.int32, (16, D), 0)
    sums = jnp.where(row == 0, dg, jnp.where(row == 3, db, small[...]))
    send[1024:1040] = sums.astype(BF)
    d_r1[...] = dr1
    dself = dr1.astype(BF)
    for ref, at in sides(ids, keep, send):
        lhs = cols(ef, at, 128)
        for j in range(2):
            span = slice(j * HALF, (j + 1) * HALF)
            g = jnp.concatenate([dot(lhs, dkv_a[:, span], TN), dot(lhs, dkv[:, span], TN)], 1)
            put(ids, PLACE_2, ref, 4, j, g)
        put(ids, PLACE_2, ref, 4, 2, dot(cols(low1, at, 128), dq, TN))
        put(ids, PLACE_2, ref, 4, 3, dot(rows_of(at1, at, 128), dself))
    d_mix1[...] = dot(dself, wb[0], NT).astype(BF)


def self_back_b(n_parts, rows, ids, xf, q, kv, p, rl, d_mix, dkv_a, dq_a, wa, d_r1, own, *rest):
    parts, (keep, send, dkv, dqt) = rest[:n_parts], rest[n_parts:]
    attend_back(4, q, kv, p, rl, d_mix, dkv, dqt)
    dq = jnp.concatenate([dq_a[...], jnp.transpose(dqt[...]).astype(BF)], 1)
    through_q = d_r1[...] + dot(dq, wa[0], NT)
    project(own, parts, dkv_a, dkv, wa[1], wa[2], through_q)
    for ref, at in sides(ids, keep, send):
        lhs = cols(xf, at, 128)
        put(ids, PLACE_2, ref, 3, 0, dot(lhs[:rows], dq, TN))
        for j in range(2):
            span = slice(j * HALF, (j + 1) * HALF)
            g = jnp.concatenate([dot(lhs, dkv_a[:, span], TN), dot(lhs, dkv[:, span], TN)], 1)
            put(ids, PLACE_2, ref, 3, 1 + j, g)


def tree_sum(terms):
    while len(terms) > 1:
        terms = [a + b for a, b in zip(terms[::2], terms[1::2])] + terms[len(terms) & ~1 :]
    return terms[0]


ANY = pl.BlockSpec(memory_space=pl.ANY)


def fetch(ref, start, count, to, sem):
    copy = pltpu.make_async_copy(ref.at[pl.ds(start, count)], to, sem)
    copy.start()
    return copy


def mix(name, *outs):
    arrays, terms, plan = [], [], []
    for dtype, segments in outs:
        plan.append([])
        for segment in segments:
            used = []
            for array, start, count in segment:
                at = [i for i, v in enumerate(arrays) if v is array]
                if not at:
                    arrays.append(array)
                used.append(len(terms))
                terms.append((at[0] if at else len(arrays) - 1, start, count, array.dtype))
            plan[-1].append(used)

    def body(*refs):
        for out, segments in zip(refs[len(arrays) :], plan):
            first = 0
            for used in segments:
                count = terms[used[0]][2]
                parts = [refs[k][start : start + count].astype(F32) for k, start, _, _ in (terms[i] for i in used)]
                out[first : first + count] = tree_sum(parts).astype(out.dtype)
                first += count

    shapes = [((sum(t[0][2] for t in segments), D), dtype) for dtype, segments in outs]
    return call(body, [(v, None) for v in arrays], shapes, name=name)


def finish(counts, *refs):
    where, refs = refs[0], refs[1:]
    sources, results = refs[: len(counts)], refs[len(counts) :]
    refs = [ref.at[:count] for ref, count in zip(sources, counts)]
    one, (out, home, e_keep, x_keep, home_x, z_own, z_got, *refs) = refs[:6], refs[6:]
    two, three = refs[:6], refs[6:]
    outputs, loss, g_x, g_e, g_in, g_so, g_cq, g_cin, g_co, g_up, g_down, g_gain, g_bias = results
    mine = where[0]
    tok = e_keep.shape[0]
    outputs[mine] = out[...]
    outputs[1 - mine] = home[:tok]
    g_e[mine] = e_keep[...]
    g_e[1 - mine] = home[tok : 2 * tok].astype(F32)
    g_x[mine] = x_keep[...]
    g_x[1 - mine] = home_x[...].astype(F32)
    t1 = tree_sum([r[...].astype(F32) for r in one] + [home[2 * tok :].astype(F32)])
    for j in range(4):
        g_up[:, j * D : (j + 1) * D] = t1[16 * j : 16 * j + 16]
    g_down[...] = t1[64:128]
    g_co[...] = t1[128:144]
    t2 = tree_sum([r[...].astype(F32) for r in two[:3]] + [r[:64].astype(F32) for r in two[3:]] + [z_got[:64].astype(F32)])
    for j in range(2):
        g_cin[:, j * D : (j + 1) * D] = t2[16 * j : 16 * j + 16]
    g_cq[...] = t2[32:48]
    g_so[...] = t2[48:64]
    t3 = tree_sum([r[...].astype(F32) for r in three] + [r[128:176].astype(F32) for r in two[3:]] + [z_got[64:112].astype(F32)])
    for j in range(3):
        g_in[:, j * D : (j + 1) * D] = t3[16 * j : 16 * j + 16]
    small = z_own[112:128].astype(F32) + z_got[112:128].astype(F32)
    total = jnp.sum(small[6:7], axis=1, keepdims=True)
    loss[...] = total / (jnp.sum(small[7:8], axis=1, keepdims=True) * D)
    column = lax.broadcasted_iota(jnp.int32, (16, D), 1)
    row = lax.broadcasted_iota(jnp.int32, (16, D), 0)
    pick = (column == where[1] * 16 + row).astype(F32)
    own = lax.dot_general(small[:8], pick, NT, precision=lax.Precision.HIGHEST, preferred_element_type=F32)
    g_gain[...] = own[0:3]
    g_bias[...] = own[3:6]


def tie(*values):
    return lax.optimization_barrier(values)


def make_shards(nd, ns):
    n_dev = nd * ns
    half = ns // 2
    per = G * 16 // n_dev
    fast = nd == 4 and ns == 8
    run = functools.partial(call, vmem=20 if fast else 48)

    core, y, x, zl, zh = ("dp", 1), ("dp", 2), ("seq", 1), ("seq", 2), ("seq", 4)

    def shards(inputs, encoder, teacher, dec_seg, enc_seg, dec_valid, self_in, self_out,
               cross_query, cross_in, cross_out, ffn_up, ffn_down, norm_gain, norm_bias):
        tok = inputs.shape[1]
        rows = 2 * tok
        length = dec_seg.shape[1]
        dp_at, seq_at = lax.axis_index("dp"), lax.axis_index("seq")
        dev = dp_at * ns + seq_at
        mine = seq_at // half

        def flip(bit, arrays):
            axis, b = bit
            size = nd if axis == "dp" else ns
            flat = [v.reshape(-1, D) for v in arrays]
            got = lax.ppermute(
                flat[0] if len(flat) == 1 else jnp.concatenate(flat, 0),
                axis, [(i, i ^ b) for i in range(size)],
            )
            out, start = [], 0
            for v, f in zip(arrays, flat):
                out.append(lax.slice_in_dim(got, start, start + f.shape[0]).reshape(v.shape))
                start += f.shape[0]
            return out

        def swap(bit, array):
            return flip(bit, [array])[0]

        def of(v, i):
            return lax.dynamic_index_in_dim(v, i, 0, keepdims=False)

        def other(v):
            return of(v, 1 - mine)

        def append(v, got):
            return jnp.concatenate([v, got], 0)

        valid_away = jnp.pad(other(dec_valid).astype(BF)[None], ((0, 15), (0, D - tok)))

        row_bits = (2, 1) if fast else tuple(1 << b for b in range(half.bit_length() - 1))
        slots = jnp.arange(half, dtype=jnp.int32)

        def pieces(bits):
            masks = sum((((slots >> i) & 1) * b) for i, b in enumerate(bits))[:, None]
            return (seq_at ^ masks ^ jnp.array([[0, half]], jnp.int32)).reshape(-1)

        pos = (pieces(row_bits)[:, None] * tok + jnp.arange(tok, dtype=jnp.int32)[None]).reshape(-1)
        dec_k = of(dec_seg, mine).reshape(ns, tok)[pieces(row_bits)].reshape(-1)
        enc_k = of(enc_seg, mine).reshape(ns, tok)[pieces(row_bits)].reshape(-1)
        segs = jnp.stack([dec_k, pos, enc_k] + [jnp.zeros_like(pos)] * 5).astype(F32)

        if fast:
            mats = [self_in, self_out, cross_in, cross_query, cross_out, ffn_up, ffn_down, norm_gain, norm_bias]
            wa, wb, wf = run(
                pack,
                [(w, None) for w in mats] + [(dev.astype(jnp.int32)[None], SMEM)],
                [((3, 16, D), BF), ((6, 16, D), BF), ((8, 16, D), BF)],
                name="pack",
                vmem=56,
            )
            wa, wb, wf = wa[None], wb[None], wf[None]
            got_x, got_a = flip(zh, [other(inputs), wa])
            got_x, got_a, wb, wf, segs = tie(got_x, got_a, wb, wf, segs)
            got_b, got_f = flip(zh, [wb, wf])
            xf, wa = jnp.stack([of(inputs, mine), got_x])[None], append(wa, got_a)
            got_x, got_a = flip(zl, [xf, wa])
            got_x, got_a, got_b, got_f, away_e = tie(got_x, got_a, got_b, got_f, other(encoder))
            xf, wa = append(xf, got_x), append(wa, got_a)
            wb, wf = append(wb, got_b), append(wf, got_f)
            got_x, got_a = flip(x, [xf, wa])
            got_e, got_t, got_v = flip(zh, [away_e, other(teacher), valid_away])
            got_b, got_f = swap(y, wb), swap(zl, wf)
            ef = jnp.stack([of(encoder, mine), got_e])[None]
            got_x, got_a, got_b, got_f, ef = tie(got_x, got_a, got_b, got_f, ef)
            wa, wb, wf = append(wa, got_a), append(wb, got_b), append(wf, got_f)
            got_a, got_b, got_e, got_f = swap(y, wa), swap(x, wb), swap(zl, ef), swap(x, wf)
            wa_far = swap(core, wa)
            got_a, got_b, got_e, wa_far = tie(got_a, got_b, got_e, wa_far)
            wa = [wa, got_a, wa_far, swap(core, got_a)]
            wb, ef = append(wb, got_b), append(ef, got_e)
            got_b, got_e = swap(zl, wb), swap(x, ef)
            got_f, wa[3] = tie(got_f, wa[3])
            wf = append(wf, got_f)
            got_f = swap(y, wf)
            wb_far, wf_far = swap(core, wb), swap(core, wf)
        else:
            got_x, got_e, got_t, got_v = flip(
                ("seq", half), [other(inputs), other(encoder), other(teacher), valid_away]
            )
            xf, ef = jnp.stack([of(inputs, mine), got_x])[None], jnp.stack([of(encoder, mine), got_e])[None]
            for bit in row_bits:
                got_x, got_e = flip(("seq", bit), [xf, ef])
                if bit != row_bits[-1]:
                    xf, ef = append(xf, got_x), append(ef, got_e)

            def gathered(w):
                return lax.all_gather(w, ("dp", "seq"), axis=0, tiled=True)

            def grouped(w):
                return w.reshape(G, 16, w.shape[1] // D, D).transpose(0, 2, 1, 3)

            wa = grouped(gathered(self_in))
            mine_only = lax.dynamic_update_slice(
                jnp.zeros((16, D), BF), jnp.concatenate([norm_gain, norm_bias], 0), (0, dev * per)
            )
            all_norms = lax.psum(mine_only.astype(F32), ("dp", "seq")).astype(BF)
            all_norms = jnp.pad(all_norms[None], ((0, G - 1), (0, 0), (0, 0)))[:, None]
            rest = [grouped(gathered(w)) for w in (self_out, cross_in, cross_query, cross_out)]
            down = gathered(ffn_down).reshape(G, 4, 16, D)
            wb = jnp.concatenate(rest + [all_norms], 1)
            wf = jnp.concatenate([grouped(gathered(ffn_up)), down], 1)
            wa, wb, wf = [[w[8 * i : 8 * i + 8] for i in range(4)] for w in (wa, wb, wf)]
        x_near, x_far = xf.reshape(-1, D), got_x.reshape(-1, D)
        teach = jnp.concatenate([of(teacher, mine), got_t], 0)
        valid = jnp.concatenate([of(dec_valid, mine).astype(F32), got_v[0, :tok].astype(F32)])[:, None]

        def spread(v, bits):
            return sum((((v & b) != 0).astype(jnp.int32) << i) for i, b in enumerate(bits))

        if fast:
            i16 = jnp.arange(16, dtype=jnp.int32)
            g32 = jnp.arange(32, dtype=jnp.int32)
            dev16 = (dp_at >> 1) * 8 + seq_at

            def came_from(bits):
                return dev ^ sum((((g32 >> i) & 1) * b for i, b in enumerate(bits)))

            ids = jnp.concatenate(
                [
                    jnp.stack([dp_at & 1, dev]).astype(jnp.int32),
                    spread(i16 ^ dev16, (4, 2, 1, 8)),
                    spread(i16 ^ dev16, (4, 2, 1, 8)),
                    came_from((4, 2, 1, 16, 8)),
                    came_from((4, 16, 1, 2, 8)),
                    came_from((4, 2, 1, 16, 8)),
                ]
            )
        else:
            i16, g32 = jnp.arange(16, dtype=jnp.int32), jnp.arange(32, dtype=jnp.int32)
            ids = jnp.concatenate([jnp.stack([0 * dev, dev]).astype(jnp.int32), i16, i16, g32, g32, g32])

        sm = (ids, SMEM)
        p_shape = (HEADS, length, rows)
        def held(*shapes):
            return (
                [pltpu.VMEM((length, rows), F32)]
                + [pltpu.VMEM(v, BF) for v in shapes]
                + [pltpu.VMEM((2, 2, length, rows), BF), pltpu.SemaphoreType.DMA((2,)), pltpu.SemaphoreType.DMA((4,))]
            )

        all_rows, own_rows, both_kv = (length, D), (rows, D), (length, 2 * D)
        own_x = x_near[:rows]
        xf, wa, q1, kv1, p1, rl1, at1 = run(
            functools.partial(self_forward, rows),
            [sm, (x_near, None), (x_far, None)] + [(v, None) for v in wa] + [(segs, None)],
            [(all_rows, BF, True), ((3, D, D), BF, True), (own_rows, BF, True), (both_kv, BF, True),
             (p_shape, BF, True), ((HEADS, 1, rows), F32), ((D, rows), BF)],
            scratch=held(all_rows, (3, D, D), own_rows, both_kv),
            name="self_forward",
        )
        if fast:
            got_b, got_e, wb_far, at1 = tie(got_b, got_e, wb_far, at1)
            wb = [wb, got_b, wb_far, swap(core, got_b)]
        e_near, e_far = ef.reshape(-1, D), got_e.reshape(-1, D)
        ef, wb, norms, xh1, rs1, low1, q2, kv2, p2, rl2, at2 = run(
            functools.partial(cross_forward, rows),
            [sm, (own_x, None), (e_near, None), (e_far, None), (at1, None)] + [(v, None) for v in wb] + [(segs, None)],
            [(all_rows, BF, True), ((5, D, D), BF), ((16, D), F32), (own_rows, F32), ((rows, 1), F32),
             (own_rows, BF, True), (own_rows, BF, True), (both_kv, BF, True), (p_shape, BF, True),
             ((HEADS, 1, rows), F32), ((D, rows), BF)],
            scratch=held(all_rows, own_rows, own_rows, both_kv),
            name="cross_forward",
        )
        if fast:
            got_f, wf_far, at2 = tie(got_f, wf_far, at2)
            wf = [wf, got_f, wf_far, swap(core, got_f)]
        out, small, d_r2, d_mix2, keep1, send1 = run(
            ffn_both,
            [sm, (xh1, None), (at2, None), (teach, None), (valid, None), (wb, None), (norms, None)]
            + [(v, None) for v in wf],
            [((rows, D), BF), ((16, D), F32), ((rows, D), F32), ((rows, D), BF)] + [((2304, D), BF)] * 2,
            scratch=[pltpu.VMEM((rows, FF), BF), pltpu.VMEM((4, rows, D), F32), pltpu.VMEM((rows, D), BF),
                     pltpu.VMEM((4, D, D), BF), pltpu.VMEM((FF, D), BF)],
            name="ffn_both",
        )

        kv_half = [((length, D), BF), ((rows, HALF), BF)]
        d_rows = [pltpu.VMEM((HALF, rows), F32)]
        both_scratch = [pltpu.VMEM((length, D), BF)] + d_rows
        row_parts = [((rows, D), F32)] + [((rows, D), BF)] * (half - 1)
        partners = [sum(((i >> k) & 1) * b for k, b in enumerate(row_bits)) for i in range(1, half)]

        if fast:
            got1 = swap(core, send1)
        dkv2, dq2 = run(
            cross_back_a,
            [(q2, None), (kv2, None), (p2, None), (rl2, None), (d_mix2, None)],
            kv_half,
            scratch=d_rows,
            name="cross_back_a",
        )
        if fast:
            got1, d_mix2, dkv2 = tie(got1, d_mix2, dkv2)
            got_y1 = swap(y, (keep1[1152:].astype(F32) + got1[1152:].astype(F32)).astype(BF))
        e_own, *rest = run(
            functools.partial(cross_back_b, half - 1),
            [sm, (ef, None), (q2, None), (kv2, None), (p2, None), (rl2, None), (d_mix2, None),
             (dkv2, None), (dq2, None), (wb, None), (norms, None), (d_r2, None), (low1, None),
             (xh1, None), (rs1, None), (at1, None), (small, None)],
            row_parts + [((rows, D), BF), ((rows, D), F32), ((1024, D), BF), ((1040, D), BF)],
            scratch=both_scratch,
            name="cross_back_b",
        )
        e_parts, (d_mix1, d_r1, keep2, send2) = rest[: half - 1], rest[half - 1 :]
        if fast:
            got2 = swap(core, send2)
        e_got = [swap(("seq", m), part) for m, part in zip(partners, e_parts)]
        dkv1, dq1 = run(
            cross_back_a,
            [(q1, None), (kv1, None), (p1, None), (rl1, None), (d_mix1, None)],
            kv_half,
            scratch=d_rows,
            name="self_back_a",
        )
        if fast:
            got2, got_y1, d_mix1, dkv1, *e_got = tie(got2, got_y1, d_mix1, dkv1, *e_got)
            one = lambda start, count: [(v, start, count) for v in (keep1, got1, got_y1)]
            away, *quads1 = mix(
                "sum_y2",
                (BF, [[(keep2, 512, 512), (got2, 512, 512)], [(send2, 1024, 16), (got2, 1024, 16)]]),
                *[(BF, [one(288 * i, 288)]) for i in (1, 2, 3)],
            )
            got_y2 = swap(y, away)
            small_y2 = (away, 512, 16)
            q1_got = [swap(("seq", m), part) for m, part in zip(partners, quads1)]
        x_own, *rest = run(
            functools.partial(self_back_b, half - 1, rows),
            [sm, (xf, None), (q1, None), (kv1, None), (p1, None), (rl1, None), (d_mix1, None),
             (dkv1, None), (dq1, None), (wa, None), (d_r1, None)],
            row_parts + [((768, D), BF)] * 2,
            scratch=both_scratch,
            name="self_back_b",
        )
        x_parts, (keep3, send3) = rest[: half - 1], rest[half - 1 :]

        def summed_rows(name, own, got, *more):
            terms = [own] + got
            return mix(name, (F32, [[(t, 0, tok) for t in terms]]),
                       (BF, [*more[:1], [(t, tok, tok) for t in terms], *more[1:]]))

        if fast:
            q1_got[0], q1_got[1], q1_got[2], got_y2, send3, *x_parts = tie(*q1_got, got_y2, send3, *x_parts)
        x_got = [swap(("seq", m), part) for m, part in zip(partners, x_parts)]
        if fast:
            got3 = swap(core, send3)
        more = [one(144, 144) + [(v, 144, 144) for v in q1_got]] if fast else []
        e_keep, away = summed_rows("sum_e", e_own, e_got, [(out, tok, tok)], *more)
        home = swap(("seq", half), away)
        if fast:
            (away,) = mix("sum_y3", (BF, [[(keep3, 384, 384), (got3, 384, 384)]]))
            got_y3 = swap(y, away)
        x_keep, away = summed_rows("sum_x", x_own, x_got)
        home_x = swap(("seq", half), away)

        if fast:
            def two(start, count):
                return [(v, start, count) for v in (keep2, got2, got_y2)]

            def three(start, count):
                return [(v, start, count) for v in (keep3, got3, got_y3)]

            quads = mix(
                "sum_quads",
                *[(BF, [two(128 * i, 128), three(96 * i, 96), [small_y2, (got_y2, 512, 16)]]) for i in (1, 2, 3)],
            )
            q_got = [swap(("seq", m), part) for m, part in zip(partners, quads)]
            (away,) = mix(
                "sum_zh",
                (BF, [two(64, 64) + [(v, 64, 64) for v in q_got], three(48, 48) + [(v, 176, 48) for v in q_got],
                      [(quads[0], 224, 16)] + [(v, 224, 16) for v in q_got]]),
            )
            got_z = swap(zh, away)
            where = jnp.stack([mine, dev]).astype(jnp.int32)

            last = [(v, 144) for v in (keep1, got1, got_y1, *q1_got)] + [(out, tok)]
            last += [(v, v.shape[0]) for v in (home, e_keep, x_keep, home_x, away, got_z)]
            last += [(v, 64) for v in (keep2, got2, got_y2)] + [(v, v.shape[0]) for v in q_got]
            last += [(v, 48) for v in (keep3, got3, got_y3)]
            counts = [c for _, c in last]
            flat = [((per, w), F32) for w in (3 * D, D, D, 2 * D, D, FF)] + [((4 * per, D), F32)]
            done = run(
                functools.partial(finish, counts),
                [(where, SMEM)] + [(v, None) for v, _ in last],
                [((2, tok, D), BF), ((1, 1), F32), ((2, tok, D), F32), ((2, tok, D), F32)] + flat + [((3, per), F32)] * 2,
                name="finish",
            )
            return (done[0], done[1].reshape(()), *done[2:])

        def back_home(kept, recv):
            return jnp.where(mine == 0, jnp.stack([kept, recv]), jnp.stack([recv, kept]))

        def summed(g):
            return lax.psum_scatter(g, ("dp", "seq"), scatter_dimension=0, tiled=True).astype(F32)

        def rejoin(keep, send, n):
            g = jnp.stack([v[: 256 * n].reshape(2, 8, n, 16, D) for v in (keep, send)], 1)
            return g.reshape(G, n, 16, D)

        def full(g):
            return g.transpose(0, 2, 1, 3).reshape(G * 16, -1)

        small = lax.psum(send2[1024:].astype(F32), ("dp", "seq"))
        all1, all2, all3 = rejoin(keep1, send1, 9), rejoin(keep2, send2, 4), rejoin(keep3, send3, 3)
        g_norm = lax.dynamic_slice(small, (0, dev * per), (6, per))
        return (
            back_home(out[:tok], home[:tok]),
            jnp.sum(small[6]) / (jnp.sum(small[7]) * D),
            back_home(x_keep, home_x.astype(F32)),
            back_home(e_keep, home[tok:].astype(F32)),
            summed(full(all3)),
            summed(full(all2[:, 3:])),
            summed(full(all2[:, 2:3])),
            summed(full(all2[:, :2])),
            summed(full(all1[:, 8:])),
            summed(full(all1[:, :4])),
            summed(all1[:, 4:8].reshape(FF, D)),
            g_norm[:3],
            g_norm[3:],
        )

    return shards


def solution(mesh):
    rows, both = P("dp", "seq", None), P(("dp", "seq"), None)
    norm = P(None, ("dp", "seq"))
    return jax.shard_map(
        make_shards(mesh.shape["dp"], mesh.shape["seq"]),
        mesh=mesh,
        in_specs=(rows, rows, rows, P("dp", None), P("dp", None), P("dp", "seq")) + (both,) * 7 + (norm, norm),
        out_specs=(rows, P(), rows, rows) + (both,) * 7 + (norm, norm),
        check_vma=False,
    )
```

```python
import functools

import jax
import jax.numpy as jnp
from jax import lax
from jax.experimental import pallas as pl
from jax.experimental.pallas import tpu as pltpu
from jax.sharding import PartitionSpec as P

HEADS = 8
HEAD_DIM = 64
EPS = 1e-5
NEG = -1e30
SCALE = 0.125
D = 512
FF = 2048
HALF = 256
G = 32
BF = jnp.bfloat16
F32 = jnp.float32
MIB = 1 << 20

DEVICE, MINE, PLACE_1, PLACE_2, SLOT_A, SLOT_B, SLOT_F = 1, 2, 3, 19, 35, 67, 99

NN = (((1,), (0,)), ((), ()))
NT = (((1,), (1,)), ((), ()))
TN = (((0,), (0,)), ((), ()))


def dot(a, b, dims=NN):
    return lax.dot_general(a, b, dims, preferred_element_type=F32)


def whole(shape):
    return pl.BlockSpec(shape, lambda i: (0,) * len(shape))


SMEM = pl.BlockSpec(memory_space=pltpu.SMEM)
HBM = pl.BlockSpec(memory_space=pltpu.HBM)


def call(body, ins, outs, scratch=(), name=None, vmem=16):
    return pl.pallas_call(
        body,
        grid=(1,),
        in_specs=[whole(a.shape) if s is None else s for a, s in ins],
        out_specs=[whole(o[0]) if len(o) == 2 else pl.BlockSpec(memory_space=pltpu.HBM) for o in outs],
        out_shape=[jax.ShapeDtypeStruct(*o) if len(o) == 2 else pltpu.HBM(*o[:2]) for o in outs],
        scratch_shapes=list(scratch),
        compiler_params=pltpu.CompilerParams(vmem_limit_bytes=vmem * MIB),
        name=name,
        cost_estimate=pl.CostEstimate(flops=1000, bytes_accessed=1000, transcendentals=0),
    )(*[a for a, _ in ins])


def unpack(ids, table, parts, *targets):
    each = parts[0].shape[0]
    for p, part in enumerate(parts):
        for i in range(each):
            group = ids[table + each * p + i]
            for ref, first, count, height in targets:
                at = pl.multiple_of(group * height, 16)
                block = part[i, first : first + count]
                if height == 16:
                    ref[:, pl.ds(at, 16), :] = block
                else:
                    ref[pl.ds(at, height), :] = block.reshape(height, D)


def norm_rows(parts):
    return sum(jnp.sum(part[:, 5].astype(F32), axis=0) for part in parts)


def set_mask(mask, segs, key, query, position):
    length, rows = mask.shape
    columns = jnp.transpose(segs[...])
    same = columns[:, key : key + 1] == segs[query : query + 1, :rows]
    ahead = columns[:, position : position + 1] <= segs[position : position + 1, :rows]
    mask[...] = jnp.where(same & ahead, 0.0, NEG)


def put(ids, first, ref, chunks_each, j, value):
    value = value.astype(BF)
    each = value.shape[0] // 16
    for i in range(16):
        at = ids[first + i] * (16 * chunks_each) + 16 * j
        ref[pl.ds(pl.multiple_of(at, 16), each), :] = value[each * i : each * i + each]


def norm_forward(resid, gain, bias):
    centre = resid - jnp.mean(resid, axis=-1, keepdims=True)
    rstd = lax.rsqrt(jnp.mean(centre * centre, axis=-1, keepdims=True) + EPS)
    xhat = centre * rstd
    return xhat, rstd, xhat * gain + bias


def norm_back(g, xhat, rstd, gain):
    e = g * gain
    m1 = jnp.mean(e, axis=-1, keepdims=True)
    m2 = jnp.mean(e * xhat, axis=-1, keepdims=True)
    dr = (e - m1 - xhat * m2) * rstd
    return dr, jnp.sum(g * xhat, axis=0, keepdims=True), jnp.sum(g, axis=0, keepdims=True)


def head_half(x, e):
    lane = lax.broadcasted_iota(jnp.int32, x.shape, 1)
    return jnp.where((lane < HEAD_DIM) == (e == 0), x, jnp.zeros_like(x))


def attend(q_ref, kv_ref, mask_ref, p_ref, rl_ref, at_ref, p_out, sems):
    def leave(hp, slot):
        return pltpu.make_async_copy(p_ref.at[slot], p_out.at[pl.ds(2 * hp, 2)], sems.at[slot])

    def pair(hp, carry):
        slot = hp % 2

        @pl.when(hp >= 2)
        def _():
            leave(hp - 2, slot).wait()

        c0 = pl.multiple_of(hp * 128, 128)
        k2 = kv_ref[:, pl.ds(c0, 128)]
        v2 = kv_ref[:, pl.ds(pl.multiple_of(D + c0, 128), 128)]
        q2 = q_ref[:, pl.ds(c0, 128)]
        for e in range(2):
            s = dot(k2, head_half(q2, e), NT) + mask_ref[...]
            p = jnp.exp(s - jnp.max(s, axis=0, keepdims=True))
            rl = 1.0 / jnp.sum(p, axis=0, keepdims=True)
            pb = p.astype(BF)
            p_ref[slot, e] = pb
            rl_ref[pl.ds(2 * hp + e, 1), :] = rl
            o = dot(v2, pb, TN) * rl
            at_ref[pl.ds(pl.multiple_of((2 * hp + e) * HEAD_DIM, HEAD_DIM), HEAD_DIM), :] = o[
                e * HEAD_DIM : (e + 1) * HEAD_DIM
            ].astype(BF)
        leave(hp, slot).start()
        return carry

    pairs = HEADS // 2
    lax.fori_loop(0, pairs, pair, 0)
    for hp in (pairs - 2, pairs - 1):
        leave(hp, hp % 2).wait()


def keep_copy(held, out, sem):
    copy = pltpu.make_async_copy(held, out, sem)
    copy.start()
    return copy


def attend_back(first, q_ref, kv_ref, p_ref, rl_ref, do_ref, dkv_ref, dqt_ref):
    def pair(i, carry):
        hp = first // 2 + i
        c0 = pl.multiple_of(hp * 128, 128)
        o0 = pl.multiple_of(i * 128, 128)
        k2 = kv_ref[:, pl.ds(c0, 128)]
        v2 = kv_ref[:, pl.ds(pl.multiple_of(D + c0, 128), 128)]
        q2 = q_ref[:, pl.ds(c0, 128)]
        do2 = do_ref[:, pl.ds(c0, 128)]
        dk = dv = None
        for e in range(2):
            dom = head_half(do2, e)
            dp = dot(v2, dom, NT)
            p = p_ref[2 * hp + e].astype(F32) * rl_ref[pl.ds(2 * hp + e, 1), :]
            t = p * dp
            ds = (t - p * jnp.sum(t, axis=0, keepdims=True)).astype(BF)
            dk_e = dot(ds, head_half(q2, e))
            dv_e = dot(p.astype(BF), dom)
            dk = dk_e if dk is None else dk + dk_e
            dv = dv_e if dv is None else dv + dv_e
            dqt = dot(k2, ds, TN) * SCALE
            dqt_ref[pl.ds(pl.multiple_of((2 * i + e) * HEAD_DIM, HEAD_DIM), HEAD_DIM), :] = dqt[
                e * HEAD_DIM : (e + 1) * HEAD_DIM
            ]
        dkv_ref[:, pl.ds(o0, 128)] = dk.astype(BF)
        dkv_ref[:, pl.ds(pl.multiple_of(HALF + o0, 128), 128)] = dv.astype(BF)
        return carry

    lax.fori_loop(0, HEADS // 4, pair, 0)


def cols(ref, c, width):
    picks = [ref[:, pl.ds(pl.multiple_of((2 * y + c) * width, width), width)] for y in range(2)]
    return jnp.concatenate(picks, 1)


def rows_of(ref, c, width):
    picks = [ref[pl.ds(pl.multiple_of((2 * y + c) * width, width), width), :] for y in range(2)]
    return jnp.concatenate(picks, 0)


def sides(ids, keep, send):
    return ((send, 1 - ids[0]), (keep, ids[0]))


def pack(s_in, s_out, c_in, c_q, c_out, up, down, gain, bias, at, pa, pb, pf):
    for j in range(3):
        pa[j] = s_in[:, j * D : (j + 1) * D]
    pb[0] = s_out[...]
    for j in range(2):
        pb[1 + j] = c_in[:, j * D : (j + 1) * D]
    pb[3] = c_q[...]
    pb[4] = c_out[...]
    for j in range(4):
        pf[j] = up[:, j * D : (j + 1) * D]
        pf[4 + j] = down[16 * j : 16 * j + 16, :]
    rows = jnp.concatenate([gain[...], bias[...], jnp.zeros((10, 16), BF)], 0)
    column = lax.broadcasted_iota(jnp.int32, (16, D), 1)
    row = lax.broadcasted_iota(jnp.int32, (16, D), 0)
    pick = (column == at[0] * 16 + row).astype(BF)
    pb[5] = dot(rows, pick).astype(BF)


def join(full, near, far):
    half = near.shape[0]
    full[:half] = near[...]
    full[half:] = far[...]


def self_forward(rows, ids, near, far, wa0, wa1, wa2, wa3, segs,
                 xf_out, w_out, q_out, kv_out, p_out, rl_out, at,
                 mask, xf, w, q, kv, p, p_sems, sems, rl):
    join(xf, near, far)
    copies = [keep_copy(xf, xf_out, sems.at[0])]
    unpack(ids, SLOT_A, (wa0, wa1, wa2, wa3), (w, 0, 3, 16))
    copies.append(keep_copy(w, w_out, sems.at[1]))
    set_mask(mask, segs, 0, 0, 1)
    q[...] = (dot(xf[:rows], w[0]).astype(BF).astype(F32) * SCALE).astype(BF)
    kv[:, :D] = dot(xf[...], w[1]).astype(BF)
    kv[:, D:] = dot(xf[...], w[2]).astype(BF)
    copies += [keep_copy(q, q_out, sems.at[2]), keep_copy(kv, kv_out, sems.at[3])]
    attend(q, kv, mask, p, rl, at, p_out, p_sems)
    copies.append(keep_copy(rl, rl_out, sems.at[8]))
    for copy in copies:
        copy.wait()


def cross_forward(rows, ids, xf, near, far, at1, wb0, wb1, wb2, wb3, segs,
                  ef_out, w, norms_out, xh1, rs1_out, low1_out, q_out, kv_out, p_out, rl_out, at_out,
                  mask, ef, low1, q, kv, p, p_sems, sems, rl, norms, rs1, at):
    join(ef, near, far)
    copies = [keep_copy(ef, ef_out, sems.at[0])]
    unpack(ids, SLOT_B, (wb0, wb1, wb2, wb3), (w, 0, 5, 16))
    set_mask(mask, segs, 2, 0, 3)
    gb = norm_rows((wb0, wb1, wb2, wb3))
    norms[...] = gb
    copies.append(keep_copy(norms, norms_out, sems.at[6]))
    resid = xf[...].astype(F32) + dot(at1[...], w[0], TN)
    xhat, rstd, n1 = norm_forward(resid, gb[0:1], gb[3:4])
    xh1[...] = xhat
    rs1[...] = jnp.broadcast_to(rstd, rs1.shape)
    copies.append(keep_copy(rs1, rs1_out, sems.at[7]))
    low1[...] = n1.astype(BF)
    copies.append(keep_copy(low1, low1_out, sems.at[1]))
    q[...] = (dot(low1[...], w[3]).astype(BF).astype(F32) * SCALE).astype(BF)
    kv[:, :D] = dot(ef[...], w[1]).astype(BF)
    kv[:, D:] = dot(ef[...], w[2]).astype(BF)
    copies += [keep_copy(q, q_out, sems.at[2]), keep_copy(kv, kv_out, sems.at[3])]
    attend(q, kv, mask, p, rl, at, p_out, p_sems)
    copies += [keep_copy(rl, rl_out, sems.at[8]), keep_copy(at, at_out, sems.at[9])]
    for copy in copies:
        copy.wait()


def ffn_both(ids, xh1, at2_in, teacher, message, dec_valid, wb, norms_in, wf0, wf1, wf2, wf3,
             out, small, d_r2, d_mix, keep, send, act, hid, low2, wup, wdn, at2, norms, sems):
    brought = [keep_copy(at2_in, at2, sems.at[0]), keep_copy(norms_in, norms, sems.at[1])]
    unpack(ids, SLOT_F, (wf0, wf1, wf2, wf3), (wup, 0, 4, 16), (wdn, 4, 4, 64))
    tok = teacher.shape[1]
    marks = jnp.where(ids[MINE] == 0, dec_valid[0:1], dec_valid[1:2]).astype(F32)
    marks = jnp.concatenate([marks, message[2 * tok : 2 * tok + 1, :tok].astype(F32)], 1)
    valid = jnp.transpose(jnp.broadcast_to(marks, (8, 2 * tok)))[:, 0:1]
    teach = jnp.concatenate([teacher[ids[MINE]], message[tok : 2 * tok]], 0)
    for copy in brought:
        copy.wait()
    gb = norms[...]
    n1 = xh1[...] * gb[0:1] + gb[3:4]
    wco = wb[4]
    xh2, rs2, n2 = norm_forward(n1 + dot(at2[...], wco, TN), gb[1:2], gb[4:5])
    low2[...] = n2.astype(BF)
    for j in range(4):
        h = dot(low2[...], wup[j])
        hid[j] = h
        act[:, j * D : (j + 1) * D] = (h / (1.0 + jnp.exp(-h))).astype(BF)
    r3 = n2 + dot(act[...], wdn[...])
    xh3, rs3, final = norm_forward(r3, gb[2:3], gb[5:6])
    out[...] = final.astype(BF)
    err = (final - teach.astype(F32)) * valid
    small[...] = jnp.zeros_like(small)
    small[6:7] = jnp.sum(err * err, axis=0, keepdims=True)
    lane = lax.broadcasted_iota(jnp.int32, (1, D), 1)
    small[7:8] = jnp.where(lane == ids[DEVICE], jnp.sum(valid), 0.0)
    d_r3, dg, db = norm_back(err, xh3, rs3, gb[2:3])
    small[2:3] = dg
    small[5:6] = db
    dffn = d_r3.astype(BF)
    for ref, at in sides(ids, keep, send):
        put(ids, PLACE_1, ref, 9, 4, dot(cols(act, at, FF // 4), dffn, TN))
    dn2 = d_r3
    for j in range(4):
        da = dot(dffn, wdn[j * D : (j + 1) * D], NT)
        h = hid[j]
        sig = 1.0 / (1.0 + jnp.exp(-h))
        dh = (da * (sig * (1.0 + h * (1.0 - sig)))).astype(BF)
        for ref, at in sides(ids, keep, send):
            put(ids, PLACE_1, ref, 9, j, dot(cols(low2, at, 128), dh, TN))
        dn2 = dn2 + dot(dh, wup[j], NT)
    dr2, dg, db = norm_back(dn2, xh2, rs2, gb[1:2])
    small[1:2] = dg
    small[4:5] = db
    d_r2[...] = dr2
    dcross = dr2.astype(BF)
    for ref, at in sides(ids, keep, send):
        put(ids, PLACE_1, ref, 9, 8, dot(rows_of(at2, at, 128), dcross))
    d_mix[...] = dot(dcross, wco, NT).astype(BF)


def cross_back_a(q, kv, p, rl, d_mix, dkv, dq, dqt):
    attend_back(0, q, kv, p, rl, d_mix, dkv, dqt)
    dq[...] = jnp.transpose(dqt[...]).astype(BF)


def project(own, parts, dkv_a, dkv_b, wk, wv, extra=0.0):
    out = dot(dkv_a[:, :HALF], wk[:, :HALF], NT) + dot(dkv_b[:, :HALF], wk[:, HALF:], NT)
    out = out + dot(dkv_a[:, HALF:], wv[:, :HALF], NT) + dot(dkv_b[:, HALF:], wv[:, HALF:], NT)
    each = own.shape[0]
    own[...] = out[:each] + extra
    for i, part in enumerate(parts):
        part[...] = out[each * (i + 1) : each * (i + 2)].astype(BF)


def cross_back_b(n_parts, ids, ef, q, kv, p, rl, d_mix, dkv_a, dq_a, wb, norms, d_r2, low1, xh1,
                 rs1, at1, small, own, *rest):
    parts, (d_mix1, d_r1, keep, send, dkv, dqt) = rest[:n_parts], rest[n_parts:]
    attend_back(4, q, kv, p, rl, d_mix, dkv, dqt)
    project(own, parts, dkv_a, dkv, wb[1], wb[2])
    dq = jnp.concatenate([dq_a[...], jnp.transpose(dqt[...]).astype(BF)], 1)
    gb = norms[...]
    dn1 = d_r2[...] + dot(dq, wb[3], NT)
    dr1, dg, db = norm_back(dn1, xh1[...], rs1[:, 0:1], gb[0:1])
    row = lax.broadcasted_iota(jnp.int32, (16, D), 0)
    sums = jnp.where(row == 0, dg, jnp.where(row == 3, db, small[...]))
    send[1024:1040] = sums.astype(BF)
    d_r1[...] = dr1
    dself = dr1.astype(BF)
    for ref, at in sides(ids, keep, send):
        lhs = cols(ef, at, 128)
        for j in range(2):
            span = slice(j * HALF, (j + 1) * HALF)
            g = jnp.concatenate([dot(lhs, dkv_a[:, span], TN), dot(lhs, dkv[:, span], TN)], 1)
            put(ids, PLACE_2, ref, 4, j, g)
        put(ids, PLACE_2, ref, 4, 2, dot(cols(low1, at, 128), dq, TN))
        put(ids, PLACE_2, ref, 4, 3, dot(rows_of(at1, at, 128), dself))
    d_mix1[...] = dot(dself, wb[0], NT).astype(BF)


def self_back_b(n_parts, rows, ids, xf, q, kv, p, rl, d_mix, dkv_a, dq_a, wa, d_r1, own, *rest):
    parts, (keep, send, dkv, dqt) = rest[:n_parts], rest[n_parts:]
    attend_back(4, q, kv, p, rl, d_mix, dkv, dqt)
    dq = jnp.concatenate([dq_a[...], jnp.transpose(dqt[...]).astype(BF)], 1)
    through_q = d_r1[...] + dot(dq, wa[0], NT)
    project(own, parts, dkv_a, dkv, wa[1], wa[2], through_q)
    for ref, at in sides(ids, keep, send):
        lhs = cols(xf, at, 128)
        put(ids, PLACE_2, ref, 3, 0, dot(lhs[:rows], dq, TN))
        for j in range(2):
            span = slice(j * HALF, (j + 1) * HALF)
            g = jnp.concatenate([dot(lhs, dkv_a[:, span], TN), dot(lhs, dkv[:, span], TN)], 1)
            put(ids, PLACE_2, ref, 3, 1 + j, g)


def tree_sum(terms):
    while len(terms) > 1:
        terms = [a + b for a, b in zip(terms[::2], terms[1::2])] + terms[len(terms) & ~1 :]
    return terms[0]


ANY = pl.BlockSpec(memory_space=pl.ANY)


def fetch(ref, start, count, to, sem):
    copy = pltpu.make_async_copy(ref.at[pl.ds(start, count)], to, sem)
    copy.start()
    return copy


def mix(name, *outs):
    arrays, terms, plan = [], [], []
    for dtype, segments in outs:
        plan.append([])
        for segment in segments:
            used = []
            for array, start, count in segment:
                at = [i for i, v in enumerate(arrays) if v is array]
                if not at:
                    arrays.append(array)
                used.append(len(terms))
                terms.append((at[0] if at else len(arrays) - 1, start, count, array.dtype))
            plan[-1].append(used)

    def body(*refs):
        for out, segments in zip(refs[len(arrays) :], plan):
            first = 0
            for used in segments:
                count = terms[used[0]][2]
                parts = [refs[k][start : start + count].astype(F32) for k, start, _, _ in (terms[i] for i in used)]
                out[first : first + count] = tree_sum(parts).astype(out.dtype)
                first += count

    shapes = [((sum(t[0][2] for t in segments), D), dtype) for dtype, segments in outs]
    return call(body, [(v, None) for v in arrays], shapes, name=name)


def finish(counts, *refs):
    where, refs = refs[0], refs[1:]
    sources, results = refs[: len(counts)], refs[len(counts) :]
    refs = [ref.at[:count] for ref, count in zip(sources, counts)]
    one, (out, home, e_keep, x_keep, home_x, z_own, z_got, *refs) = refs[:6], refs[6:]
    two, three = refs[:6], refs[6:]
    outputs, loss, g_x, g_e, g_in, g_so, g_cq, g_cin, g_co, g_up, g_down, g_gain, g_bias = results
    mine = where[0]
    tok = e_keep.shape[0]
    outputs[mine] = out[...]
    outputs[1 - mine] = home[:tok]
    g_e[mine] = e_keep[...]
    g_e[1 - mine] = home[tok:].astype(F32)
    g_x[mine] = x_keep[...]
    g_x[1 - mine] = home_x[:tok].astype(F32)
    t1 = tree_sum([r[...].astype(F32) for r in one] + [home_x[tok:].astype(F32)])
    for j in range(4):
        g_up[:, j * D : (j + 1) * D] = t1[16 * j : 16 * j + 16]
    g_down[...] = t1[64:128]
    g_co[...] = t1[128:144]
    t2 = tree_sum([r[...].astype(F32) for r in two[:3]] + [r[:64].astype(F32) for r in two[3:]] + [z_got[:64].astype(F32)])
    for j in range(2):
        g_cin[:, j * D : (j + 1) * D] = t2[16 * j : 16 * j + 16]
    g_cq[...] = t2[32:48]
    g_so[...] = t2[48:64]
    t3 = tree_sum([r[...].astype(F32) for r in three] + [r[128:176].astype(F32) for r in two[3:]] + [z_got[64:112].astype(F32)])
    for j in range(3):
        g_in[:, j * D : (j + 1) * D] = t3[16 * j : 16 * j + 16]
    small = z_own[112:128].astype(F32) + z_got[112:128].astype(F32)
    total = jnp.sum(small[6:7], axis=1, keepdims=True)
    loss[...] = total / (jnp.sum(small[7:8], axis=1, keepdims=True) * D)
    column = lax.broadcasted_iota(jnp.int32, (16, D), 1)
    row = lax.broadcasted_iota(jnp.int32, (16, D), 0)
    pick = (column == where[1] * 16 + row).astype(F32)
    own = lax.dot_general(small[:8], pick, NT, precision=lax.Precision.HIGHEST, preferred_element_type=F32)
    g_gain[...] = own[0:3]
    g_bias[...] = own[3:6]


def tie(*values):
    return lax.optimization_barrier(values)


def make_shards(nd, ns):
    n_dev = nd * ns
    half = ns // 2
    per = G * 16 // n_dev
    fast = nd == 4 and ns == 8
    run = functools.partial(call, vmem=20 if fast else 48)

    core, y, x, zl, zh = ("dp", 1), ("dp", 2), ("seq", 1), ("seq", 2), ("seq", 4)

    def shards(inputs, encoder, teacher, dec_seg, enc_seg, dec_valid, self_in, self_out,
               cross_query, cross_in, cross_out, ffn_up, ffn_down, norm_gain, norm_bias):
        tok = inputs.shape[1]
        rows = 2 * tok
        length = dec_seg.shape[1]
        dp_at, seq_at = lax.axis_index("dp"), lax.axis_index("seq")
        dev = dp_at * ns + seq_at
        mine = seq_at // half

        def flip(bit, arrays):
            axis, b = bit
            size = nd if axis == "dp" else ns
            flat = [v.reshape(-1, D) for v in arrays]
            got = lax.ppermute(
                flat[0] if len(flat) == 1 else jnp.concatenate(flat, 0),
                axis, [(i, i ^ b) for i in range(size)],
            )
            out, start = [], 0
            for v, f in zip(arrays, flat):
                out.append(lax.slice_in_dim(got, start, start + f.shape[0]).reshape(v.shape))
                start += f.shape[0]
            return out

        def swap(bit, array):
            return flip(bit, [array])[0]

        def of(v, i):
            return lax.dynamic_index_in_dim(v, i, 0, keepdims=False)

        def other(v):
            return of(v, 1 - mine)

        def append(v, got):
            return jnp.concatenate([v, got], 0)

        valid_away = jnp.pad(other(dec_valid).astype(BF)[None], ((0, 15), (0, D - tok)))

        row_bits = (2, 1) if fast else tuple(1 << b for b in range(half.bit_length() - 1))
        slots = jnp.arange(half, dtype=jnp.int32)

        def pieces(bits):
            masks = sum((((slots >> i) & 1) * b) for i, b in enumerate(bits))[:, None]
            return (seq_at ^ masks ^ jnp.array([[0, half]], jnp.int32)).reshape(-1)

        pos = (pieces(row_bits)[:, None] * tok + jnp.arange(tok, dtype=jnp.int32)[None]).reshape(-1)
        dec_k = of(dec_seg, mine).reshape(ns, tok)[pieces(row_bits)].reshape(-1)
        enc_k = of(enc_seg, mine).reshape(ns, tok)[pieces(row_bits)].reshape(-1)
        segs = jnp.stack([dec_k, pos, enc_k] + [jnp.zeros_like(pos)] * 5).astype(F32)

        def spread(v, bits):
            return sum((((v & b) != 0).astype(jnp.int32) << i) for i, b in enumerate(bits))

        if fast:
            i16 = jnp.arange(16, dtype=jnp.int32)
            g32 = jnp.arange(32, dtype=jnp.int32)
            dev16 = (dp_at >> 1) * 8 + seq_at

            def came_from(bits):
                return dev ^ sum((((g32 >> i) & 1) * b for i, b in enumerate(bits)))

            ids = jnp.concatenate(
                [
                    jnp.stack([dp_at & 1, dev, mine]).astype(jnp.int32),
                    spread(i16 ^ dev16, (4, 2, 1, 8)),
                    spread(i16 ^ dev16, (4, 2, 1, 8)),
                    came_from((4, 2, 1, 16, 8)),
                    came_from((4, 16, 1, 2, 8)),
                    came_from((4, 2, 1, 16, 8)),
                ]
            )
        else:
            i16, g32 = jnp.arange(16, dtype=jnp.int32), jnp.arange(32, dtype=jnp.int32)
            ids = jnp.concatenate([jnp.stack([0 * dev, dev, mine]).astype(jnp.int32), i16, i16, g32, g32, g32])

        if fast:
            mats = [self_in, self_out, cross_in, cross_query, cross_out, ffn_up, ffn_down, norm_gain, norm_bias]
            wa, wb, wf = run(
                pack,
                [(w, None) for w in mats] + [(dev.astype(jnp.int32)[None], SMEM)],
                [((3, 16, D), BF), ((6, 16, D), BF), ((8, 16, D), BF)],
                name="pack",
                vmem=56,
            )
            wa, wb, wf = wa[None], wb[None], wf[None]
            got_x, got_a = flip(zh, [other(inputs), wa])
            got_x, got_a, wb, wf, segs, ids = tie(got_x, got_a, wb, wf, segs, ids)
            got_b, got_f = flip(zh, [wb, wf])
            xf, wa = jnp.stack([of(inputs, mine), got_x])[None], append(wa, got_a)
            got_x, got_a = flip(zl, [xf, wa])
            got_x, got_a, got_b, got_f, away_e = tie(got_x, got_a, got_b, got_f, other(encoder))
            xf, wa = append(xf, got_x), append(wa, got_a)
            wb, wf = append(wb, got_b), append(wf, got_f)
            got_x, got_a = flip(x, [xf, wa])
            message = swap(zh, jnp.concatenate([away_e, other(teacher), valid_away], 0))
            got_e = message[:tok]
            got_b, got_f = swap(y, wb), swap(zl, wf)
            ef = jnp.stack([of(encoder, mine), got_e])[None]
            got_x, got_a, got_b, got_f, ef = tie(got_x, got_a, got_b, got_f, ef)
            wa, wb, wf = append(wa, got_a), append(wb, got_b), append(wf, got_f)
            got_a, got_b, got_e, got_f = swap(y, wa), swap(x, wb), swap(zl, ef), swap(x, wf)
            wa_far = swap(core, wa)
            got_a, got_b, got_e, wa_far = tie(got_a, got_b, got_e, wa_far)
            wa = [wa, got_a, wa_far, swap(core, got_a)]
            wb, ef = append(wb, got_b), append(ef, got_e)
            got_b, got_e = swap(zl, wb), swap(x, ef)
            got_f, wa[3] = tie(got_f, wa[3])
            wf = append(wf, got_f)
            got_f = swap(y, wf)
            wb_far, wf_far = swap(core, wb), swap(core, wf)
        else:
            got_x = swap(("seq", half), other(inputs))
            message = swap(("seq", half), jnp.concatenate([other(encoder), other(teacher), valid_away], 0))
            got_e = message[:tok]
            xf, ef = jnp.stack([of(inputs, mine), got_x])[None], jnp.stack([of(encoder, mine), got_e])[None]
            for bit in row_bits:
                got_x, got_e = flip(("seq", bit), [xf, ef])
                if bit != row_bits[-1]:
                    xf, ef = append(xf, got_x), append(ef, got_e)

            def gathered(w):
                return lax.all_gather(w, ("dp", "seq"), axis=0, tiled=True)

            def grouped(w):
                return w.reshape(G, 16, w.shape[1] // D, D).transpose(0, 2, 1, 3)

            wa = grouped(gathered(self_in))
            mine_only = lax.dynamic_update_slice(
                jnp.zeros((16, D), BF), jnp.concatenate([norm_gain, norm_bias], 0), (0, dev * per)
            )
            all_norms = lax.psum(mine_only.astype(F32), ("dp", "seq")).astype(BF)
            all_norms = jnp.pad(all_norms[None], ((0, G - 1), (0, 0), (0, 0)))[:, None]
            rest = [grouped(gathered(w)) for w in (self_out, cross_in, cross_query, cross_out)]
            down = gathered(ffn_down).reshape(G, 4, 16, D)
            wb = jnp.concatenate(rest + [all_norms], 1)
            wf = jnp.concatenate([grouped(gathered(ffn_up)), down], 1)
            wa, wb, wf = [[w[8 * i : 8 * i + 8] for i in range(4)] for w in (wa, wb, wf)]
        x_near, x_far = xf.reshape(-1, D), got_x.reshape(-1, D)

        sm = (ids, SMEM)
        p_shape = (HEADS, length, rows)
        def held(*shapes):
            return (
                [pltpu.VMEM((length, rows), F32)]
                + [pltpu.VMEM(v, BF) for v in shapes]
                + [pltpu.VMEM((2, 2, length, rows), BF), pltpu.SemaphoreType.DMA((2,)), pltpu.SemaphoreType.DMA((10,))]
                + [pltpu.VMEM((HEADS, rows), F32)]
            )

        all_rows, own_rows, both_kv = (length, D), (rows, D), (length, 2 * D)
        own_x = x_near[:rows]
        xf, wa, q1, kv1, p1, rl1, at1 = run(
            functools.partial(self_forward, rows),
            [sm, (x_near, None), (x_far, None)] + [(v, None) for v in wa] + [(segs, None)],
            [(all_rows, BF, True), ((3, D, D), BF, True), (own_rows, BF, True), (both_kv, BF, True),
             (p_shape, BF, True), ((HEADS, rows), F32, True), ((D, rows), BF)],
            scratch=held(all_rows, (3, D, D), own_rows, both_kv),
            name="self_forward",
        )
        if fast:
            got_b, got_e, wb_far, at1 = tie(got_b, got_e, wb_far, at1)
            wb = [wb, got_b, wb_far, swap(core, got_b)]
        e_near, e_far = ef.reshape(-1, D), got_e.reshape(-1, D)
        ef, wb, norms, xh1, rs1, low1, q2, kv2, p2, rl2, at2 = run(
            functools.partial(cross_forward, rows),
            [sm, (own_x, None), (e_near, None), (e_far, None), (at1, None)] + [(v, None) for v in wb] + [(segs, None)],
            [(all_rows, BF, True), ((5, D, D), BF), ((16, D), F32, True), (own_rows, F32), ((rows, 128), F32, True),
             (own_rows, BF, True), (own_rows, BF, True), (both_kv, BF, True), (p_shape, BF, True),
             ((HEADS, rows), F32, True), ((D, rows), BF, True)],
            scratch=held(all_rows, own_rows, own_rows, both_kv)
            + [pltpu.VMEM((16, D), F32), pltpu.VMEM((rows, 128), F32), pltpu.VMEM((D, rows), BF)],
            name="cross_forward",
        )
        if fast:
            got_f, wf_far, at2 = tie(got_f, wf_far, at2)
            wf = [wf, got_f, wf_far, swap(core, got_f)]
        out, small, d_r2, d_mix2, keep1, send1 = run(
            ffn_both,
            [sm, (xh1, None), (at2, HBM), (teacher, None), (message, None), (dec_valid, None), (wb, None), (norms, HBM)]
            + [(v, None) for v in wf],
            [((rows, D), BF), ((16, D), F32), ((rows, D), F32), ((rows, D), BF)] + [((2304, D), BF)] * 2,
            scratch=[pltpu.VMEM((rows, FF), BF), pltpu.VMEM((4, rows, D), F32), pltpu.VMEM((rows, D), BF),
                     pltpu.VMEM((4, D, D), BF), pltpu.VMEM((FF, D), BF), pltpu.VMEM((D, rows), BF),
                     pltpu.VMEM((16, D), F32), pltpu.SemaphoreType.DMA((2,))],
            name="ffn_both",
        )

        kv_half = [((length, D), BF), ((rows, HALF), BF)]
        d_rows = [pltpu.VMEM((HALF, rows), F32)]
        both_scratch = [pltpu.VMEM((length, D), BF)] + d_rows
        row_parts = [((rows, D), F32)] + [((rows, D), BF)] * (half - 1)
        partners = [sum(((i >> k) & 1) * b for k, b in enumerate(row_bits)) for i in range(1, half)]

        if fast:
            got1 = swap(core, send1)
        dkv2, dq2 = run(
            cross_back_a,
            [(q2, None), (kv2, None), (p2, None), (rl2, None), (d_mix2, None)],
            kv_half,
            scratch=d_rows,
            name="cross_back_a",
        )
        if fast:
            got1, d_mix2, dkv2 = tie(got1, d_mix2, dkv2)
            got_y1 = swap(y, (keep1[1152:].astype(F32) + got1[1152:].astype(F32)).astype(BF))
        e_own, *rest = run(
            functools.partial(cross_back_b, half - 1),
            [sm, (ef, None), (q2, None), (kv2, None), (p2, None), (rl2, None), (d_mix2, None),
             (dkv2, None), (dq2, None), (wb, None), (norms, None), (d_r2, None), (low1, None),
             (xh1, None), (rs1, None), (at1, None), (small, None)],
            row_parts + [((rows, D), BF), ((rows, D), F32), ((1024, D), BF), ((1040, D), BF)],
            scratch=both_scratch,
            name="cross_back_b",
        )
        e_parts, (d_mix1, d_r1, keep2, send2) = rest[: half - 1], rest[half - 1 :]
        if fast:
            got2 = swap(core, send2)
        e_got = [swap(("seq", m), part) for m, part in zip(partners, e_parts)]
        dkv1, dq1 = run(
            cross_back_a,
            [(q1, None), (kv1, None), (p1, None), (rl1, None), (d_mix1, None)],
            kv_half,
            scratch=d_rows,
            name="self_back_a",
        )
        if fast:
            got2, d_mix1, dkv1 = tie(got2, d_mix1, dkv1)
        x_own, *rest = run(
            functools.partial(self_back_b, half - 1, rows),
            [sm, (xf, None), (q1, None), (kv1, None), (p1, None), (rl1, None), (d_mix1, None),
             (dkv1, None), (dq1, None), (wa, None), (d_r1, None)],
            row_parts + [((768, D), BF)] * 2,
            scratch=both_scratch,
            name="self_back_b",
        )
        x_parts, (keep3, send3) = rest[: half - 1], rest[half - 1 :]

        if fast:
            n = half - 1
            got_y1, send3, *both_parts = tie(got_y1, send3, *x_parts, *e_got)
            x_parts, e_got = both_parts[:n], both_parts[n:]
            (away,) = mix(
                "sum_y2",
                (BF, [[(keep2, 512, 512), (got2, 512, 512)], [(send2, 1024, 16), (got2, 1024, 16)]]),
            )
            got_y2 = swap(y, away)
            small_y2 = (away, 512, 16)
            one = lambda start, count: [(v, start, count) for v in (keep1, got1, got_y1)]
            quads1 = mix(
                "sum_quads1", *[(BF, [one(288 * i, 288), [(x_parts[i - 1], 0, rows)]]) for i in (1, 2, 3)]
            )
            q1_got = [swap(("seq", m), part) for m, part in zip(partners, quads1)]
        else:
            x_got = [swap(("seq", m), part) for m, part in zip(partners, x_parts)]
        if fast:
            got3 = swap(core, send3)
        e_terms = lambda start: [(v, start, tok) for v in (e_own, *e_got)]
        e_keep, away = mix("sum_e", (F32, [e_terms(0)]), (BF, [[(out, tok, tok)], e_terms(tok)]))
        home = swap(("seq", half), away)
        if fast:
            (away,) = mix("sum_y3", (BF, [[(keep3, 384, 384), (got3, 384, 384)]]))
            got_y3 = swap(y, away)
            got_y3, home = tie(got_y3, home)
        if fast:
            x_terms = lambda start: [(x_own, start, tok)] + [(v, 288 + start, tok) for v in q1_got]
            more = [one(144, 144) + [(v, 144, 144) for v in q1_got]]
        else:
            x_terms = lambda start: [(v, start, tok) for v in (x_own, *x_got)]
            more = []
        x_keep, away = mix("sum_x", (F32, [x_terms(0)]), (BF, [x_terms(tok), *more]))
        home_x = swap(("seq", half), away)

        if fast:
            def two(start, count):
                return [(v, start, count) for v in (keep2, got2, got_y2)]

            def three(start, count):
                return [(v, start, count) for v in (keep3, got3, got_y3)]

            quads = mix(
                "sum_quads",
                *[(BF, [two(128 * i, 128), three(96 * i, 96), [small_y2, (got_y2, 512, 16)]]) for i in (1, 2, 3)],
            )
            q_got = [swap(("seq", m), part) for m, part in zip(partners, quads)]
            (away,) = mix(
                "sum_zh",
                (BF, [two(64, 64) + [(v, 64, 64) for v in q_got], three(48, 48) + [(v, 176, 48) for v in q_got],
                      [(quads[0], 224, 16)] + [(v, 224, 16) for v in q_got]]),
            )
            got_z = swap(zh, away)
            where = jnp.stack([mine, dev]).astype(jnp.int32)

            last = [(v, 144) for v in (keep1, got1, got_y1, *q1_got)] + [(out, tok)]
            last += [(v, v.shape[0]) for v in (home, e_keep, x_keep, home_x, away, got_z)]
            last += [(v, 64) for v in (keep2, got2, got_y2)] + [(v, v.shape[0]) for v in q_got]
            last += [(v, 48) for v in (keep3, got3, got_y3)]
            counts = [c for _, c in last]
            flat = [((per, w), F32) for w in (3 * D, D, D, 2 * D, D, FF)] + [((4 * per, D), F32)]
            done = run(
                functools.partial(finish, counts),
                [(where, SMEM)] + [(v, None) for v, _ in last],
                [((2, tok, D), BF), ((1, 1), F32), ((2, tok, D), F32), ((2, tok, D), F32)] + flat + [((3, per), F32)] * 2,
                name="finish",
            )
            return (done[0], done[1].reshape(()), *done[2:])

        def back_home(kept, recv):
            return jnp.where(mine == 0, jnp.stack([kept, recv]), jnp.stack([recv, kept]))

        def summed(g):
            return lax.psum_scatter(g, ("dp", "seq"), scatter_dimension=0, tiled=True).astype(F32)

        def rejoin(keep, send, n):
            g = jnp.stack([v[: 256 * n].reshape(2, 8, n, 16, D) for v in (keep, send)], 1)
            return g.reshape(G, n, 16, D)

        def full(g):
            return g.transpose(0, 2, 1, 3).reshape(G * 16, -1)

        small = lax.psum(send2[1024:].astype(F32), ("dp", "seq"))
        all1, all2, all3 = rejoin(keep1, send1, 9), rejoin(keep2, send2, 4), rejoin(keep3, send3, 3)
        g_norm = lax.dynamic_slice(small, (0, dev * per), (6, per))
        return (
            back_home(out[:tok], home[:tok]),
            jnp.sum(small[6]) / (jnp.sum(small[7]) * D),
            back_home(x_keep, home_x.astype(F32)),
            back_home(e_keep, home[tok:].astype(F32)),
            summed(full(all3)),
            summed(full(all2[:, 3:])),
            summed(full(all2[:, 2:3])),
            summed(full(all2[:, :2])),
            summed(full(all1[:, 8:])),
            summed(full(all1[:, :4])),
            summed(all1[:, 4:8].reshape(FF, D)),
            g_norm[:3],
            g_norm[3:],
        )

    return shards


def solution(mesh):
    rows, both = P("dp", "seq", None), P(("dp", "seq"), None)
    norm = P(None, ("dp", "seq"))
    return jax.shard_map(
        make_shards(mesh.shape["dp"], mesh.shape["seq"]),
        mesh=mesh,
        in_specs=(rows, rows, rows, P("dp", None), P("dp", None), P("dp", "seq")) + (both,) * 7 + (norm, norm),
        out_specs=(rows, P(), rows, rows) + (both,) * 7 + (norm, norm),
        check_vma=False,
    )
```

```python
import functools

import jax
import jax.numpy as jnp
from jax import lax
from jax.experimental import pallas as pl
from jax.experimental.pallas import tpu as pltpu
from jax.sharding import PartitionSpec as P

HEADS = 8
HEAD_DIM = 64
EPS = 1e-5
NEG = -1e30
SCALE = 0.125
D = 512
FF = 2048
HALF = 256
G = 32
BF = jnp.bfloat16
F32 = jnp.float32
MIB = 1 << 20

DEVICE, MINE, PLACE_1, PLACE_2, SLOT_A, SLOT_B, SLOT_F = 1, 2, 3, 19, 35, 67, 99

NN = (((1,), (0,)), ((), ()))
NT = (((1,), (1,)), ((), ()))
TN = (((0,), (0,)), ((), ()))


def dot(a, b, dims=NN):
    return lax.dot_general(a, b, dims, preferred_element_type=F32)


def whole(shape):
    return pl.BlockSpec(shape, lambda i: (0,) * len(shape))


SMEM = pl.BlockSpec(memory_space=pltpu.SMEM)
HBM = pl.BlockSpec(memory_space=pltpu.HBM)


def call(body, ins, outs, scratch=(), name=None, vmem=16):
    return pl.pallas_call(
        body,
        grid=(1,),
        in_specs=[whole(a.shape) if s is None else s for a, s in ins],
        out_specs=[whole(o[0]) if len(o) == 2 else pl.BlockSpec(memory_space=pltpu.HBM) for o in outs],
        out_shape=[jax.ShapeDtypeStruct(*o) if len(o) == 2 else pltpu.HBM(*o[:2]) for o in outs],
        scratch_shapes=list(scratch),
        compiler_params=pltpu.CompilerParams(vmem_limit_bytes=vmem * MIB),
        name=name,
        cost_estimate=pl.CostEstimate(flops=1000, bytes_accessed=1000, transcendentals=0),
    )(*[a for a, _ in ins])


def unpack(ids, table, parts, *targets):
    each = parts[0].shape[0]
    for p, part in enumerate(parts):
        for i in range(each):
            group = ids[table + each * p + i]
            for ref, first, count, height in targets:
                at = pl.multiple_of(group * height, 16)
                block = part[i, first : first + count]
                if height == 16:
                    ref[:, pl.ds(at, 16), :] = block
                else:
                    ref[pl.ds(at, height), :] = block.reshape(height, D)


def norm_rows(parts):
    return sum(jnp.sum(part[:, 5].astype(F32), axis=0) for part in parts)


def set_mask(mask, segs, key, query, position):
    length, rows = mask.shape
    columns = jnp.transpose(segs[...])
    same = columns[:, key : key + 1] == segs[query : query + 1, :rows]
    ahead = columns[:, position : position + 1] <= segs[position : position + 1, :rows]
    mask[...] = jnp.where(same & ahead, 0.0, NEG)


def put(ids, first, ref, chunks_each, j, value):
    value = value.astype(BF)
    each = value.shape[0] // 16
    for i in range(16):
        at = ids[first + i] * (16 * chunks_each) + 16 * j
        ref[pl.ds(pl.multiple_of(at, 16), each), :] = value[each * i : each * i + each]


def norm_forward(resid, gain, bias):
    centre = resid - jnp.mean(resid, axis=-1, keepdims=True)
    rstd = lax.rsqrt(jnp.mean(centre * centre, axis=-1, keepdims=True) + EPS)
    xhat = centre * rstd
    return xhat, rstd, xhat * gain + bias


def norm_back(g, xhat, rstd, gain):
    e = g * gain
    m1 = jnp.mean(e, axis=-1, keepdims=True)
    m2 = jnp.mean(e * xhat, axis=-1, keepdims=True)
    dr = (e - m1 - xhat * m2) * rstd
    return dr, jnp.sum(g * xhat, axis=0, keepdims=True), jnp.sum(g, axis=0, keepdims=True)


def head_half(x, e):
    lane = lax.broadcasted_iota(jnp.int32, x.shape, 1)
    return jnp.where((lane < HEAD_DIM) == (e == 0), x, jnp.zeros_like(x))


def two_heads(x):
    return jnp.concatenate([head_half(x, 0), head_half(x, 1)], 0)


def attend(q_ref, kv_ref, mask_ref, p_ref, rl_ref, at_ref, p_out, sems):
    rows = mask_ref.shape[1]

    def leave(hp, slot):
        return pltpu.make_async_copy(p_ref.at[slot], p_out.at[pl.ds(2 * hp, 2)], sems.at[slot])

    def pair(hp, carry):
        slot = hp % 2

        @pl.when(hp >= 2)
        def _():
            leave(hp - 2, slot).wait()

        c0 = pl.multiple_of(hp * 128, 128)
        k2 = kv_ref[:, pl.ds(c0, 128)]
        v2 = kv_ref[:, pl.ds(pl.multiple_of(D + c0, 128), 128)]
        q2 = q_ref[:, pl.ds(c0, 128)]
        both = dot(k2, two_heads(q2), NT)
        probs, scales = [], []
        for e in range(2):
            s = both[:, e * rows : (e + 1) * rows] + mask_ref[...]
            p = jnp.exp(s - jnp.max(s, axis=0, keepdims=True))
            rl = 1.0 / jnp.sum(p, axis=0, keepdims=True)
            probs.append(p.astype(BF))
            p_ref[slot, e] = probs[e]
            rl_ref[pl.ds(2 * hp + e, 1), :] = rl
            scales.append(rl)
        o = dot(v2, jnp.concatenate(probs, 1), TN)
        for e in range(2):
            out = o[e * HEAD_DIM : (e + 1) * HEAD_DIM, e * rows : (e + 1) * rows] * scales[e]
            at_ref[pl.ds(pl.multiple_of((2 * hp + e) * HEAD_DIM, HEAD_DIM), HEAD_DIM), :] = out.astype(BF)
        leave(hp, slot).start()
        return carry

    pairs = HEADS // 2
    lax.fori_loop(0, pairs, pair, 0)
    for hp in (pairs - 2, pairs - 1):
        leave(hp, hp % 2).wait()


def keep_copy(held, out, sem):
    copy = pltpu.make_async_copy(held, out, sem)
    copy.start()
    return copy


def attend_back(first, q_ref, kv_ref, p_ref, rl_ref, do_ref, dkv_ref, dqt_ref):
    rows = q_ref.shape[0]

    def pair(i, carry):
        hp = first // 2 + i
        c0 = pl.multiple_of(hp * 128, 128)
        o0 = pl.multiple_of(i * 128, 128)
        k2 = kv_ref[:, pl.ds(c0, 128)]
        v2 = kv_ref[:, pl.ds(pl.multiple_of(D + c0, 128), 128)]
        q2 = q_ref[:, pl.ds(c0, 128)]
        do2 = do_ref[:, pl.ds(c0, 128)]
        dobd = two_heads(do2)
        both = dot(v2, dobd, NT)
        probs, grads = [], []
        for e in range(2):
            p = p_ref[2 * hp + e].astype(F32) * rl_ref[pl.ds(2 * hp + e, 1), :]
            t = p * both[:, e * rows : (e + 1) * rows]
            grads.append((t - p * jnp.sum(t, axis=0, keepdims=True)).astype(BF))
            probs.append(p.astype(BF))
        ds = jnp.concatenate(grads, 1)
        dk = dot(ds, two_heads(q2))
        dv = dot(jnp.concatenate(probs, 1), dobd)
        dqt = dot(k2, ds, TN) * SCALE
        for e in range(2):
            dqt_ref[pl.ds(pl.multiple_of((2 * i + e) * HEAD_DIM, HEAD_DIM), HEAD_DIM), :] = dqt[
                e * HEAD_DIM : (e + 1) * HEAD_DIM, e * rows : (e + 1) * rows
            ]
        dkv_ref[:, pl.ds(o0, 128)] = dk.astype(BF)
        dkv_ref[:, pl.ds(pl.multiple_of(HALF + o0, 128), 128)] = dv.astype(BF)
        return carry

    lax.fori_loop(0, HEADS // 4, pair, 0, unroll=True)


def cols(ref, c, width):
    picks = [ref[:, pl.ds(pl.multiple_of((2 * y + c) * width, width), width)] for y in range(2)]
    return jnp.concatenate(picks, 1)


def rows_of(ref, c, width):
    picks = [ref[pl.ds(pl.multiple_of((2 * y + c) * width, width), width), :] for y in range(2)]
    return jnp.concatenate(picks, 0)


def sides(ids, keep, send):
    return ((send, 1 - ids[0]), (keep, ids[0]))


def pack(s_in, s_out, c_in, c_q, c_out, up, down, gain, bias, at, pa, pb, pf):
    for j in range(3):
        pa[j] = s_in[:, j * D : (j + 1) * D]
    pb[0] = s_out[...]
    for j in range(2):
        pb[1 + j] = c_in[:, j * D : (j + 1) * D]
    pb[3] = c_q[...]
    pb[4] = c_out[...]
    for j in range(4):
        pf[j] = up[:, j * D : (j + 1) * D]
        pf[4 + j] = down[16 * j : 16 * j + 16, :]
    rows = jnp.concatenate([gain[...], bias[...], jnp.zeros((10, 16), BF)], 0)
    column = lax.broadcasted_iota(jnp.int32, (16, D), 1)
    row = lax.broadcasted_iota(jnp.int32, (16, D), 0)
    pick = (column == at[0] * 16 + row).astype(BF)
    pb[5] = dot(rows, pick).astype(BF)


def join(full, near, far):
    half = near.shape[0]
    full[:half] = near[...]
    full[half:] = far[...]


def self_forward(rows, ids, near, far, wa0, wa1, wa2, wa3, segs,
                 xf_out, w_out, q_out, kv_out, p_out, rl_out, at,
                 mask, xf, w, q, kv, p, p_sems, sems, rl):
    join(xf, near, far)
    copies = [keep_copy(xf, xf_out, sems.at[0])]
    unpack(ids, SLOT_A, (wa0, wa1, wa2, wa3), (w, 0, 3, 16))
    copies.append(keep_copy(w, w_out, sems.at[1]))
    set_mask(mask, segs, 0, 0, 1)
    q[...] = (dot(xf[:rows], w[0]).astype(BF).astype(F32) * SCALE).astype(BF)
    kv[:, :D] = dot(xf[...], w[1]).astype(BF)
    kv[:, D:] = dot(xf[...], w[2]).astype(BF)
    copies += [keep_copy(q, q_out, sems.at[2]), keep_copy(kv, kv_out, sems.at[3])]
    attend(q, kv, mask, p, rl, at, p_out, p_sems)
    copies.append(keep_copy(rl, rl_out, sems.at[8]))
    for copy in copies:
        copy.wait()


def cross_forward(rows, ids, xf, near, far, at1, wb0, wb1, wb2, wb3, segs,
                  ef_out, w, norms_out, xh1, rs1_out, low1_out, q_out, kv_out, p_out, rl_out, at_out,
                  mask, ef, low1, q, kv, p, p_sems, sems, rl, norms, rs1, at):
    join(ef, near, far)
    copies = [keep_copy(ef, ef_out, sems.at[0])]
    unpack(ids, SLOT_B, (wb0, wb1, wb2, wb3), (w, 0, 5, 16))
    set_mask(mask, segs, 2, 0, 3)
    gb = norm_rows((wb0, wb1, wb2, wb3))
    norms[...] = gb
    copies.append(keep_copy(norms, norms_out, sems.at[6]))
    resid = xf[...].astype(F32) + dot(at1[...], w[0], TN)
    xhat, rstd, n1 = norm_forward(resid, gb[0:1], gb[3:4])
    xh1[...] = xhat
    rs1[...] = jnp.broadcast_to(rstd, rs1.shape)
    copies.append(keep_copy(rs1, rs1_out, sems.at[7]))
    low1[...] = n1.astype(BF)
    copies.append(keep_copy(low1, low1_out, sems.at[1]))
    q[...] = (dot(low1[...], w[3]).astype(BF).astype(F32) * SCALE).astype(BF)
    kv[:, :D] = dot(ef[...], w[1]).astype(BF)
    kv[:, D:] = dot(ef[...], w[2]).astype(BF)
    copies += [keep_copy(q, q_out, sems.at[2]), keep_copy(kv, kv_out, sems.at[3])]
    attend(q, kv, mask, p, rl, at, p_out, p_sems)
    copies += [keep_copy(rl, rl_out, sems.at[8]), keep_copy(at, at_out, sems.at[9])]
    for copy in copies:
        copy.wait()


def ffn_both(ids, xh1, at2_in, teacher, message, dec_valid, wb, norms_in, wf0, wf1, wf2, wf3,
             out, small, d_r2, d_mix, keep, send, act, hid, low2, wup, wdn, at2, norms, sems):
    brought = [keep_copy(at2_in, at2, sems.at[0]), keep_copy(norms_in, norms, sems.at[1])]
    unpack(ids, SLOT_F, (wf0, wf1, wf2, wf3), (wup, 0, 4, 16), (wdn, 4, 4, 64))
    tok = teacher.shape[1]
    marks = jnp.where(ids[MINE] == 0, dec_valid[0:1], dec_valid[1:2]).astype(F32)
    marks = jnp.concatenate([marks, message[2 * tok : 2 * tok + 1, :tok].astype(F32)], 1)
    valid = jnp.transpose(jnp.broadcast_to(marks, (8, 2 * tok)))[:, 0:1]
    teach = jnp.concatenate([teacher[ids[MINE]], message[tok : 2 * tok]], 0)
    for copy in brought:
        copy.wait()
    gb = norms[...]
    n1 = xh1[...] * gb[0:1] + gb[3:4]
    wco = wb[4]
    xh2, rs2, n2 = norm_forward(n1 + dot(at2[...], wco, TN), gb[1:2], gb[4:5])
    low2[...] = n2.astype(BF)
    for j in range(4):
        h = dot(low2[...], wup[j])
        hid[j] = h
        act[:, j * D : (j + 1) * D] = (h / (1.0 + jnp.exp(-h))).astype(BF)
    r3 = n2 + dot(act[...], wdn[...])
    xh3, rs3, final = norm_forward(r3, gb[2:3], gb[5:6])
    out[...] = final.astype(BF)
    err = (final - teach.astype(F32)) * valid
    small[...] = jnp.zeros_like(small)
    small[6:7] = jnp.sum(err * err, axis=0, keepdims=True)
    lane = lax.broadcasted_iota(jnp.int32, (1, D), 1)
    small[7:8] = jnp.where(lane == ids[DEVICE], jnp.sum(valid), 0.0)
    d_r3, dg, db = norm_back(err, xh3, rs3, gb[2:3])
    small[2:3] = dg
    small[5:6] = db
    dffn = d_r3.astype(BF)
    for ref, at in sides(ids, keep, send):
        put(ids, PLACE_1, ref, 9, 4, dot(cols(act, at, FF // 4), dffn, TN))
    dn2 = d_r3
    for j in range(4):
        da = dot(dffn, wdn[j * D : (j + 1) * D], NT)
        h = hid[j]
        sig = 1.0 / (1.0 + jnp.exp(-h))
        dh = (da * (sig * (1.0 + h * (1.0 - sig)))).astype(BF)
        for ref, at in sides(ids, keep, send):
            put(ids, PLACE_1, ref, 9, j, dot(cols(low2, at, 128), dh, TN))
        dn2 = dn2 + dot(dh, wup[j], NT)
    dr2, dg, db = norm_back(dn2, xh2, rs2, gb[1:2])
    small[1:2] = dg
    small[4:5] = db
    d_r2[...] = dr2
    dcross = dr2.astype(BF)
    for ref, at in sides(ids, keep, send):
        put(ids, PLACE_1, ref, 9, 8, dot(rows_of(at2, at, 128), dcross))
    d_mix[...] = dot(dcross, wco, NT).astype(BF)


def cross_back_a(q, kv, p, rl, d_mix, dkv, dq, dqt):
    attend_back(0, q, kv, p, rl, d_mix, dkv, dqt)
    dq[...] = jnp.transpose(dqt[...]).astype(BF)


def project(own, parts, dkv_a, dkv_b, wk, wv, extra=0.0):
    out = dot(dkv_a[:, :HALF], wk[:, :HALF], NT) + dot(dkv_b[:, :HALF], wk[:, HALF:], NT)
    out = out + dot(dkv_a[:, HALF:], wv[:, :HALF], NT) + dot(dkv_b[:, HALF:], wv[:, HALF:], NT)
    each = own.shape[0]
    own[...] = out[:each] + extra
    for i, part in enumerate(parts):
        part[...] = out[each * (i + 1) : each * (i + 2)].astype(BF)


def cross_back_b(n_parts, ids, ef, q, kv, p, rl, d_mix, dkv_a, dq_a, wb, norms, d_r2, low1, xh1,
                 rs1, at1, small, own, *rest):
    parts, (d_mix1, d_r1, keep, send, dkv, dqt) = rest[:n_parts], rest[n_parts:]
    attend_back(4, q, kv, p, rl, d_mix, dkv, dqt)
    project(own, parts, dkv_a, dkv, wb[1], wb[2])
    dq = jnp.concatenate([dq_a[...], jnp.transpose(dqt[...]).astype(BF)], 1)
    gb = norms[...]
    dn1 = d_r2[...] + dot(dq, wb[3], NT)
    dr1, dg, db = norm_back(dn1, xh1[...], rs1[:, 0:1], gb[0:1])
    row = lax.broadcasted_iota(jnp.int32, (16, D), 0)
    sums = jnp.where(row == 0, dg, jnp.where(row == 3, db, small[...]))
    send[1024:1040] = sums.astype(BF)
    d_r1[...] = dr1
    dself = dr1.astype(BF)
    for ref, at in sides(ids, keep, send):
        lhs = cols(ef, at, 128)
        for j in range(2):
            span = slice(j * HALF, (j + 1) * HALF)
            g = jnp.concatenate([dot(lhs, dkv_a[:, span], TN), dot(lhs, dkv[:, span], TN)], 1)
            put(ids, PLACE_2, ref, 4, j, g)
        put(ids, PLACE_2, ref, 4, 2, dot(cols(low1, at, 128), dq, TN))
        put(ids, PLACE_2, ref, 4, 3, dot(rows_of(at1, at, 128), dself))
    d_mix1[...] = dot(dself, wb[0], NT).astype(BF)


def self_back_b(n_parts, rows, ids, xf, q, kv, p, rl, d_mix, dkv_a, dq_a, wa, d_r1, own, *rest):
    parts, (keep, send, dkv, dqt) = rest[:n_parts], rest[n_parts:]
    attend_back(4, q, kv, p, rl, d_mix, dkv, dqt)
    dq = jnp.concatenate([dq_a[...], jnp.transpose(dqt[...]).astype(BF)], 1)
    through_q = d_r1[...] + dot(dq, wa[0], NT)
    project(own, parts, dkv_a, dkv, wa[1], wa[2], through_q)
    for ref, at in sides(ids, keep, send):
        lhs = cols(xf, at, 128)
        put(ids, PLACE_2, ref, 3, 0, dot(lhs[:rows], dq, TN))
        for j in range(2):
            span = slice(j * HALF, (j + 1) * HALF)
            g = jnp.concatenate([dot(lhs, dkv_a[:, span], TN), dot(lhs, dkv[:, span], TN)], 1)
            put(ids, PLACE_2, ref, 3, 1 + j, g)


def tree_sum(terms):
    while len(terms) > 1:
        terms = [a + b for a, b in zip(terms[::2], terms[1::2])] + terms[len(terms) & ~1 :]
    return terms[0]


ANY = pl.BlockSpec(memory_space=pl.ANY)


def fetch(ref, start, count, to, sem):
    copy = pltpu.make_async_copy(ref.at[pl.ds(start, count)], to, sem)
    copy.start()
    return copy


def mix(name, *outs):
    arrays, terms, plan = [], [], []
    for dtype, segments in outs:
        plan.append([])
        for segment in segments:
            used = []
            for array, start, count in segment:
                at = [i for i, v in enumerate(arrays) if v is array]
                if not at:
                    arrays.append(array)
                used.append(len(terms))
                terms.append((at[0] if at else len(arrays) - 1, start, count, array.dtype))
            plan[-1].append(used)

    def body(*refs):
        for out, segments in zip(refs[len(arrays) :], plan):
            first = 0
            for used in segments:
                count = terms[used[0]][2]
                parts = [refs[k][start : start + count].astype(F32) for k, start, _, _ in (terms[i] for i in used)]
                out[first : first + count] = tree_sum(parts).astype(out.dtype)
                first += count

    shapes = [((sum(t[0][2] for t in segments), D), dtype) for dtype, segments in outs]
    return call(body, [(v, None) for v in arrays], shapes, name=name)


def finish(counts, *refs):
    where, refs = refs[0], refs[1:]
    sources, results = refs[: len(counts)], refs[len(counts) :]
    refs = [ref.at[:count] for ref, count in zip(sources, counts)]
    one, (out, home, e_keep, x_keep, home_x, z_own, z_got, *refs) = refs[:5], refs[5:]
    two, three = refs[:6], refs[6:]
    outputs, loss, g_x, g_e, g_in, g_so, g_cq, g_cin, g_co, g_up, g_down, g_gain, g_bias = results
    mine = where[0]
    tok = e_keep.shape[0]
    outputs[mine] = out[...]
    outputs[1 - mine] = home[:tok]
    g_e[mine] = e_keep[...]
    g_e[1 - mine] = home[tok:].astype(F32)
    g_x[mine] = x_keep[...]
    g_x[1 - mine] = home_x[:tok].astype(F32)
    t1 = tree_sum([r[...].astype(F32) for r in one] + [home_x[tok:].astype(F32)])
    for j in range(4):
        g_up[:, j * D : (j + 1) * D] = t1[16 * j : 16 * j + 16]
    g_down[...] = t1[64:128]
    g_co[...] = t1[128:144]
    t2 = tree_sum([r[...].astype(F32) for r in two[:3]] + [r[:64].astype(F32) for r in two[3:]] + [z_got[:64].astype(F32)])
    for j in range(2):
        g_cin[:, j * D : (j + 1) * D] = t2[16 * j : 16 * j + 16]
    g_cq[...] = t2[32:48]
    g_so[...] = t2[48:64]
    t3 = tree_sum([r[...].astype(F32) for r in three] + [r[128:176].astype(F32) for r in two[3:]] + [z_got[64:112].astype(F32)])
    for j in range(3):
        g_in[:, j * D : (j + 1) * D] = t3[16 * j : 16 * j + 16]
    small = z_own[112:128].astype(F32) + z_got[112:128].astype(F32)
    total = jnp.sum(small[6:7], axis=1, keepdims=True)
    loss[...] = total / (jnp.sum(small[7:8], axis=1, keepdims=True) * D)
    column = lax.broadcasted_iota(jnp.int32, (16, D), 1)
    row = lax.broadcasted_iota(jnp.int32, (16, D), 0)
    pick = (column == where[1] * 16 + row).astype(F32)
    own = lax.dot_general(small[:8], pick, NT, precision=lax.Precision.HIGHEST, preferred_element_type=F32)
    g_gain[...] = own[0:3]
    g_bias[...] = own[3:6]


def tie(*values):
    return lax.optimization_barrier(values)


def make_shards(nd, ns):
    n_dev = nd * ns
    half = ns // 2
    per = G * 16 // n_dev
    fast = nd == 4 and ns == 8
    run = functools.partial(call, vmem=20 if fast else 48)

    core, y, x, zl, zh = ("dp", 1), ("dp", 2), ("seq", 1), ("seq", 2), ("seq", 4)

    def shards(inputs, encoder, teacher, dec_seg, enc_seg, dec_valid, self_in, self_out,
               cross_query, cross_in, cross_out, ffn_up, ffn_down, norm_gain, norm_bias):
        tok = inputs.shape[1]
        rows = 2 * tok
        length = dec_seg.shape[1]
        dp_at, seq_at = lax.axis_index("dp"), lax.axis_index("seq")
        dev = dp_at * ns + seq_at
        mine = seq_at // half

        def flip(bit, arrays):
            axis, b = bit
            size = nd if axis == "dp" else ns
            flat = [v.reshape(-1, D) for v in arrays]
            got = lax.ppermute(
                flat[0] if len(flat) == 1 else jnp.concatenate(flat, 0),
                axis, [(i, i ^ b) for i in range(size)],
            )
            out, start = [], 0
            for v, f in zip(arrays, flat):
                out.append(lax.slice_in_dim(got, start, start + f.shape[0]).reshape(v.shape))
                start += f.shape[0]
            return out

        def swap(bit, array):
            return flip(bit, [array])[0]

        def of(v, i):
            return lax.dynamic_index_in_dim(v, i, 0, keepdims=False)

        def other(v):
            return of(v, 1 - mine)

        def append(v, got):
            return jnp.concatenate([v, got], 0)

        valid_away = jnp.pad(other(dec_valid).astype(BF)[None], ((0, 15), (0, D - tok)))

        row_bits = (2, 1) if fast else tuple(1 << b for b in range(half.bit_length() - 1))
        slots = jnp.arange(half, dtype=jnp.int32)

        def pieces(bits):
            masks = sum((((slots >> i) & 1) * b) for i, b in enumerate(bits))[:, None]
            return (seq_at ^ masks ^ jnp.array([[0, half]], jnp.int32)).reshape(-1)

        pos = (pieces(row_bits)[:, None] * tok + jnp.arange(tok, dtype=jnp.int32)[None]).reshape(-1)
        dec_k = of(dec_seg, mine).reshape(ns, tok)[pieces(row_bits)].reshape(-1)
        enc_k = of(enc_seg, mine).reshape(ns, tok)[pieces(row_bits)].reshape(-1)
        segs = jnp.stack([dec_k, pos, enc_k] + [jnp.zeros_like(pos)] * 5).astype(F32)

        def spread(v, bits):
            return sum((((v & b) != 0).astype(jnp.int32) << i) for i, b in enumerate(bits))

        if fast:
            i16 = jnp.arange(16, dtype=jnp.int32)
            g32 = jnp.arange(32, dtype=jnp.int32)
            dev16 = (dp_at >> 1) * 8 + seq_at

            def came_from(bits):
                return dev ^ sum((((g32 >> i) & 1) * b for i, b in enumerate(bits)))

            ids = jnp.concatenate(
                [
                    jnp.stack([dp_at & 1, dev, mine]).astype(jnp.int32),
                    spread(i16 ^ dev16, (4, 2, 1, 8)),
                    spread(i16 ^ dev16, (4, 2, 1, 8)),
                    came_from((4, 2, 1, 16, 8)),
                    came_from((4, 16, 1, 2, 8)),
                    came_from((4, 2, 1, 16, 8)),
                ]
            )
        else:
            i16, g32 = jnp.arange(16, dtype=jnp.int32), jnp.arange(32, dtype=jnp.int32)
            ids = jnp.concatenate([jnp.stack([0 * dev, dev, mine]).astype(jnp.int32), i16, i16, g32, g32, g32])

        if fast:
            mats = [self_in, self_out, cross_in, cross_query, cross_out, ffn_up, ffn_down, norm_gain, norm_bias]
            wa, wb, wf = run(
                pack,
                [(w, None) for w in mats] + [(dev.astype(jnp.int32)[None], SMEM)],
                [((3, 16, D), BF), ((6, 16, D), BF), ((8, 16, D), BF)],
                name="pack",
                vmem=56,
            )
            wa, wb, wf = wa[None], wb[None], wf[None]
            got_x, got_a = flip(zh, [other(inputs), wa])
            got_x, got_a, wb, wf, segs, ids = tie(got_x, got_a, wb, wf, segs, ids)
            got_b, got_f = flip(zh, [wb, wf])
            xf, wa = jnp.stack([of(inputs, mine), got_x])[None], append(wa, got_a)
            got_x, got_a = flip(zl, [xf, wa])
            got_x, got_a, got_b, got_f, away_e = tie(got_x, got_a, got_b, got_f, other(encoder))
            xf, wa = append(xf, got_x), append(wa, got_a)
            wb, wf = append(wb, got_b), append(wf, got_f)
            got_x, got_a = flip(x, [xf, wa])
            message = swap(zh, jnp.concatenate([away_e, other(teacher), valid_away], 0))
            got_e = message[:tok]
            got_b, got_f = swap(y, wb), swap(zl, wf)
            ef = jnp.stack([of(encoder, mine), got_e])[None]
            got_x, got_a, got_b, got_f, ef = tie(got_x, got_a, got_b, got_f, ef)
            wa, wb, wf = append(wa, got_a), append(wb, got_b), append(wf, got_f)
            got_a, got_b, got_e, got_f = swap(y, wa), swap(x, wb), swap(zl, ef), swap(x, wf)
            wa_far = swap(core, wa)
            got_a, got_b, got_e, wa_far = tie(got_a, got_b, got_e, wa_far)
            wa = [wa, got_a, wa_far, swap(core, got_a)]
            wb, ef = append(wb, got_b), append(ef, got_e)
            got_b, got_e = swap(zl, wb), swap(x, ef)
            got_f, wa[3] = tie(got_f, wa[3])
            wf = append(wf, got_f)
            got_f = swap(y, wf)
            wb_far, wf_far = swap(core, wb), swap(core, wf)
        else:
            got_x = swap(("seq", half), other(inputs))
            message = swap(("seq", half), jnp.concatenate([other(encoder), other(teacher), valid_away], 0))
            got_e = message[:tok]
            xf, ef = jnp.stack([of(inputs, mine), got_x])[None], jnp.stack([of(encoder, mine), got_e])[None]
            for bit in row_bits:
                got_x, got_e = flip(("seq", bit), [xf, ef])
                if bit != row_bits[-1]:
                    xf, ef = append(xf, got_x), append(ef, got_e)

            def gathered(w):
                return lax.all_gather(w, ("dp", "seq"), axis=0, tiled=True)

            def grouped(w):
                return w.reshape(G, 16, w.shape[1] // D, D).transpose(0, 2, 1, 3)

            wa = grouped(gathered(self_in))
            mine_only = lax.dynamic_update_slice(
                jnp.zeros((16, D), BF), jnp.concatenate([norm_gain, norm_bias], 0), (0, dev * per)
            )
            all_norms = lax.psum(mine_only.astype(F32), ("dp", "seq")).astype(BF)
            all_norms = jnp.pad(all_norms[None], ((0, G - 1), (0, 0), (0, 0)))[:, None]
            rest = [grouped(gathered(w)) for w in (self_out, cross_in, cross_query, cross_out)]
            down = gathered(ffn_down).reshape(G, 4, 16, D)
            wb = jnp.concatenate(rest + [all_norms], 1)
            wf = jnp.concatenate([grouped(gathered(ffn_up)), down], 1)
            wa, wb, wf = [[w[8 * i : 8 * i + 8] for i in range(4)] for w in (wa, wb, wf)]
        x_near, x_far = xf.reshape(-1, D), got_x.reshape(-1, D)

        sm = (ids, SMEM)
        p_shape = (HEADS, length, rows)
        def held(*shapes):
            return (
                [pltpu.VMEM((length, rows), F32)]
                + [pltpu.VMEM(v, BF) for v in shapes]
                + [pltpu.VMEM((2, 2, length, rows), BF), pltpu.SemaphoreType.DMA((2,)), pltpu.SemaphoreType.DMA((10,))]
                + [pltpu.VMEM((HEADS, rows), F32)]
            )

        all_rows, own_rows, both_kv = (length, D), (rows, D), (length, 2 * D)
        own_x = x_near[:rows]
        xf, wa, q1, kv1, p1, rl1, at1 = run(
            functools.partial(self_forward, rows),
            [sm, (x_near, None), (x_far, None)] + [(v, None) for v in wa] + [(segs, None)],
            [(all_rows, BF, True), ((3, D, D), BF, True), (own_rows, BF, True), (both_kv, BF, True),
             (p_shape, BF, True), ((HEADS, rows), F32, True), ((D, rows), BF)],
            scratch=held(all_rows, (3, D, D), own_rows, both_kv),
            name="self_forward",
        )
        if fast:
            got_b, got_e, wb_far, at1 = tie(got_b, got_e, wb_far, at1)
            wb = [wb, got_b, wb_far, swap(core, got_b)]
        e_near, e_far = ef.reshape(-1, D), got_e.reshape(-1, D)
        ef, wb, norms, xh1, rs1, low1, q2, kv2, p2, rl2, at2 = run(
            functools.partial(cross_forward, rows),
            [sm, (own_x, None), (e_near, None), (e_far, None), (at1, None)] + [(v, None) for v in wb] + [(segs, None)],
            [(all_rows, BF, True), ((5, D, D), BF), ((16, D), F32, True), (own_rows, F32), ((rows, 128), F32, True),
             (own_rows, BF, True), (own_rows, BF, True), (both_kv, BF, True), (p_shape, BF, True),
             ((HEADS, rows), F32, True), ((D, rows), BF, True)],
            scratch=held(all_rows, own_rows, own_rows, both_kv)
            + [pltpu.VMEM((16, D), F32), pltpu.VMEM((rows, 128), F32), pltpu.VMEM((D, rows), BF)],
            name="cross_forward",
        )
        if fast:
            got_f, wf_far, at2 = tie(got_f, wf_far, at2)
            wf = [wf, got_f, wf_far, swap(core, got_f)]
        out, small, d_r2, d_mix2, keep1, send1 = run(
            ffn_both,
            [sm, (xh1, None), (at2, HBM), (teacher, None), (message, None), (dec_valid, None), (wb, None), (norms, HBM)]
            + [(v, None) for v in wf],
            [((rows, D), BF), ((16, D), F32), ((rows, D), F32), ((rows, D), BF)] + [((2304, D), BF)] * 2,
            scratch=[pltpu.VMEM((rows, FF), BF), pltpu.VMEM((4, rows, D), F32), pltpu.VMEM((rows, D), BF),
                     pltpu.VMEM((4, D, D), BF), pltpu.VMEM((FF, D), BF), pltpu.VMEM((D, rows), BF),
                     pltpu.VMEM((16, D), F32), pltpu.SemaphoreType.DMA((2,))],
            name="ffn_both",
        )

        kv_half = [((length, D), BF), ((rows, HALF), BF)]
        d_rows = [pltpu.VMEM((HALF, rows), F32)]
        both_scratch = [pltpu.VMEM((length, D), BF)] + d_rows
        row_parts = [((rows, D), F32)] + [((rows, D), BF)] * (half - 1)
        partners = [sum(((i >> k) & 1) * b for k, b in enumerate(row_bits)) for i in range(1, half)]

        if fast:
            got1 = swap(core, send1)
        dkv2, dq2 = run(
            cross_back_a,
            [(q2, None), (kv2, None), (p2, None), (rl2, None), (d_mix2, None)],
            kv_half,
            scratch=d_rows,
            name="cross_back_a",
        )
        if fast:
            got1, d_mix2, dkv2 = tie(got1, d_mix2, dkv2)
            got_y1 = swap(y, (keep1[1152:].astype(F32) + got1[1152:].astype(F32)).astype(BF))
        e_own, *rest = run(
            functools.partial(cross_back_b, half - 1),
            [sm, (ef, None), (q2, None), (kv2, None), (p2, None), (rl2, None), (d_mix2, None),
             (dkv2, None), (dq2, None), (wb, None), (norms, None), (d_r2, None), (low1, None),
             (xh1, None), (rs1, None), (at1, None), (small, None)],
            row_parts + [((rows, D), BF), ((rows, D), F32), ((1024, D), BF), ((1040, D), BF)],
            scratch=both_scratch,
            name="cross_back_b",
        )
        e_parts, (d_mix1, d_r1, keep2, send2) = rest[: half - 1], rest[half - 1 :]
        if fast:
            got2 = swap(core, send2)
        e_got = [swap(("seq", m), part) for m, part in zip(partners, e_parts)]
        dkv1, dq1 = run(
            cross_back_a,
            [(q1, None), (kv1, None), (p1, None), (rl1, None), (d_mix1, None)],
            kv_half,
            scratch=d_rows,
            name="self_back_a",
        )
        if fast:
            got2, d_mix1, dkv1 = tie(got2, d_mix1, dkv1)
        x_own, *rest = run(
            functools.partial(self_back_b, half - 1, rows),
            [sm, (xf, None), (q1, None), (kv1, None), (p1, None), (rl1, None), (d_mix1, None),
             (dkv1, None), (dq1, None), (wa, None), (d_r1, None)],
            row_parts + [((768, D), BF)] * 2,
            scratch=both_scratch,
            name="self_back_b",
        )
        x_parts, (keep3, send3) = rest[: half - 1], rest[half - 1 :]

        if fast:
            (away,) = mix("away_x", (BF, [[(x_parts[0], 0, rows)], [(x_parts[2], 0, rows)]]))
            got_xa = swap(zl, away)
            got_y1, send3, *e_got = tie(got_y1, send3, *e_got)
            (away,) = mix(
                "sum_y2",
                (BF, [[(keep2, 512, 512), (got2, 512, 512)], [(send2, 1024, 16), (got2, 1024, 16)]]),
            )
            got_y2 = swap(y, away)
            small_y2 = (away, 512, 16)
            one = lambda start, count: [(v, start, count) for v in (keep1, got1, got_y1)]
            (away,) = mix("sum_1x", (BF, [one(576, 576)]))
            got_1a = swap(x, away)
        else:
            x_got = [swap(("seq", m), part) for m, part in zip(partners, x_parts)]
        if fast:
            got3 = swap(core, send3)
        e_terms = lambda start: [(v, start, tok) for v in (e_own, *e_got)]
        e_keep, away = mix("sum_e", (F32, [e_terms(0)]), (BF, [[(out, tok, tok)], e_terms(tok)]))
        home = swap(("seq", half), away)
        if fast:
            (away,) = mix("sum_y3", (BF, [[(keep3, 384, 384), (got3, 384, 384)]]))
            got_y3 = swap(y, away)
            got_y3, home = tie(got_y3, home)
        if fast:
            (away,) = mix("sum_xx", (BF, [[(x_parts[1], 0, rows), (got_xa, rows, rows)]]))
            got_xb = swap(x, away)
            (away,) = mix("sum_1z", (BF, [one(288, 288) + [(got_1a, 288, 288)]]))
            got_1b = swap(zl, away)
            x_terms = lambda start: [(v, start, tok) for v in (x_own, got_xa, got_xb)]
            more = [one(144, 144) + [(got_1a, 144, 144), (got_1b, 144, 144)]]
        else:
            x_terms = lambda start: [(v, start, tok) for v in (x_own, *x_got)]
            more = []
        x_keep, away = mix("sum_x", (F32, [x_terms(0)]), (BF, [x_terms(tok), *more]))
        home_x = swap(("seq", half), away)

        if fast:
            def two(start, count):
                return [(v, start, count) for v in (keep2, got2, got_y2)]

            def three(start, count):
                return [(v, start, count) for v in (keep3, got3, got_y3)]

            quads = mix(
                "sum_quads",
                *[(BF, [two(128 * i, 128), three(96 * i, 96), [small_y2, (got_y2, 512, 16)]]) for i in (1, 2, 3)],
            )
            q_got = [swap(("seq", m), part) for m, part in zip(partners, quads)]
            (away,) = mix(
                "sum_zh",
                (BF, [two(64, 64) + [(v, 64, 64) for v in q_got], three(48, 48) + [(v, 176, 48) for v in q_got],
                      [(quads[0], 224, 16)] + [(v, 224, 16) for v in q_got]]),
            )
            got_z = swap(zh, away)
            where = jnp.stack([mine, dev]).astype(jnp.int32)

            last = [(v, 144) for v in (keep1, got1, got_y1, got_1a, got_1b)] + [(out, tok)]
            last += [(v, v.shape[0]) for v in (home, e_keep, x_keep, home_x, away, got_z)]
            last += [(v, 64) for v in (keep2, got2, got_y2)] + [(v, v.shape[0]) for v in q_got]
            last += [(v, 48) for v in (keep3, got3, got_y3)]
            counts = [c for _, c in last]
            flat = [((per, w), F32) for w in (3 * D, D, D, 2 * D, D, FF)] + [((4 * per, D), F32)]
            done = run(
                functools.partial(finish, counts),
                [(where, SMEM)] + [(v, None) for v, _ in last],
                [((2, tok, D), BF), ((1, 1), F32), ((2, tok, D), F32), ((2, tok, D), F32)] + flat + [((3, per), F32)] * 2,
                name="finish",
            )
            return (done[0], done[1].reshape(()), *done[2:])

        def back_home(kept, recv):
            return jnp.where(mine == 0, jnp.stack([kept, recv]), jnp.stack([recv, kept]))

        def summed(g):
            return lax.psum_scatter(g, ("dp", "seq"), scatter_dimension=0, tiled=True).astype(F32)

        def rejoin(keep, send, n):
            g = jnp.stack([v[: 256 * n].reshape(2, 8, n, 16, D) for v in (keep, send)], 1)
            return g.reshape(G, n, 16, D)

        def full(g):
            return g.transpose(0, 2, 1, 3).reshape(G * 16, -1)

        small = lax.psum(send2[1024:].astype(F32), ("dp", "seq"))
        all1, all2, all3 = rejoin(keep1, send1, 9), rejoin(keep2, send2, 4), rejoin(keep3, send3, 3)
        g_norm = lax.dynamic_slice(small, (0, dev * per), (6, per))
        return (
            back_home(out[:tok], home[:tok]),
            jnp.sum(small[6]) / (jnp.sum(small[7]) * D),
            back_home(x_keep, home_x.astype(F32)),
            back_home(e_keep, home[tok:].astype(F32)),
            summed(full(all3)),
            summed(full(all2[:, 3:])),
            summed(full(all2[:, 2:3])),
            summed(full(all2[:, :2])),
            summed(full(all1[:, 8:])),
            summed(full(all1[:, :4])),
            summed(all1[:, 4:8].reshape(FF, D)),
            g_norm[:3],
            g_norm[3:],
        )

    return shards


def solution(mesh):
    rows, both = P("dp", "seq", None), P(("dp", "seq"), None)
    norm = P(None, ("dp", "seq"))
    return jax.shard_map(
        make_shards(mesh.shape["dp"], mesh.shape["seq"]),
        mesh=mesh,
        in_specs=(rows, rows, rows, P("dp", None), P("dp", None), P("dp", "seq")) + (both,) * 7 + (norm, norm),
        out_specs=(rows, P(), rows, rows) + (both,) * 7 + (norm, norm),
        check_vma=False,
    )
```

```python
import functools

import jax
import jax.numpy as jnp
from jax import lax
from jax.experimental import pallas as pl
from jax.experimental.pallas import tpu as pltpu
from jax.sharding import PartitionSpec as P

HEADS = 8
HEAD_DIM = 64
EPS = 1e-5
NEG = -1e30
SCALE = 0.125
D = 512
FF = 2048
HALF = 256
G = 32
BF = jnp.bfloat16
F32 = jnp.float32
MIB = 1 << 20

DEVICE, MINE, PLACE_1, PLACE_2, SLOT_A, SLOT_B, SLOT_F = 1, 2, 3, 19, 35, 67, 99

NN = (((1,), (0,)), ((), ()))
NT = (((1,), (1,)), ((), ()))
TN = (((0,), (0,)), ((), ()))


def dot(a, b, dims=NN):
    return lax.dot_general(a, b, dims, preferred_element_type=F32)


def in_hbm(v):
    return pltpu.with_memory_space_constraint(v, pltpu.HBM)


def whole(shape):
    return pl.BlockSpec(shape, lambda i: (0,) * len(shape))


SMEM = pl.BlockSpec(memory_space=pltpu.SMEM)
HBM = pl.BlockSpec(memory_space=pltpu.HBM)


def call(body, ins, outs, scratch=(), name=None, vmem=16):
    return pl.pallas_call(
        body,
        grid=(1,),
        in_specs=[whole(a.shape) if s is None else s for a, s in ins],
        out_specs=[whole(o[0]) if len(o) == 2 else pl.BlockSpec(memory_space=pltpu.HBM) for o in outs],
        out_shape=[jax.ShapeDtypeStruct(*o) if len(o) == 2 else pltpu.HBM(*o[:2]) for o in outs],
        scratch_shapes=list(scratch),
        compiler_params=pltpu.CompilerParams(vmem_limit_bytes=vmem * MIB),
        name=name,
        cost_estimate=pl.CostEstimate(flops=1000, bytes_accessed=1000, transcendentals=0),
    )(*[a for a, _ in ins])


def unpack(ids, table, parts, *targets):
    each = parts[0].shape[0]
    for p, part in enumerate(parts):
        for i in range(each):
            group = ids[table + each * p + i]
            for ref, first, count, height in targets:
                at = pl.multiple_of(group * height, 16)
                block = part[i, first : first + count]
                if height == 16:
                    ref[:, pl.ds(at, 16), :] = block
                else:
                    ref[pl.ds(at, height), :] = block.reshape(height, D)


def norm_rows(parts):
    return sum(jnp.sum(part[:, 5].astype(F32), axis=0) for part in parts)


def set_mask(mask, segs, key, query, position):
    length, rows = mask.shape
    columns = jnp.transpose(segs[...])
    same = columns[:, key : key + 1] == segs[query : query + 1, :rows]
    ahead = columns[:, position : position + 1] <= segs[position : position + 1, :rows]
    mask[...] = jnp.where(same & ahead, 0.0, NEG)


def put(ids, first, ref, chunks_each, j, value):
    value = value.astype(BF)
    each = value.shape[0] // 16
    for i in range(16):
        at = ids[first + i] * (16 * chunks_each) + 16 * j
        ref[pl.ds(pl.multiple_of(at, 16), each), :] = value[each * i : each * i + each]


def norm_forward(resid, gain, bias):
    centre = resid - jnp.mean(resid, axis=-1, keepdims=True)
    rstd = lax.rsqrt(jnp.mean(centre * centre, axis=-1, keepdims=True) + EPS)
    xhat = centre * rstd
    return xhat, rstd, xhat * gain + bias


def norm_back(g, xhat, rstd, gain):
    e = g * gain
    m1 = jnp.mean(e, axis=-1, keepdims=True)
    m2 = jnp.mean(e * xhat, axis=-1, keepdims=True)
    dr = (e - m1 - xhat * m2) * rstd
    return dr, jnp.sum(g * xhat, axis=0, keepdims=True), jnp.sum(g, axis=0, keepdims=True)


def head_half(x, e):
    lane = lax.broadcasted_iota(jnp.int32, x.shape, 1)
    return jnp.where((lane < HEAD_DIM) == (e == 0), x, jnp.zeros_like(x))


def two_heads(x):
    return jnp.concatenate([head_half(x, 0), head_half(x, 1)], 0)


def attend(q_ref, kv_ref, mask_ref, p_ref, rl_ref, at_ref, p_out, sems):
    rows = mask_ref.shape[1]

    def leave(hp, slot):
        return pltpu.make_async_copy(p_ref.at[slot], p_out.at[pl.ds(2 * hp, 2)], sems.at[slot])

    def pair(hp, carry):
        slot = hp % 2

        @pl.when(hp >= 2)
        def _():
            leave(hp - 2, slot).wait()

        c0 = pl.multiple_of(hp * 128, 128)
        k2 = kv_ref[:, pl.ds(c0, 128)]
        v2 = kv_ref[:, pl.ds(pl.multiple_of(D + c0, 128), 128)]
        q2 = q_ref[:, pl.ds(c0, 128)]
        both = dot(k2, two_heads(q2), NT)
        probs, scales = [], []
        for e in range(2):
            s = both[:, e * rows : (e + 1) * rows] + mask_ref[...]
            p = jnp.exp(s - jnp.max(s, axis=0, keepdims=True))
            rl = 1.0 / jnp.sum(p, axis=0, keepdims=True)
            probs.append(p.astype(BF))
            p_ref[slot, e] = probs[e]
            rl_ref[pl.ds(2 * hp + e, 1), :] = rl
            scales.append(rl)
        o = dot(v2, jnp.concatenate(probs, 1), TN)
        for e in range(2):
            out = o[e * HEAD_DIM : (e + 1) * HEAD_DIM, e * rows : (e + 1) * rows] * scales[e]
            at_ref[pl.ds(pl.multiple_of((2 * hp + e) * HEAD_DIM, HEAD_DIM), HEAD_DIM), :] = out.astype(BF)
        leave(hp, slot).start()
        return carry

    pairs = HEADS // 2
    lax.fori_loop(0, pairs, pair, 0)
    for hp in (pairs - 2, pairs - 1):
        leave(hp, hp % 2).wait()


def keep_copy(held, out, sem):
    copy = pltpu.make_async_copy(held, out, sem)
    copy.start()
    return copy


def attend_back(first, q_ref, kv_ref, p_ref, rl_ref, do_ref, dkv_ref, dqt_ref):
    rows = q_ref.shape[0]

    def pair(i, carry):
        hp = first // 2 + i
        c0 = pl.multiple_of(hp * 128, 128)
        o0 = pl.multiple_of(i * 128, 128)
        k2 = kv_ref[:, pl.ds(c0, 128)]
        v2 = kv_ref[:, pl.ds(pl.multiple_of(D + c0, 128), 128)]
        q2 = q_ref[:, pl.ds(c0, 128)]
        do2 = do_ref[:, pl.ds(c0, 128)]
        dobd = two_heads(do2)
        both = dot(v2, dobd, NT)
        probs, grads = [], []
        for e in range(2):
            p = p_ref[2 * hp + e].astype(F32) * rl_ref[pl.ds(2 * hp + e, 1), :]
            t = p * both[:, e * rows : (e + 1) * rows]
            grads.append((t - p * jnp.sum(t, axis=0, keepdims=True)).astype(BF))
            probs.append(p.astype(BF))
        ds = jnp.concatenate(grads, 1)
        dk = dot(ds, two_heads(q2))
        dv = dot(jnp.concatenate(probs, 1), dobd)
        dqt = dot(k2, ds, TN) * SCALE
        for e in range(2):
            dqt_ref[pl.ds(pl.multiple_of((2 * i + e) * HEAD_DIM, HEAD_DIM), HEAD_DIM), :] = dqt[
                e * HEAD_DIM : (e + 1) * HEAD_DIM, e * rows : (e + 1) * rows
            ]
        dkv_ref[:, pl.ds(o0, 128)] = dk.astype(BF)
        dkv_ref[:, pl.ds(pl.multiple_of(HALF + o0, 128), 128)] = dv.astype(BF)
        return carry

    lax.fori_loop(0, HEADS // 4, pair, 0, unroll=True)


def cols(ref, c, width):
    picks = [ref[:, pl.ds(pl.multiple_of((2 * y + c) * width, width), width)] for y in range(2)]
    return jnp.concatenate(picks, 1)


def rows_of(ref, c, width):
    picks = [ref[pl.ds(pl.multiple_of((2 * y + c) * width, width), width), :] for y in range(2)]
    return jnp.concatenate(picks, 0)


def sides(ids, keep, send):
    return ((send, 1 - ids[0]), (keep, ids[0]))


def pack(s_in, s_out, c_in, c_q, c_out, up, down, gain, bias, inputs, encoder, teacher, valid, at,
         first, second, third, own_x, own_e):
    tok = own_x.shape[0]
    mine = at[1]
    first[:tok] = inputs[1 - mine]
    own_x[...] = inputs[mine]
    own_e[...] = encoder[mine]
    for j in range(3):
        first[tok + 16 * j : tok + 16 * j + 16] = s_in[:, j * D : (j + 1) * D]
    parts = [s_out] + [c_in.at[:, j * D : (j + 1) * D] for j in range(2)] + [c_q, c_out, None]
    parts += [up.at[:, j * D : (j + 1) * D] for j in range(4)] + [down.at[16 * j : 16 * j + 16] for j in range(4)]
    for j, part in enumerate(parts):
        if part is not None:
            second[16 * j : 16 * j + 16] = part[...]
    rows = jnp.concatenate([gain[...], bias[...], jnp.zeros((10, 16), BF)], 0)
    column = lax.broadcasted_iota(jnp.int32, (16, D), 1)
    row = lax.broadcasted_iota(jnp.int32, (16, D), 0)
    pick = (column == at[0] * 16 + row).astype(BF)
    second[80:96] = dot(rows, pick).astype(BF)
    third[:tok] = encoder[1 - mine]
    third[tok : 2 * tok] = teacher[1 - mine]
    marks = jnp.where(mine == 0, valid[1:2], valid[0:1]).astype(F32)
    marks = jnp.concatenate([marks, jnp.zeros((1, D - tok), F32)], 1)
    third[2 * tok :] = jnp.where(row == 0, marks, 0.0).astype(BF)


def join(full, near, far):
    half = near.shape[0]
    full[:half] = near[...]
    full[half:] = far[...]


def self_forward(rows, ids, near, far, wa0, wa1, wa2, wa3, segs,
                 xf_out, w_out, q_out, kv_out, p_out, rl_out, at,
                 mask, xf, w, q, kv, p, p_sems, sems, rl):
    join(xf, near, far)
    copies = [keep_copy(xf, xf_out, sems.at[0])]
    unpack(ids, SLOT_A, (wa0, wa1, wa2, wa3), (w, 0, 3, 16))
    copies.append(keep_copy(w, w_out, sems.at[1]))
    set_mask(mask, segs, 0, 0, 1)
    q[...] = (dot(xf[:rows], w[0]).astype(BF).astype(F32) * SCALE).astype(BF)
    kv[:, :D] = dot(xf[...], w[1]).astype(BF)
    kv[:, D:] = dot(xf[...], w[2]).astype(BF)
    copies += [keep_copy(q, q_out, sems.at[2]), keep_copy(kv, kv_out, sems.at[3])]
    attend(q, kv, mask, p, rl, at, p_out, p_sems)
    copies.append(keep_copy(rl, rl_out, sems.at[8]))
    for copy in copies:
        copy.wait()


def cross_forward(rows, ids, xf, near, far, at1, wb0, wb1, wb2, wb3, segs,
                  ef_out, w, norms_out, xh1, rs1_out, low1_out, q_out, kv_out, p_out, rl_out, at_out,
                  mask, ef, low1, q, kv, p, p_sems, sems, rl, norms, rs1, at):
    join(ef, near, far)
    copies = [keep_copy(ef, ef_out, sems.at[0])]
    unpack(ids, SLOT_B, (wb0, wb1, wb2, wb3), (w, 0, 5, 16))
    set_mask(mask, segs, 2, 0, 3)
    gb = norm_rows((wb0, wb1, wb2, wb3))
    norms[...] = gb
    copies.append(keep_copy(norms, norms_out, sems.at[6]))
    resid = xf[...].astype(F32) + dot(at1[...], w[0], TN)
    xhat, rstd, n1 = norm_forward(resid, gb[0:1], gb[3:4])
    xh1[...] = xhat
    rs1[...] = jnp.broadcast_to(rstd, rs1.shape)
    copies.append(keep_copy(rs1, rs1_out, sems.at[7]))
    low1[...] = n1.astype(BF)
    copies.append(keep_copy(low1, low1_out, sems.at[1]))
    q[...] = (dot(low1[...], w[3]).astype(BF).astype(F32) * SCALE).astype(BF)
    kv[:, :D] = dot(ef[...], w[1]).astype(BF)
    kv[:, D:] = dot(ef[...], w[2]).astype(BF)
    copies += [keep_copy(q, q_out, sems.at[2]), keep_copy(kv, kv_out, sems.at[3])]
    attend(q, kv, mask, p, rl, at, p_out, p_sems)
    copies += [keep_copy(rl, rl_out, sems.at[8]), keep_copy(at, at_out, sems.at[9])]
    for copy in copies:
        copy.wait()


def ffn_both(ids, xh1, at2_in, teacher, message, dec_valid, wb, norms_in, wf0, wf1, wf2, wf3,
             out, small, d_r2, d_mix, keep, send, act, hid, low2, wup, wdn, at2, norms, sems):
    brought = [keep_copy(at2_in, at2, sems.at[0]), keep_copy(norms_in, norms, sems.at[1])]
    unpack(ids, SLOT_F, (wf0, wf1, wf2, wf3), (wup, 0, 4, 16), (wdn, 4, 4, 64))
    tok = teacher.shape[1]
    marks = jnp.where(ids[MINE] == 0, dec_valid[0:1], dec_valid[1:2]).astype(F32)
    marks = jnp.concatenate([marks, message[2 * tok : 2 * tok + 1, :tok].astype(F32)], 1)
    valid = jnp.transpose(jnp.broadcast_to(marks, (8, 2 * tok)))[:, 0:1]
    teach = jnp.concatenate([teacher[ids[MINE]], message[tok : 2 * tok]], 0)
    for copy in brought:
        copy.wait()
    gb = norms[...]
    n1 = xh1[...] * gb[0:1] + gb[3:4]
    wco = wb[4]
    xh2, rs2, n2 = norm_forward(n1 + dot(at2[...], wco, TN), gb[1:2], gb[4:5])
    low2[...] = n2.astype(BF)
    for j in range(4):
        h = dot(low2[...], wup[j])
        hid[j] = h
        act[:, j * D : (j + 1) * D] = (h / (1.0 + jnp.exp(-h))).astype(BF)
    r3 = n2 + dot(act[...], wdn[...])
    xh3, rs3, final = norm_forward(r3, gb[2:3], gb[5:6])
    out[...] = final.astype(BF)
    err = (final - teach.astype(F32)) * valid
    small[...] = jnp.zeros_like(small)
    small[6:7] = jnp.sum(err * err, axis=0, keepdims=True)
    lane = lax.broadcasted_iota(jnp.int32, (1, D), 1)
    small[7:8] = jnp.where(lane == ids[DEVICE], jnp.sum(valid), 0.0)
    d_r3, dg, db = norm_back(err, xh3, rs3, gb[2:3])
    small[2:3] = dg
    small[5:6] = db
    dffn = d_r3.astype(BF)
    for ref, at in sides(ids, keep, send):
        put(ids, PLACE_1, ref, 9, 4, dot(cols(act, at, FF // 4), dffn, TN))
    dn2 = d_r3
    for j in range(4):
        da = dot(dffn, wdn[j * D : (j + 1) * D], NT)
        h = hid[j]
        sig = 1.0 / (1.0 + jnp.exp(-h))
        dh = (da * (sig * (1.0 + h * (1.0 - sig)))).astype(BF)
        for ref, at in sides(ids, keep, send):
            put(ids, PLACE_1, ref, 9, j, dot(cols(low2, at, 128), dh, TN))
        dn2 = dn2 + dot(dh, wup[j], NT)
    dr2, dg, db = norm_back(dn2, xh2, rs2, gb[1:2])
    small[1:2] = dg
    small[4:5] = db
    d_r2[...] = dr2
    dcross = dr2.astype(BF)
    for ref, at in sides(ids, keep, send):
        put(ids, PLACE_1, ref, 9, 8, dot(rows_of(at2, at, 128), dcross))
    d_mix[...] = dot(dcross, wco, NT).astype(BF)


def cross_back_a(q, kv, p, rl, d_mix, dkv, dq, dqt):
    attend_back(0, q, kv, p, rl, d_mix, dkv, dqt)
    dq[...] = jnp.transpose(dqt[...]).astype(BF)


def project(own, parts, dkv_a, dkv_b, wk, wv, extra=0.0):
    out = dot(dkv_a[:, :HALF], wk[:, :HALF], NT) + dot(dkv_b[:, :HALF], wk[:, HALF:], NT)
    out = out + dot(dkv_a[:, HALF:], wv[:, :HALF], NT) + dot(dkv_b[:, HALF:], wv[:, HALF:], NT)
    each = own.shape[0]
    own[...] = out[:each] + extra
    for i, part in enumerate(parts):
        part[...] = out[each * (i + 1) : each * (i + 2)].astype(BF)


def cross_back_b(n_parts, ids, ef, q, kv, p, rl, d_mix, dkv_a, dq_a, wb, norms, d_r2, low1, xh1,
                 rs1, at1, small, own, *rest):
    parts, (d_mix1, d_r1, keep, send, dkv, dqt) = rest[:n_parts], rest[n_parts:]
    attend_back(4, q, kv, p, rl, d_mix, dkv, dqt)
    project(own, parts, dkv_a, dkv, wb[1], wb[2])
    dq = jnp.concatenate([dq_a[...], jnp.transpose(dqt[...]).astype(BF)], 1)
    gb = norms[...]
    dn1 = d_r2[...] + dot(dq, wb[3], NT)
    dr1, dg, db = norm_back(dn1, xh1[...], rs1[:, 0:1], gb[0:1])
    row = lax.broadcasted_iota(jnp.int32, (16, D), 0)
    sums = jnp.where(row == 0, dg, jnp.where(row == 3, db, small[...]))
    send[1024:1040] = sums.astype(BF)
    d_r1[...] = dr1
    dself = dr1.astype(BF)
    for ref, at in sides(ids, keep, send):
        lhs = cols(ef, at, 128)
        for j in range(2):
            span = slice(j * HALF, (j + 1) * HALF)
            g = jnp.concatenate([dot(lhs, dkv_a[:, span], TN), dot(lhs, dkv[:, span], TN)], 1)
            put(ids, PLACE_2, ref, 4, j, g)
        put(ids, PLACE_2, ref, 4, 2, dot(cols(low1, at, 128), dq, TN))
        put(ids, PLACE_2, ref, 4, 3, dot(rows_of(at1, at, 128), dself))
    d_mix1[...] = dot(dself, wb[0], NT).astype(BF)


def self_back_b(n_parts, rows, ids, xf, q, kv, p, rl, d_mix, dkv_a, dq_a, wa, d_r1, own, *rest):
    parts, (keep, send, dkv, dqt) = rest[:n_parts], rest[n_parts:]
    attend_back(4, q, kv, p, rl, d_mix, dkv, dqt)
    dq = jnp.concatenate([dq_a[...], jnp.transpose(dqt[...]).astype(BF)], 1)
    through_q = d_r1[...] + dot(dq, wa[0], NT)
    project(own, parts, dkv_a, dkv, wa[1], wa[2], through_q)
    for ref, at in sides(ids, keep, send):
        lhs = cols(xf, at, 128)
        put(ids, PLACE_2, ref, 3, 0, dot(lhs[:rows], dq, TN))
        for j in range(2):
            span = slice(j * HALF, (j + 1) * HALF)
            g = jnp.concatenate([dot(lhs, dkv_a[:, span], TN), dot(lhs, dkv[:, span], TN)], 1)
            put(ids, PLACE_2, ref, 3, 1 + j, g)


def tree_sum(terms):
    while len(terms) > 1:
        terms = [a + b for a, b in zip(terms[::2], terms[1::2])] + terms[len(terms) & ~1 :]
    return terms[0]


ANY = pl.BlockSpec(memory_space=pl.ANY)


def fetch(ref, start, count, to, sem):
    copy = pltpu.make_async_copy(ref.at[pl.ds(start, count)], to, sem)
    copy.start()
    return copy


def mix(name, *outs):
    arrays, terms, plan = [], [], []
    for dtype, segments in outs:
        plan.append([])
        for segment in segments:
            used = []
            for array, start, count in segment:
                at = [i for i, v in enumerate(arrays) if v is array]
                if not at:
                    arrays.append(array)
                used.append(len(terms))
                terms.append((at[0] if at else len(arrays) - 1, start, count, array.dtype))
            plan[-1].append(used)

    def body(*refs):
        for out, segments in zip(refs[len(arrays) :], plan):
            first = 0
            for used in segments:
                count = terms[used[0]][2]
                parts = [refs[k][start : start + count].astype(F32) for k, start, _, _ in (terms[i] for i in used)]
                out[first : first + count] = tree_sum(parts).astype(out.dtype)
                first += count

    shapes = [((sum(t[0][2] for t in segments), D), dtype) for dtype, segments in outs]
    return call(body, [(v, None) for v in arrays], shapes, name=name)


def finish(counts, *refs):
    where, refs = refs[0], refs[1:]
    sources, results = refs[: len(counts)], refs[len(counts) :]
    refs = [ref.at[:count] for ref, count in zip(sources, counts)]
    one, (out, home, e_keep, x_keep, home_x, z_own, z_got, *refs) = refs[:5], refs[5:]
    two, three = refs[:6], refs[6:]
    outputs, loss, g_x, g_e, g_in, g_so, g_cq, g_cin, g_co, g_up, g_down, g_gain, g_bias = results
    mine = where[0]
    tok = e_keep.shape[0]
    outputs[mine] = out[...]
    outputs[1 - mine] = home[:tok]
    g_e[mine] = e_keep[...]
    g_e[1 - mine] = home[tok:].astype(F32)
    g_x[mine] = x_keep[...]
    g_x[1 - mine] = home_x[:tok].astype(F32)
    t1 = tree_sum([r[...].astype(F32) for r in one] + [home_x[tok:].astype(F32)])
    for j in range(4):
        g_up[:, j * D : (j + 1) * D] = t1[16 * j : 16 * j + 16]
    g_down[...] = t1[64:128]
    g_co[...] = t1[128:144]
    t2 = tree_sum([r[...].astype(F32) for r in two[:3]] + [r[:64].astype(F32) for r in two[3:]] + [z_got[:64].astype(F32)])
    for j in range(2):
        g_cin[:, j * D : (j + 1) * D] = t2[16 * j : 16 * j + 16]
    g_cq[...] = t2[32:48]
    g_so[...] = t2[48:64]
    t3 = tree_sum([r[...].astype(F32) for r in three] + [r[128:176].astype(F32) for r in two[3:]] + [z_got[64:112].astype(F32)])
    for j in range(3):
        g_in[:, j * D : (j + 1) * D] = t3[16 * j : 16 * j + 16]
    small = z_own[112:128].astype(F32) + z_got[112:128].astype(F32)
    total = jnp.sum(small[6:7], axis=1, keepdims=True)
    loss[...] = total / (jnp.sum(small[7:8], axis=1, keepdims=True) * D)
    column = lax.broadcasted_iota(jnp.int32, (16, D), 1)
    row = lax.broadcasted_iota(jnp.int32, (16, D), 0)
    pick = (column == where[1] * 16 + row).astype(F32)
    own = lax.dot_general(small[:8], pick, NT, precision=lax.Precision.HIGHEST, preferred_element_type=F32)
    g_gain[...] = own[0:3]
    g_bias[...] = own[3:6]


def tie(*values):
    return lax.optimization_barrier(values)


def make_shards(nd, ns):
    n_dev = nd * ns
    half = ns // 2
    per = G * 16 // n_dev
    fast = nd == 4 and ns == 8
    run = functools.partial(call, vmem=20 if fast else 48)

    core, y, x, zl, zh = ("dp", 1), ("dp", 2), ("seq", 1), ("seq", 2), ("seq", 4)

    def shards(inputs, encoder, teacher, dec_seg, enc_seg, dec_valid, self_in, self_out,
               cross_query, cross_in, cross_out, ffn_up, ffn_down, norm_gain, norm_bias):
        tok = inputs.shape[1]
        rows = 2 * tok
        length = dec_seg.shape[1]
        dp_at, seq_at = lax.axis_index("dp"), lax.axis_index("seq")
        dev = dp_at * ns + seq_at
        mine = seq_at // half

        def flip(bit, arrays):
            axis, b = bit
            size = nd if axis == "dp" else ns
            flat = [v.reshape(-1, D) for v in arrays]
            got = lax.ppermute(
                flat[0] if len(flat) == 1 else jnp.concatenate(flat, 0),
                axis, [(i, i ^ b) for i in range(size)],
            )
            out, start = [], 0
            for v, f in zip(arrays, flat):
                out.append(lax.slice_in_dim(got, start, start + f.shape[0]).reshape(v.shape))
                start += f.shape[0]
            return out

        def swap(bit, array):
            return flip(bit, [array])[0]

        def of(v, i):
            return lax.dynamic_index_in_dim(v, i, 0, keepdims=False)

        def other(v):
            return of(v, 1 - mine)

        def append(v, got):
            return jnp.concatenate([v, got], 0)


        row_bits = (2, 1) if fast else tuple(1 << b for b in range(half.bit_length() - 1))
        slots = jnp.arange(half, dtype=jnp.int32)

        def pieces(bits):
            masks = sum((((slots >> i) & 1) * b) for i, b in enumerate(bits))[:, None]
            return (seq_at ^ masks ^ jnp.array([[0, half]], jnp.int32)).reshape(-1)

        pos = (pieces(row_bits)[:, None] * tok + jnp.arange(tok, dtype=jnp.int32)[None]).reshape(-1)
        dec_k = of(dec_seg, mine).reshape(ns, tok)[pieces(row_bits)].reshape(-1)
        enc_k = of(enc_seg, mine).reshape(ns, tok)[pieces(row_bits)].reshape(-1)
        segs = jnp.stack([dec_k, pos, enc_k] + [jnp.zeros_like(pos)] * 5).astype(F32)

        def spread(v, bits):
            return sum((((v & b) != 0).astype(jnp.int32) << i) for i, b in enumerate(bits))

        if fast:
            i16 = jnp.arange(16, dtype=jnp.int32)
            g32 = jnp.arange(32, dtype=jnp.int32)
            dev16 = (dp_at >> 1) * 8 + seq_at

            def came_from(bits):
                return dev ^ sum((((g32 >> i) & 1) * b for i, b in enumerate(bits)))

            ids = jnp.concatenate(
                [
                    jnp.stack([dp_at & 1, dev, mine]).astype(jnp.int32),
                    spread(i16 ^ dev16, (4, 2, 1, 8)),
                    spread(i16 ^ dev16, (4, 2, 1, 8)),
                    came_from((4, 2, 1, 16, 8)),
                    came_from((4, 16, 1, 2, 8)),
                    came_from((4, 2, 1, 16, 8)),
                ]
            )
        else:
            i16, g32 = jnp.arange(16, dtype=jnp.int32), jnp.arange(32, dtype=jnp.int32)
            ids = jnp.concatenate([jnp.stack([0 * dev, dev, mine]).astype(jnp.int32), i16, i16, g32, g32, g32])

        if fast:
            mats = [self_in, self_out, cross_in, cross_query, cross_out, ffn_up, ffn_down, norm_gain, norm_bias]
            first, second, third, own_x, own_e = run(
                pack,
                [(w, None) for w in mats + [inputs, encoder, teacher, dec_valid]]
                + [(jnp.stack([dev, mine]).astype(jnp.int32), SMEM)],
                [((tok + 48, D), BF), ((224, D), BF), ((2 * tok + 16, D), BF), ((tok, D), BF), ((tok, D), BF)],
                name="pack",
                vmem=56,
            )

            def split(v, *counts):
                ends = [sum(counts[: i + 1]) for i in range(len(counts))]
                return [v[e - c : e].reshape(1, c // 16, 16, D) for c, e in zip(counts, ends)]

            got = swap(zh, first)
            got, second, segs, ids = tie(got, second, segs, ids)
            xf = jnp.stack([own_x, got[:tok]])[None]
            wa = append(*(v[tok:].reshape(1, 3, 16, D) for v in (first, got)))
            got_bf = swap(zh, second)
            got_x, got_a = flip(zl, [xf, wa])
            got_x, got_a, got_bf, third = tie(got_x, got_a, got_bf, third)
            xf, wa = append(xf, got_x), append(wa, got_a)
            wb, wf = (append(*both) for both in zip(split(second, 96, 128), split(got_bf, 96, 128)))
            got_x, got_a = flip(x, [xf, wa])
            message = swap(zh, third)
            got_e = message[:tok]
            got_b, got_f = swap(y, wb), swap(zl, wf)
            ef = jnp.stack([own_e, got_e])[None]
            got_x, got_a, got_b, got_f, ef = tie(got_x, got_a, got_b, got_f, ef)
            wa, wb, wf = append(wa, got_a), append(wb, got_b), append(wf, got_f)
            got_a, got_b, got_e, got_f = swap(y, wa), swap(x, wb), swap(zl, ef), swap(x, wf)
            wa_far = swap(core, wa)
            got_a, got_b, got_e, wa_far = tie(got_a, got_b, got_e, wa_far)
            wa = [wa, got_a, wa_far, swap(core, got_a)]
            wb, ef = append(wb, got_b), append(ef, got_e)
            got_b, got_e = swap(zl, wb), swap(x, ef)
            got_f, wa[3] = tie(got_f, wa[3])
            wf = append(wf, got_f)
            got_f = swap(y, wf)
            wb_far, wf_far = swap(core, wb), swap(core, wf)
        else:
            valid_away = jnp.pad(other(dec_valid).astype(BF)[None], ((0, 15), (0, D - tok)))
            got_x = swap(("seq", half), other(inputs))
            message = swap(("seq", half), jnp.concatenate([other(encoder), other(teacher), valid_away], 0))
            got_e = message[:tok]
            xf, ef = jnp.stack([of(inputs, mine), got_x])[None], jnp.stack([of(encoder, mine), got_e])[None]
            for bit in row_bits:
                got_x, got_e = flip(("seq", bit), [xf, ef])
                if bit != row_bits[-1]:
                    xf, ef = append(xf, got_x), append(ef, got_e)

            def gathered(w):
                return lax.all_gather(w, ("dp", "seq"), axis=0, tiled=True)

            def grouped(w):
                return w.reshape(G, 16, w.shape[1] // D, D).transpose(0, 2, 1, 3)

            wa = grouped(gathered(self_in))
            mine_only = lax.dynamic_update_slice(
                jnp.zeros((16, D), BF), jnp.concatenate([norm_gain, norm_bias], 0), (0, dev * per)
            )
            all_norms = lax.psum(mine_only.astype(F32), ("dp", "seq")).astype(BF)
            all_norms = jnp.pad(all_norms[None], ((0, G - 1), (0, 0), (0, 0)))[:, None]
            rest = [grouped(gathered(w)) for w in (self_out, cross_in, cross_query, cross_out)]
            down = gathered(ffn_down).reshape(G, 4, 16, D)
            wb = jnp.concatenate(rest + [all_norms], 1)
            wf = jnp.concatenate([grouped(gathered(ffn_up)), down], 1)
            wa, wb, wf = [[w[8 * i : 8 * i + 8] for i in range(4)] for w in (wa, wb, wf)]
        x_near, x_far = xf.reshape(-1, D), got_x.reshape(-1, D)

        sm = (ids, SMEM)
        p_shape = (HEADS, length, rows)
        def held(*shapes):
            return (
                [pltpu.VMEM((length, rows), F32)]
                + [pltpu.VMEM(v, BF) for v in shapes]
                + [pltpu.VMEM((2, 2, length, rows), BF), pltpu.SemaphoreType.DMA((2,)), pltpu.SemaphoreType.DMA((10,))]
                + [pltpu.VMEM((HEADS, rows), F32)]
            )

        all_rows, own_rows, both_kv = (length, D), (rows, D), (length, 2 * D)
        own_x = x_near[:rows]
        xf, wa, q1, kv1, p1, rl1, at1 = run(
            functools.partial(self_forward, rows),
            [sm, (x_near, None), (x_far, None)] + [(v, None) for v in wa] + [(segs, None)],
            [(all_rows, BF, True), ((3, D, D), BF, True), (own_rows, BF, True), (both_kv, BF, True),
             (p_shape, BF, True), ((HEADS, rows), F32, True), ((D, rows), BF)],
            scratch=held(all_rows, (3, D, D), own_rows, both_kv),
            name="self_forward",
        )
        if fast:
            got_b, got_e, wb_far, at1 = tie(got_b, got_e, wb_far, at1)
            wb = [wb, got_b, wb_far, swap(core, got_b)]
        e_near, e_far = ef.reshape(-1, D), got_e.reshape(-1, D)
        ef, wb, norms, xh1, rs1, low1, q2, kv2, p2, rl2, at2 = run(
            functools.partial(cross_forward, rows),
            [sm, (own_x, None), (e_near, None), (e_far, None), (at1, None)] + [(v, None) for v in wb] + [(segs, None)],
            [(all_rows, BF, True), ((5, D, D), BF), ((16, D), F32, True), (own_rows, F32), ((rows, 128), F32, True),
             (own_rows, BF, True), (own_rows, BF, True), (both_kv, BF, True), (p_shape, BF, True),
             ((HEADS, rows), F32, True), ((D, rows), BF, True)],
            scratch=held(all_rows, own_rows, own_rows, both_kv)
            + [pltpu.VMEM((16, D), F32), pltpu.VMEM((rows, 128), F32), pltpu.VMEM((D, rows), BF)],
            name="cross_forward",
        )
        if fast:
            got_f, wf_far, at2 = tie(got_f, wf_far, at2)
            wf = [wf, got_f, wf_far, swap(core, got_f)]
        out, small, d_r2, d_mix2, keep1, send1 = run(
            ffn_both,
            [sm, (xh1, None), (in_hbm(at2), HBM), (teacher, None), (message, None), (dec_valid, None), (wb, None), (in_hbm(norms), HBM)]
            + [(v, None) for v in wf],
            [((rows, D), BF), ((16, D), F32), ((rows, D), F32), ((rows, D), BF)] + [((2304, D), BF)] * 2,
            scratch=[pltpu.VMEM((rows, FF), BF), pltpu.VMEM((4, rows, D), F32), pltpu.VMEM((rows, D), BF),
                     pltpu.VMEM((4, D, D), BF), pltpu.VMEM((FF, D), BF), pltpu.VMEM((D, rows), BF),
                     pltpu.VMEM((16, D), F32), pltpu.SemaphoreType.DMA((2,))],
            name="ffn_both",
        )

        kv_half = [((length, D), BF), ((rows, HALF), BF)]
        d_rows = [pltpu.VMEM((HALF, rows), F32)]
        both_scratch = [pltpu.VMEM((length, D), BF)] + d_rows
        row_parts = [((rows, D), F32)] + [((rows, D), BF)] * (half - 1)
        partners = [sum(((i >> k) & 1) * b for k, b in enumerate(row_bits)) for i in range(1, half)]

        if fast:
            got1 = swap(core, send1)
        dkv2, dq2 = run(
            cross_back_a,
            [(q2, None), (kv2, None), (p2, None), (rl2, None), (d_mix2, None)],
            kv_half,
            scratch=d_rows,
            name="cross_back_a",
        )
        if fast:
            got1, d_mix2, dkv2 = tie(got1, d_mix2, dkv2)
            got_y1 = swap(y, (keep1[1152:].astype(F32) + got1[1152:].astype(F32)).astype(BF))
        e_own, *rest = run(
            functools.partial(cross_back_b, half - 1),
            [sm, (ef, None), (q2, None), (kv2, None), (p2, None), (rl2, None), (d_mix2, None),
             (dkv2, None), (dq2, None), (wb, None), (norms, None), (d_r2, None), (low1, None),
             (xh1, None), (rs1, None), (at1, None), (small, None)],
            row_parts + [((rows, D), BF), ((rows, D), F32), ((1024, D), BF), ((1040, D), BF)],
            scratch=both_scratch,
            name="cross_back_b",
        )
        e_parts, (d_mix1, d_r1, keep2, send2) = rest[: half - 1], rest[half - 1 :]
        if fast:
            got2 = swap(core, send2)
        e_got = [swap(("seq", m), part) for m, part in zip(partners, e_parts)]
        dkv1, dq1 = run(
            cross_back_a,
            [(q1, None), (kv1, None), (p1, None), (rl1, None), (d_mix1, None)],
            kv_half,
            scratch=d_rows,
            name="self_back_a",
        )
        if fast:
            got2, d_mix1, dkv1 = tie(got2, d_mix1, dkv1)
        x_own, *rest = run(
            functools.partial(self_back_b, half - 1, rows),
            [sm, (xf, None), (q1, None), (kv1, None), (p1, None), (rl1, None), (d_mix1, None),
             (dkv1, None), (dq1, None), (wa, None), (d_r1, None)],
            row_parts + [((768, D), BF)] * 2,
            scratch=both_scratch,
            name="self_back_b",
        )
        x_parts, (keep3, send3) = rest[: half - 1], rest[half - 1 :]

        if fast:
            (away,) = mix("away_x", (BF, [[(x_parts[0], 0, rows)], [(x_parts[2], 0, rows)]]))
            got_xa = swap(zl, away)
            got_y1, send3, *e_got = tie(got_y1, send3, *e_got)
            (away,) = mix(
                "sum_y2",
                (BF, [[(keep2, 512, 512), (got2, 512, 512)], [(send2, 1024, 16), (got2, 1024, 16)]]),
            )
            got_y2 = swap(y, away)
            small_y2 = (away, 512, 16)
            one = lambda start, count: [(v, start, count) for v in (keep1, got1, got_y1)]
            (away,) = mix("sum_1x", (BF, [one(576, 576)]))
            got_1a = swap(x, away)
        else:
            x_got = [swap(("seq", m), part) for m, part in zip(partners, x_parts)]
        if fast:
            got3 = swap(core, send3)
        e_terms = lambda start: [(v, start, tok) for v in (e_own, *e_got)]
        e_keep, away = mix("sum_e", (F32, [e_terms(0)]), (BF, [[(out, tok, tok)], e_terms(tok)]))
        home = swap(("seq", half), away)
        if fast:
            (away,) = mix("sum_y3", (BF, [[(keep3, 384, 384), (got3, 384, 384)]]))
            got_y3 = swap(y, away)
            got_y3, home = tie(got_y3, home)
        if fast:
            (away,) = mix("sum_xx", (BF, [[(x_parts[1], 0, rows), (got_xa, rows, rows)]]))
            got_xb = swap(x, away)
            (away,) = mix("sum_1z", (BF, [one(288, 288) + [(got_1a, 288, 288)]]))
            got_1b = swap(zl, away)
            x_terms = lambda start: [(v, start, tok) for v in (x_own, got_xa, got_xb)]
            more = [one(144, 144) + [(got_1a, 144, 144), (got_1b, 144, 144)]]
        else:
            x_terms = lambda start: [(v, start, tok) for v in (x_own, *x_got)]
            more = []
        x_keep, away = mix("sum_x", (F32, [x_terms(0)]), (BF, [x_terms(tok), *more]))
        home_x = swap(("seq", half), away)

        if fast:
            def two(start, count):
                return [(v, start, count) for v in (keep2, got2, got_y2)]

            def three(start, count):
                return [(v, start, count) for v in (keep3, got3, got_y3)]

            quads = mix(
                "sum_quads",
                *[(BF, [two(128 * i, 128), three(96 * i, 96), [small_y2, (got_y2, 512, 16)]]) for i in (1, 2, 3)],
            )
            q_got = [swap(("seq", m), part) for m, part in zip(partners, quads)]
            (away,) = mix(
                "sum_zh",
                (BF, [two(64, 64) + [(v, 64, 64) for v in q_got], three(48, 48) + [(v, 176, 48) for v in q_got],
                      [(quads[0], 224, 16)] + [(v, 224, 16) for v in q_got]]),
            )
            got_z = swap(zh, away)
            where = jnp.stack([mine, dev]).astype(jnp.int32)

            last = [(v, 144) for v in (keep1, got1, got_y1, got_1a, got_1b)] + [(out, tok)]
            last += [(v, v.shape[0]) for v in (home, e_keep, x_keep, home_x, away, got_z)]
            last += [(v, 64) for v in (keep2, got2, got_y2)] + [(v, v.shape[0]) for v in q_got]
            last += [(v, 48) for v in (keep3, got3, got_y3)]
            counts = [c for _, c in last]
            flat = [((per, w), F32) for w in (3 * D, D, D, 2 * D, D, FF)] + [((4 * per, D), F32)]
            done = run(
                functools.partial(finish, counts),
                [(where, SMEM)] + [(v, None) for v, _ in last],
                [((2, tok, D), BF), ((1, 1), F32), ((2, tok, D), F32), ((2, tok, D), F32)] + flat + [((3, per), F32)] * 2,
                name="finish",
            )
            return (done[0], done[1].reshape(()), *done[2:])

        def back_home(kept, recv):
            return jnp.where(mine == 0, jnp.stack([kept, recv]), jnp.stack([recv, kept]))

        def summed(g):
            return lax.psum_scatter(g, ("dp", "seq"), scatter_dimension=0, tiled=True).astype(F32)

        def rejoin(keep, send, n):
            g = jnp.stack([v[: 256 * n].reshape(2, 8, n, 16, D) for v in (keep, send)], 1)
            return g.reshape(G, n, 16, D)

        def full(g):
            return g.transpose(0, 2, 1, 3).reshape(G * 16, -1)

        small = lax.psum(send2[1024:].astype(F32), ("dp", "seq"))
        all1, all2, all3 = rejoin(keep1, send1, 9), rejoin(keep2, send2, 4), rejoin(keep3, send3, 3)
        g_norm = lax.dynamic_slice(small, (0, dev * per), (6, per))
        return (
            back_home(out[:tok], home[:tok]),
            jnp.sum(small[6]) / (jnp.sum(small[7]) * D),
            back_home(x_keep, home_x.astype(F32)),
            back_home(e_keep, home[tok:].astype(F32)),
            summed(full(all3)),
            summed(full(all2[:, 3:])),
            summed(full(all2[:, 2:3])),
            summed(full(all2[:, :2])),
            summed(full(all1[:, 8:])),
            summed(full(all1[:, :4])),
            summed(all1[:, 4:8].reshape(FF, D)),
            g_norm[:3],
            g_norm[3:],
        )

    return shards


def solution(mesh):
    rows, both = P("dp", "seq", None), P(("dp", "seq"), None)
    norm = P(None, ("dp", "seq"))
    return jax.shard_map(
        make_shards(mesh.shape["dp"], mesh.shape["seq"]),
        mesh=mesh,
        in_specs=(rows, rows, rows, P("dp", None), P("dp", None), P("dp", "seq")) + (both,) * 7 + (norm, norm),
        out_specs=(rows, P(), rows, rows) + (both,) * 7 + (norm, norm),
        check_vma=False,
    )
```
